256 devices in a mesh: depth: 2 (over core), pos: 128 (over x, z, y).
Axes of the slice: x: 4, y: 4, z: 8, core: 2. Of those that a mesh axis runs over, the one named last changes fastest.
Arguments:
- object_field: bfloat16 [2, 2, 2048, 32768], P('depth', None, None, 'pos'), may hold values from -4.1875 to 4.1875
- probe: bfloat16 [4, 2, 256, 256], replicated, may hold values from -4.1875 to 4.1875
- prop_phase: float32 [256, 256], replicated, may hold values from -3.140625 to 3.140625
- measured: float32 [256, 256, 256], P('pos'), may hold values from 0 to 8
- positions: int32 [256, 2], replicated, may hold values from 0 to 32512, as said below
Outputs:
- object_grad: bfloat16 [2, 2, 2048, 32768], P('depth', None, None, 'pos')
The draws below stay inside these ranges and needn't reach their ends.
Inputs may be any that keep to these rules, and one draw needn't show every extreme that they name: `positions`: row r holds (row offset, column offset). For the block b = r // 2, column offsets lie from b * 256 to b * 256 + 255; in the last block they equal b * 256. Row offsets lie from 0 to 1792. Row 0 is (0, 0).
All inputs are finite; a program needn't handle non-finite values.
Results may differ from the reference program's by a relative error of at most 0.019.
Values may be sent and summed in bfloat16 or wider, within the bound.
A program may use at most 64 MiB of HBM per device.

```python
import math
import jax
import jax.numpy as jnp
from jax import lax

NP = 256
MODES = 4
POS_DEV = 2
H = 2048
SLICES = 2
W = 32768
POSITIONS = 256
N_POS = 128


def draw_positions(key, part):
    key_rows = jax.random.fold_in(key, 11)
    key_cols = jax.random.fold_in(key, 23)
    rows_off = jax.random.randint(key_rows, (POSITIONS,), 0, H - NP + 1, dtype=jnp.int32)
    shifts = jax.random.randint(key_cols, (POSITIONS,), 0, NP, dtype=jnp.int32)
    ramp = jnp.arange(POSITIONS, dtype=jnp.int32)
    owner = ramp // POS_DEV
    shifts = jnp.where(owner == N_POS - 1, 0, shifts)
    shifts = jnp.where(ramp == 0, 0, shifts)
    rows_off = jnp.where(ramp == 0, 0, rows_off)
    cols_off = owner * NP + shifts
    return jnp.stack([rows_off, cols_off], axis=1).astype(jnp.int32)


def level_of(stream_key, shape, pieces, low, largest):
    gain, own = 1.0, jax.random.fold_in(stream_key, 6)
    for dim, blocks in pieces:
        draws = jnp.exp(jax.random.uniform(jax.random.fold_in(own, dim), (blocks,), jnp.float32, low / len(pieces), largest / len(pieces)))
        gain = gain * jnp.repeat(draws, shape[dim] // blocks).reshape([-1 if axis == dim else 1 for axis in range(len(shape))])
    return gain


def bell_draw(own_key, dims, spread, limit, pieces=(), kind=jnp.bfloat16):
    result = jax.random.normal(own_key, dims, jnp.float32) * spread
    if len(pieces) > 0:
        result = level_of(own_key, dims, pieces, -0.22, 0.18) * result
    return jnp.clip(result, min=-limit, max=limit).astype(kind)


def setup_inputs(seed: int = 0) -> dict:
    key_of = jax.random.split(jax.random.key(seed), 6)
    object_field = bell_draw(key_of[0], (SLICES, 2, H, W), 0.7, 4.1875, ((0, 2), (3, 128)))
    probe = bell_draw(key_of[1], (MODES, 2, NP, NP), 0.7, 4.1875)
    prop_phase = jnp.clip(jax.random.uniform(key_of[2], (NP, NP), jnp.float32, -3.140625, 3.140625), -3.140625, 3.140625)
    measured = jnp.clip(8.0 * jax.random.uniform(key_of[3], (POSITIONS, NP, NP), jnp.float32) ** level_of(key_of[3], (POSITIONS, NP, NP), ((0, 128),), -0.2, 0.2), 0.0, 8.0)
    positions = draw_positions(jax.random.fold_in(key_of[5], 71), 0)
    return dict(object_field=object_field, probe=probe, prop_phase=prop_phase, measured=measured, positions=positions)


def dft_tables(frame):
    ramp = jnp.arange(frame, dtype=jnp.int32)
    phases = ramp[:, None] * ramp[None, :] % frame
    angles = phases.astype(jnp.float32) * (2.0 * math.pi / frame)
    factor = 1.0 / math.sqrt(frame)
    return ((jnp.cos(angles) * factor).astype(jnp.bfloat16), (-jnp.sin(angles) * factor).astype(jnp.bfloat16))

def left_mult(table, values):
    return jnp.einsum('ab,nmbc->nmac', table.astype(jnp.float32), values.astype(jnp.float32), precision=lax.Precision.HIGHEST)

def right_mult(values, table):
    return jnp.einsum('nmab,bc->nmac', values.astype(jnp.float32), table.astype(jnp.float32), precision=lax.Precision.HIGHEST)

def transform(real_in, imag_in, fourier_table_real, fourier_table_imaginary):
    in_r = real_in.astype(jnp.bfloat16)
    in_i = imag_in.astype(jnp.bfloat16)
    mid_r = (left_mult(fourier_table_real, in_r) - left_mult(fourier_table_imaginary, in_i)).astype(jnp.bfloat16)
    mid_i = (left_mult(fourier_table_real, in_i) + left_mult(fourier_table_imaginary, in_r)).astype(jnp.bfloat16)
    out_r = right_mult(mid_r, fourier_table_real) - right_mult(mid_i, fourier_table_imaginary)
    out_i = right_mult(mid_r, fourier_table_imaginary) + right_mult(mid_i, fourier_table_real)
    return (out_r, out_i)

def forward_front(patch_r, patch_i, probe, kern_r, kern_i, fourier_table_real, fourier_table_imaginary):
    obj_r = patch_r.astype(jnp.float32)[:, None]
    obj_i = patch_i.astype(jnp.float32)[:, None]
    probe_r = probe[:, 0].astype(jnp.float32)[None]
    probe_i = probe[:, 1].astype(jnp.float32)[None]
    wave_r = probe_r * obj_r - probe_i * obj_i
    wave_i = probe_r * obj_i + probe_i * obj_r
    spectrum_real, spectrum_imaginary = transform(wave_r, wave_i, fourier_table_real, fourier_table_imaginary)
    return ((spectrum_real * kern_r - spectrum_imaginary * kern_i).astype(jnp.bfloat16), (spectrum_real * kern_i + spectrum_imaginary * kern_r).astype(jnp.bfloat16))

def backward_tail(spectrum_real, spectrum_imaginary, patch_r, patch_i, measured, fourier_table_real, fourier_table_imaginary):
    conj_i = -fourier_table_imaginary
    wave_r, wave_i = transform(spectrum_real, spectrum_imaginary, fourier_table_real, conj_i)
    obj_r = patch_r.astype(jnp.float32)[:, None]
    obj_i = patch_i.astype(jnp.float32)[:, None]
    exit_r = wave_r * obj_r - wave_i * obj_i
    exit_i = wave_r * obj_i + wave_i * obj_r
    far_r, far_i = transform(exit_r, exit_i, fourier_table_real, fourier_table_imaginary)
    intensity = lax.optimization_barrier(jnp.sum(far_r * far_r + far_i * far_i, axis=1))
    weight = ((intensity - measured) * 0.125)[:, None]
    back_r, back_i = transform(weight * far_r, weight * far_i, fourier_table_real, conj_i)
    grad_r = lax.optimization_barrier(jnp.sum(wave_r * back_r + wave_i * back_i, axis=1))
    grad_i = lax.optimization_barrier(jnp.sum(wave_r * back_i - wave_i * back_r, axis=1))
    adj_r = obj_r * back_r + obj_i * back_i
    adj_i = obj_r * back_i - obj_i * back_r
    out_r, out_i = transform(adj_r, adj_i, fourier_table_real, fourier_table_imaginary)
    return (out_r.astype(jnp.bfloat16), out_i.astype(jnp.bfloat16), grad_r, grad_i)

def back_front(adj_r, adj_i, probe, kern_r, kern_i, fourier_table_real, fourier_table_imaginary):
    cot_r = adj_r.astype(jnp.float32)
    cot_i = adj_i.astype(jnp.float32)
    turn_r = kern_r * cot_r + kern_i * cot_i
    turn_i = kern_r * cot_i - kern_i * cot_r
    wave_r, wave_i = transform(turn_r, turn_i, fourier_table_real, -fourier_table_imaginary)
    probe_r = probe[:, 0].astype(jnp.float32)[None]
    probe_i = probe[:, 1].astype(jnp.float32)[None]
    grad_r = lax.optimization_barrier(jnp.sum(probe_r * wave_r + probe_i * wave_i, axis=1))
    grad_i = lax.optimization_barrier(jnp.sum(probe_r * wave_i - probe_i * wave_r, axis=1))
    return (grad_r, grad_i)

def reference(object_field, probe, prop_phase, measured, positions):
    fourier_table_real, fourier_table_imaginary = dft_tables(NP)
    kern_r = jnp.cos(prop_phase)
    kern_i = jnp.sin(prop_phase)

    def one_position(grad, entry_value):
        frame_measured, window_offset = entry_value
        row_at = window_offset[0].astype(jnp.int32)
        col_at = window_offset[1].astype(jnp.int32)
        zero = jnp.zeros((), jnp.int32)
        first = lax.dynamic_slice(object_field[0], (zero, row_at, col_at), (2, NP, NP))
        second_slice = lax.dynamic_slice(object_field[1], (zero, row_at, col_at), (2, NP, NP))
        spectrum_real, spectrum_imaginary = forward_front(first[0][None], first[1][None], probe, kern_r, kern_i, fourier_table_real, fourier_table_imaginary)
        spectrum_grad_real, spectrum_grad_imaginary, slice_one_grad_real, slice_one_grad_imaginary = backward_tail(spectrum_real, spectrum_imaginary, second_slice[0][None], second_slice[1][None], frame_measured[None], fourier_table_real, fourier_table_imaginary)
        g0_r, g0_i = back_front(spectrum_grad_real, spectrum_grad_imaginary, probe, kern_r, kern_i, fourier_table_real, fourier_table_imaginary)
        stacked = jnp.stack([jnp.stack([g0_r[0], g0_i[0]]), jnp.stack([slice_one_grad_real[0], slice_one_grad_imaginary[0]])])
        current = lax.dynamic_slice(grad, (zero, zero, row_at, col_at), (2, 2, NP, NP))
        grad = lax.dynamic_update_slice(grad, current + stacked, (zero, zero, row_at, col_at))
        return (grad, None)
    start = jnp.zeros((SLICES, 2, H, W), jnp.float32)
    total, unused = lax.scan(one_position, start, (measured, positions))
    return total.astype(jnp.bfloat16)
```

```python
import functools
import math
import numpy as np
import jax, jax.numpy as jnp
from jax import lax
from jax.experimental import pallas as pl
from jax.experimental.pallas import tpu as pltpu
from jax.sharding import PartitionSpec as PS
BF=jnp.bfloat16; F32=jnp.float32
N=256; HF=128
MODES=4

def tables():
    k=np.arange(N); ph=(k[:,None]*k[None,:])%N
    ang=ph*(2*math.pi/N)
    fr=np.cos(ang)/16.0; fi=-np.sin(ang)/16.0
    tb=np.concatenate([fr[0::2],fi[0::2],fr[1::2],fi[1::2]],0)
    return jnp.asarray(tb,dtype=BF), jnp.asarray(tb.T,dtype=BF)

def dot(a,b): return jnp.dot(a,b,preferred_element_type=F32)
def iota(shape,d): return lax.broadcasted_iota(jnp.int32,shape,d)

def prep_tables(tb,tbt,tab,y,c):
    for r,f1,f2 in ((y,0,1),(c,3,2)):
        onehot=(iota((N,HF),0)==((iota((N,HF),1)-r)&255)).astype(F32).astype(BF)
        m1=dot(tb[...],onehot).astype(BF)
        onet=(iota((HF,N),1)==((iota((HF,N),0)-r)&255)).astype(F32).astype(BF)
        m2=dot(onet,tbt[...]).astype(BF)
        for par in range(2):
            a=m1[par*256:par*256+128]; b=m1[par*256+128:par*256+256]
            tab[f1,par,0:128,0:128]=a; tab[f1,par,0:128,128:256]=-b
            tab[f1,par,128:256,0:128]=b; tab[f1,par,128:256,128:256]=a
            a=m2[:,par*256:par*256+128]; b=m2[:,par*256+128:par*256+256]
            tab[f2,par,0:128,0:128]=a; tab[f2,par,0:128,128:256]=b
            tab[f2,par,128:256,0:128]=-b; tab[f2,par,128:256,128:256]=a

def prep_probe(probe,pr,tmp,y,c):
    ryt=(iota((N,N),1)==((iota((N,N),0)-y)&255)).astype(F32).astype(BF)
    rc=(iota((N,N),0)==((iota((N,N),1)-c)&255)).astype(F32).astype(BF)
    for m in range(4):
        for q in range(2):
            t=dot(ryt,probe[m,q]).astype(BF)
            pr[m,q]=dot(t,rc).astype(BF)

def perms():
    i0=iota((N,N),0); i1=iota((N,N),1)
    pt=(i1==(2*(i0&127)+(i0>>7))).astype(F32).astype(BF)
    p=(i0==(2*(i1&127)+(i1>>7))).astype(F32).astype(BF)
    return pt,p

def prep_k(phase,kk):
    pt,p=perms()
    x=phase[...]
    acc=None
    for _ in range(3):
        h=x.astype(BF)
        x=x-h.astype(F32)
        t=dot(dot(pt,h).astype(BF),p)
        acc=t if acc is None else acc+t
    kk[0]=jnp.cos(acc); kk[1]=jnp.sin(acc)

def prep_meas(meas,mp):
    pt,p=perms()
    mp[...]=dot(dot(pt,meas[...]).astype(BF),p)

def s1f(tab,P,L):
    for par in range(2):
        V=dot(tab[0,par],P[par])
        for q in range(2):
            lo=V[q*128:q*128+128,:128]; hi=V[q*128:q*128+128,128:]
            L[0,par*128:par*128+128,q*128:q*128+128]=(lo+hi).astype(BF)
            L[1,par*128:par*128+128,q*128:q*128+128]=(lo-hi).astype(BF)

def s1i(tab,P,L):
    E0=dot(tab[1,0],P[0]); E1=dot(tab[1,1],P[1])
    for q in range(2):
        for cp in range(2):
            a=E0[q*128:q*128+128,cp*128:cp*128+128]; b=E1[q*128:q*128+128,cp*128:cp*128+128]
            L[cp,0:128,q*128:q*128+128]=(a+b).astype(BF)
            L[cp,128:256,q*128:q*128+128]=(a-b).astype(BF)

def s2f(tab,L,cp): return dot(L[cp],tab[2,cp])
def s2i(tab,L):
    D0=dot(L[0],tab[3,0]); D1=dot(L[1],tab[3,1])
    return [[D0[:,q*128:q*128+128]+D1[:,q*128:q*128+128], D0[:,q*128:q*128+128]-D1[:,q*128:q*128+128]] for q in range(2)]

def put_rows(P,q,uc,x):
    a=x[:128]; b=x[128:]
    P[0,q*128:q*128+128,uc*128:uc*128+128]=(a+b).astype(BF)
    P[1,q*128:q*128+128,uc*128:uc*128+128]=(a-b).astype(BF)

def put_freq(P,q,cp,x):
    P[0,q*128:q*128+128,cp*128:cp*128+128]=x[:128].astype(BF)
    P[1,q*128:q*128+128,cp*128:cp*128+128]=x[128:].astype(BF)

def phase_a(m,tab,pr,o0,kk,P,L,psi1):
    for uc in range(2):
        sl=slice(uc*128,uc*128+128)
        a=pr[m,0,:,sl].astype(F32); b=pr[m,1,:,sl].astype(F32)
        c=o0[0,:,sl].astype(F32); d=o0[1,:,sl].astype(F32)
        put_rows(P,0,uc,a*c-b*d); put_rows(P,1,uc,a*d+b*c)
    s1f(tab,P,L)
    for cp in range(2):
        S=s2f(tab,L,cp)
        sl=slice(cp*128,cp*128+128)
        kr=kk[0,:,sl]; ki=kk[1,:,sl]
        put_freq(P,0,cp,S[:,:128]*kr-S[:,128:]*ki)
        put_freq(P,1,cp,S[:,:128]*ki+S[:,128:]*kr)
    s1i(tab,P,L)
    D=s2i(tab,L)
    for uc in range(2):
        sl=slice(uc*128,uc*128+128)
        for q in range(2): psi1[m,q,:,sl]=D[q][uc]

def phase_b(m,tab,o1,P,L,psi1,far,inten):
    for uc in range(2):
        sl=slice(uc*128,uc*128+128)
        a=psi1[m,0,:,sl]; b=psi1[m,1,:,sl]
        c=o1[0,:,sl].astype(F32); d=o1[1,:,sl].astype(F32)
        put_rows(P,0,uc,a*c-b*d); put_rows(P,1,uc,a*d+b*c)
    s1f(tab,P,L)
    for cp in range(2):
        S=s2f(tab,L,cp)
        far[m,cp]=S
        inten[cp]+=S[:,:128]*S[:,:128]+S[:,128:]*S[:,128:]

def phase_c(m,tab,o1,P,L,psi1,far,inten,g1,adj):
    for cp in range(2):
        w=inten[cp]
        put_freq(P,0,cp,w*far[m,cp,:,:128]); put_freq(P,1,cp,w*far[m,cp,:,128:])
    s1i(tab,P,L)
    D=s2i(tab,L)
    for uc in range(2):
        sl=slice(uc*128,uc*128+128)
        br=D[0][uc]; bi=D[1][uc]
        a=psi1[m,0,:,sl]; b=psi1[m,1,:,sl]
        g1[0,:,sl]+=a*br+b*bi; g1[1,:,sl]+=a*bi-b*br
        c=o1[0,:,sl].astype(F32); d=o1[1,:,sl].astype(F32)
        put_rows(adj.at[m],0,uc,c*br+d*bi); put_rows(adj.at[m],1,uc,c*bi-d*br)

def phase_d(m,tab,pr,kk,P,L,adj,g0):
    s1f(tab,adj.at[m],L)
    for cp in range(2):
        S=s2f(tab,L,cp).astype(BF).astype(F32)
        sl=slice(cp*128,cp*128+128)
        kr=kk[0,:,sl]; ki=kk[1,:,sl]
        put_freq(P,0,cp,kr*S[:,:128]+ki*S[:,128:])
        put_freq(P,1,cp,kr*S[:,128:]-ki*S[:,:128])
    s1i(tab,P,L)
    D=s2i(tab,L)
    for uc in range(2):
        sl=slice(uc*128,uc*128+128)
        wr=D[0][uc]; wi=D[1][uc]
        a=pr[m,0,:,sl].astype(F32); b=pr[m,1,:,sl].astype(F32)
        g0[0,:,sl]+=a*wr+b*wi; g0[1,:,sl]+=a*wi-b*wr


MESH = pl.DeviceIdType.MESH


def main_kernel(chips, height, pos, obj, probe_h, phase_h, meas_h, tb_h, tbt_h, out,
                band, w_left, w_right, w_part, near, farw, ob, probe, phase, meas, mtmp,
                tb, tbt, tab, pr, kk, mp, P, L, psi1, far, inten, adj, g, gs,
                in_sem, obj_send, obj_recv, near_send, near_recv, m_send, m_recv,
                g_send, g_recv, loc_sem):
    d = lax.axis_index("depth")
    p = lax.axis_index("pos")
    left = lax.rem(p + chips - 1, chips)
    right = lax.rem(p + 1, chips)
    nb = lax.rem(p + 1 - 2 * d + chips, chips)
    total = 2 * chips
    mine = lax.rem(2 * p - d + total, total)
    other = lax.rem(2 * p + d - 1 + total, total)
    q_left = lax.rem(2 * p - 2 + total, total)
    q_right = 2 * p + 1

    loads = [
        pltpu.make_async_copy(obj, band, in_sem.at[0]),
        pltpu.make_async_copy(meas_h.at[d], mtmp, in_sem.at[1]),
        pltpu.make_async_copy(tb_h, tb, in_sem.at[2]),
        pltpu.make_async_copy(tbt_h, tbt, in_sem.at[3]),
        pltpu.make_async_copy(probe_h, probe, in_sem.at[4]),
        pltpu.make_async_copy(phase_h, phase, in_sem.at[5]),
    ]
    for cp in loads:
        cp.start()
    barrier = pltpu.get_barrier_semaphore()
    peers = ((1 - d, p), (0, left), (1, right), (d, nb))
    for peer in peers:
        pl.semaphore_signal(barrier, inc=1, device_id=peer, device_id_type=MESH)

    blocks = height // N
    row_id = iota((N, N), 0)

    def window(q, part):
        y = pos[q, 0]
        k = y >> 8
        k2 = jnp.minimum(k + 1, blocks - 1)
        a = band[part, k]
        b = band[part, k2]
        return jnp.where(row_id >= (y & 255), a.astype(F32), b.astype(F32)).astype(BF)

    loads[0].wait()
    for part in range(2):
        w_left[part] = window(q_left, part)
    for part in range(2):
        w_right[part] = window(q_right, part)
    for part in range(2):
        w_part[part] = window(other, part)
    pl.semaphore_wait(barrier, 4)

    def remote(src, dst, ss, rs, dev):
        return pltpu.make_async_remote_copy(src_ref=src, dst_ref=dst, send_sem=ss, recv_sem=rs,
                                            device_id=dev, device_id_type=MESH)

    c_left = remote(w_left, farw.at[d], obj_send.at[0], obj_recv.at[d], (0, left))
    c_right = remote(w_right, farw.at[d], obj_send.at[1], obj_recv.at[d], (1, right))
    c_part = remote(w_part, near.at[d], near_send, near_recv, (1 - d, p))
    c_left.start()
    c_right.start()
    c_part.start()
    for part in range(2):
        near[d, part] = window(mine, part)

    loads[1].wait()
    c_meas = remote(meas.at[0], meas.at[1], m_send, m_recv, (1, right))
    meas[0] = mtmp[...].astype(BF)

    @pl.when(d == 1)
    def _():
        c_meas.start()

    y = pos[mine, 0] & 255
    c = pos[mine, 1] & 255
    loads[2].wait()
    loads[3].wait()
    prep_tables(tb, tbt, tab, y, c)
    loads[4].wait()
    prep_probe(probe, pr, None, y, c)
    loads[5].wait()
    prep_k(phase, kk)
    inten[...] = jnp.zeros_like(inten)
    g[...] = jnp.zeros_like(g)

    near_mask = (iota((N, N), 1) - c) * (1 - 2 * d) - d >= 0

    def merge(s):
        for part in range(2):
            ob[s, part] = jnp.where(near_mask, near[s, part].astype(F32),
                                    farw[s, part].astype(F32)).astype(BF)

    def loop(f):
        for m in range(MODES):
            f(m)

    c_part.wait_recv()
    remote(w_left, farw.at[0], obj_send.at[0], obj_recv.at[0], (0, left)).wait_recv()
    merge(0)
    loop(lambda m: phase_a(m, tab, pr, ob.at[0], kk, P, L, psi1))
    remote(w_left, farw.at[1], obj_send.at[0], obj_recv.at[1], (0, left)).wait_recv()
    merge(1)
    loop(lambda m: phase_b(m, tab, ob.at[1], P, L, psi1, far, inten))

    @pl.when(d == 1)
    def _():
        c_meas.wait()

    prep_meas(meas.at[d], mp)
    for cp in range(2):
        inten[cp] = (inten[cp] - mp[:, cp * 128:cp * 128 + 128]) * 0.125
    loop(lambda m: phase_c(m, tab, ob.at[1], P, L, psi1, far, inten, g.at[1], adj))

    def ship(s):
        gs[s] = g[s].astype(BF)
        to_far = remote(gs.at[s], out.at[2 + d], g_send.at[s], g_recv.at[2 + d], (s, nb))
        to_near = remote(gs.at[s], out.at[d], g_send.at[2], g_recv.at[d], (s, p))
        stay = pltpu.make_async_copy(gs.at[s], out.at[d], loc_sem)
        to_far.start()

        @pl.when(d != s)
        def _():
            to_near.start()

        @pl.when(d == s)
        def _():
            stay.start()

        return to_far, to_near, stay

    first = ship(1)
    loop(lambda m: phase_d(m, tab, pr, kk, P, L, adj, g.at[0]))
    last = ship(0)

    c_left.wait_send()
    c_right.wait_send()
    c_part.wait_send()
    for s, (to_far, to_near, stay) in ((1, first), (0, last)):
        to_far.wait_send()

        @pl.when(d != s)
        def _():
            to_near.wait_send()

        @pl.when(d == s)
        def _():
            stay.wait()

    remote(gs.at[0], out.at[1 - d], g_send.at[2], g_recv.at[1 - d], (0, p)).wait_recv()
    remote(gs.at[0], out.at[2], g_send.at[0], g_recv.at[2], (0, nb)).wait_recv()
    remote(gs.at[0], out.at[3], g_send.at[0], g_recv.at[3], (0, nb)).wait_recv()


def final_kernel(chips, blocks, pos, slots, out):
    i = pl.program_id(0)
    p = lax.axis_index("pos")
    total = 2 * chips
    out[...] = jnp.zeros_like(out)
    rows = iota((N, N), 0)
    cols = iota((N, N), 1)
    for slot, (off, ge) in enumerate(((0, True), (total - 1, False), (total - 2, False), (1, True))):
        q = lax.rem(2 * p + off, total)
        y = pos[q, 0]
        k = y >> 8
        yy = y & 255
        c = pos[q, 1] & 255
        cm = (cols >= c) if ge else (cols < c)
        for step in range(2):

            @pl.when(i == k + step)
            def _():
                rm = (rows >= yy) if step == 0 else (rows < yy)
                for part in range(2):
                    out[part] = out[part] + jnp.where(cm & rm, slots[slot, part].astype(F32), 0.0)


def final_wrap(chips, blocks, pos, slots, out, acc):
    final_kernel(chips, blocks, pos, slots, acc)
    out[...] = acc[...].astype(BF)


def local(object_field, probe, prop_phase, measured, positions):
    chips = lax.axis_size("pos")
    height = object_field.shape[2]
    blocks = height // N
    tb, tbt = tables()
    any_ = pl.BlockSpec(memory_space=pl.ANY)
    smem = pl.BlockSpec(memory_space=pltpu.SMEM)
    V = pltpu.VMEM
    win = V((2, N, N), BF)
    dma = pltpu.SemaphoreType.DMA
    slots = pl.pallas_call(
        functools.partial(main_kernel, chips, height),
        out_shape=jax.ShapeDtypeStruct((4, 2, N, N), BF),
        in_specs=[smem] + [pl.BlockSpec(memory_space=pltpu.HBM)] * 6,
        out_specs=any_,
        scratch_shapes=[
            V((2, blocks, N, N), BF), win, win, win, V((2, 2, N, N), BF), V((2, 2, N, N), BF),
            V((2, 2, N, N), BF), V((4, 2, N, N), BF), V((N, N), F32), V((2, N, N), BF), V((N, N), F32),
            V((512, N), BF), V((N, 512), BF), V((4, 2, N, N), BF), V((4, 2, N, N), BF),
            V((2, N, N), F32), V((N, N), F32), V((2, N, N), BF), V((2, N, N), BF),
            V((4, 2, N, N), F32), V((4, 2, N, N), F32), V((2, N, 128), F32), V((4, 2, N, N), BF),
            V((2, 2, N, N), F32), V((2, 2, N, N), BF),
            dma((6,)), dma((2,)), dma((2,)), dma, dma, dma, dma, dma((3,)), dma((4,)), dma,
        ],
        compiler_params=pltpu.CompilerParams(
            collective_id=0, has_side_effects=True, vmem_limit_bytes=48 * 1024 * 1024),
        name="ptycho",
    )(positions, object_field.reshape(2, blocks, N, N), probe, prop_phase, measured, tb, tbt)
    band = pl.pallas_call(
        functools.partial(final_wrap, chips, blocks),
        out_shape=jax.ShapeDtypeStruct((2, height, N), BF),
        grid_spec=pltpu.PrefetchScalarGridSpec(
            num_scalar_prefetch=1, grid=(blocks,),
            in_specs=[pl.BlockSpec((4, 2, N, N), lambda i, s: (0, 0, 0, 0))],
            out_specs=pl.BlockSpec((2, N, N), lambda i, s: (0, i, 0)),
            scratch_shapes=[V((2, N, N), F32)]),
        compiler_params=pltpu.CompilerParams(vmem_limit_bytes=16 * 1024 * 1024),
        name="assemble",
    )(positions, slots)
    return band[None]


def solution(mesh):
    placed = (PS("depth", None, None, "pos"), PS(), PS(), PS("pos", None, None), PS())
    return jax.shard_map(
        local, mesh=mesh, in_specs=placed, out_specs=PS("depth", None, None, "pos"), check_vma=False
    )
```

```python
import functools
import math
import numpy as np
import jax, jax.numpy as jnp
from jax import lax
from jax.experimental import pallas as pl
from jax.experimental.pallas import tpu as pltpu
from jax.sharding import PartitionSpec as PS
BF=jnp.bfloat16; F32=jnp.float32
N=256; HF=128
MODES=4

def tables():
    k=np.arange(N); ph=(k[:,None]*k[None,:])%N
    ang=ph*(2*math.pi/N)
    fr=np.cos(ang)/16.0; fi=-np.sin(ang)/16.0
    tb=np.concatenate([fr[0::2],fi[0::2],fr[1::2],fi[1::2]],0)
    return jnp.asarray(tb,dtype=BF), jnp.asarray(tb.T,dtype=BF)

def dot(a,b): return jnp.dot(a,b,preferred_element_type=F32)
def iota(shape,d): return lax.broadcasted_iota(jnp.int32,shape,d)

def prep_tables(tb,tbt,tab,y,c):
    for r,f1,f2 in ((y,0,1),(c,3,2)):
        onehot=(iota((N,HF),0)==((iota((N,HF),1)-r)&255)).astype(F32).astype(BF)
        m1=dot(tb[...],onehot).astype(BF)
        onet=(iota((HF,N),1)==((iota((HF,N),0)-r)&255)).astype(F32).astype(BF)
        m2=dot(onet,tbt[...]).astype(BF)
        for par in range(2):
            a=m1[par*256:par*256+128]; b=m1[par*256+128:par*256+256]
            tab[f1,par,0:128,0:128]=a; tab[f1,par,0:128,128:256]=-b
            tab[f1,par,128:256,0:128]=b; tab[f1,par,128:256,128:256]=a
            a=m2[:,par*256:par*256+128]; b=m2[:,par*256+128:par*256+256]
            tab[f2,par,0:128,0:128]=a; tab[f2,par,0:128,128:256]=b
            tab[f2,par,128:256,0:128]=-b; tab[f2,par,128:256,128:256]=a

def prep_probe(probe,pr,tmp,y,c):
    ryt=(iota((N,N),1)==((iota((N,N),0)-y)&255)).astype(F32).astype(BF)
    rc=(iota((N,N),0)==((iota((N,N),1)-c)&255)).astype(F32).astype(BF)
    for m in range(4):
        for q in range(2):
            t=dot(ryt,probe[m,q]).astype(BF)
            pr[m,q]=dot(t,rc).astype(BF)

def perms():
    i0=iota((N,N),0); i1=iota((N,N),1)
    pt=(i1==(2*(i0&127)+(i0>>7))).astype(F32).astype(BF)
    p=(i0==(2*(i1&127)+(i1>>7))).astype(F32).astype(BF)
    return pt,p

def prep_k(phase,kk):
    pt,p=perms()
    x=phase[...]
    acc=None
    for _ in range(3):
        h=x.astype(BF)
        x=x-h.astype(F32)
        t=dot(dot(pt,h).astype(BF),p)
        acc=t if acc is None else acc+t
    kk[0]=jnp.cos(acc); kk[1]=jnp.sin(acc)

def prep_meas(meas,mp):
    pt,p=perms()
    mp[...]=dot(dot(pt,meas[...]).astype(BF),p)

def s1f(tab,P,L):
    for par in range(2):
        V=dot(tab[0,par],P[par])
        for q in range(2):
            lo=V[q*128:q*128+128,:128]; hi=V[q*128:q*128+128,128:]
            L[0,par*128:par*128+128,q*128:q*128+128]=(lo+hi).astype(BF)
            L[1,par*128:par*128+128,q*128:q*128+128]=(lo-hi).astype(BF)

def s1i(tab,P,L):
    E0=dot(tab[1,0],P[0]); E1=dot(tab[1,1],P[1])
    for q in range(2):
        for cp in range(2):
            a=E0[q*128:q*128+128,cp*128:cp*128+128]; b=E1[q*128:q*128+128,cp*128:cp*128+128]
            L[cp,0:128,q*128:q*128+128]=(a+b).astype(BF)
            L[cp,128:256,q*128:q*128+128]=(a-b).astype(BF)

def s2f(tab,L,cp): return dot(L[cp],tab[2,cp])
def s2i(tab,L):
    D0=dot(L[0],tab[3,0]); D1=dot(L[1],tab[3,1])
    return [[D0[:,q*128:q*128+128]+D1[:,q*128:q*128+128], D0[:,q*128:q*128+128]-D1[:,q*128:q*128+128]] for q in range(2)]

def put_rows(P,q,uc,x):
    a=x[:128]; b=x[128:]
    P[0,q*128:q*128+128,uc*128:uc*128+128]=(a+b).astype(BF)
    P[1,q*128:q*128+128,uc*128:uc*128+128]=(a-b).astype(BF)

def put_freq(P,q,cp,x):
    P[0,q*128:q*128+128,cp*128:cp*128+128]=x[:128].astype(BF)
    P[1,q*128:q*128+128,cp*128:cp*128+128]=x[128:].astype(BF)

def phase_a(m,tab,pr,o0,kk,P,L,psi1):
    for uc in range(2):
        sl=slice(uc*128,uc*128+128)
        a=pr[m,0,:,sl].astype(F32); b=pr[m,1,:,sl].astype(F32)
        c=o0[0,:,sl].astype(F32); d=o0[1,:,sl].astype(F32)
        put_rows(P,0,uc,a*c-b*d); put_rows(P,1,uc,a*d+b*c)
    s1f(tab,P,L)
    for cp in range(2):
        S=s2f(tab,L,cp)
        sl=slice(cp*128,cp*128+128)
        kr=kk[0,:,sl]; ki=kk[1,:,sl]
        put_freq(P,0,cp,S[:,:128]*kr-S[:,128:]*ki)
        put_freq(P,1,cp,S[:,:128]*ki+S[:,128:]*kr)
    s1i(tab,P,L)
    D=s2i(tab,L)
    for uc in range(2):
        sl=slice(uc*128,uc*128+128)
        for q in range(2): psi1[m,q,:,sl]=D[q][uc]

def phase_b(m,tab,o1,P,L,psi1,far,inten):
    for uc in range(2):
        sl=slice(uc*128,uc*128+128)
        a=psi1[m,0,:,sl]; b=psi1[m,1,:,sl]
        c=o1[0,:,sl].astype(F32); d=o1[1,:,sl].astype(F32)
        put_rows(P,0,uc,a*c-b*d); put_rows(P,1,uc,a*d+b*c)
    s1f(tab,P,L)
    for cp in range(2):
        S=s2f(tab,L,cp)
        far[m,cp]=S
        inten[cp]+=S[:,:128]*S[:,:128]+S[:,128:]*S[:,128:]

def phase_c(m,tab,o1,P,L,psi1,far,inten,g1,adj):
    for cp in range(2):
        w=inten[cp]
        put_freq(P,0,cp,w*far[m,cp,:,:128]); put_freq(P,1,cp,w*far[m,cp,:,128:])
    s1i(tab,P,L)
    D=s2i(tab,L)
    for uc in range(2):
        sl=slice(uc*128,uc*128+128)
        br=D[0][uc]; bi=D[1][uc]
        a=psi1[m,0,:,sl]; b=psi1[m,1,:,sl]
        g1[0,:,sl]+=a*br+b*bi; g1[1,:,sl]+=a*bi-b*br
        c=o1[0,:,sl].astype(F32); d=o1[1,:,sl].astype(F32)
        put_rows(adj.at[m],0,uc,c*br+d*bi); put_rows(adj.at[m],1,uc,c*bi-d*br)

def phase_d(m,tab,kk,P,L,L2,adj):
    s1f(tab,adj.at[m],L)
    for cp in range(2):
        S=s2f(tab,L,cp).astype(BF).astype(F32)
        sl=slice(cp*128,cp*128+128)
        kr=kk[0,:,sl]; ki=kk[1,:,sl]
        put_freq(P,0,cp,kr*S[:,:128]+ki*S[:,128:])
        put_freq(P,1,cp,kr*S[:,128:]-ki*S[:,:128])
    E0=dot(tab[1,0],P[0]); E1=dot(tab[1,1],P[1])
    for q in range(2):
        for cp in range(2):
            for h in range(2):
                r=slice(q*128+h*64,q*128+h*64+64); sl=slice(cp*128,cp*128+128); to=slice(q*128,q*128+128)
                L2[cp,h,m,:,to]=(E0[r,sl]+E1[r,sl]).astype(BF)
                L2[cp,2+h,m,:,to]=(E0[r,sl]-E1[r,sl]).astype(BF)

def phase_e(r,tab,pr,L2,gs):
    D0=dot(L2[0,r].reshape(256,256),tab[3,0]); D1=dot(L2[1,r].reshape(256,256),tab[3,1])
    rows=slice(r*64,r*64+64)
    for uc in range(2):
        sl=slice(uc*128,uc*128+128)
        W=[D0[:,q*128:q*128+128]+D1[:,q*128:q*128+128] if uc==0 else D0[:,q*128:q*128+128]-D1[:,q*128:q*128+128] for q in range(2)]
        gr=None
        for m in range(4):
            wr=W[0][m*64:m*64+64]; wi=W[1][m*64:m*64+64]
            a=pr[m,0,rows,sl].astype(F32); b=pr[m,1,rows,sl].astype(F32)
            tr=a*wr+b*wi; ti=a*wi-b*wr
            gr,gi=(tr,ti) if gr is None else (gr+tr,gi+ti)
        gs[0,rows,sl]=gr.astype(BF); gs[1,rows,sl]=gi.astype(BF)


MESH = pl.DeviceIdType.MESH


def main_kernel(chips, height, pos_h, obj, probe_h, phase_h, meas_h, tb_h, tbt_h, out,
                pos, band, w_left, w_right, w_part, near, farw, ob, probe, phase, meas, mtmp,
                tb, tbt, tab, pr, kk, mp, P, L, psi1, far, inten, adj, L2, g, gs,
                in_sem, obj_send, obj_recv, near_send, near_recv, m_send, m_recv,
                g_send, g_recv, c_send, c_recv, loc_sem):
    d = lax.axis_index("depth")
    p = lax.axis_index("pos")
    left = lax.rem(p + chips - 1, chips)
    right = lax.rem(p + 1, chips)
    nb = lax.rem(p + 1 - 2 * d + chips, chips)
    total = 2 * chips
    mine = lax.rem(2 * p - d + total, total)
    other = lax.rem(2 * p + d - 1 + total, total)
    q_left = lax.rem(2 * p - 2 + total, total)
    q_right = 2 * p + 1

    loads = [
        pltpu.make_async_copy(obj, band, in_sem.at[0]),
        pltpu.make_async_copy(meas_h.at[d], mtmp, in_sem.at[1]),
        pltpu.make_async_copy(tb_h, tb, in_sem.at[2]),
        pltpu.make_async_copy(tbt_h, tbt, in_sem.at[3]),
        pltpu.make_async_copy(probe_h, probe, in_sem.at[4]),
        pltpu.make_async_copy(phase_h, phase, in_sem.at[5]),
        pltpu.make_async_copy(pos_h, pos, in_sem.at[6]),
    ]
    for cp in loads:
        cp.start()
    barrier = pltpu.get_barrier_semaphore()
    peers = ((1 - d, p), (0, left), (1, right), (d, nb))
    for peer in peers:
        pl.semaphore_signal(barrier, inc=1, device_id=peer, device_id_type=MESH)

    blocks = height // N
    row_id = iota((N, N), 0)

    def window(q, part):
        y = pos[0, q]
        k = y >> 8
        k2 = jnp.minimum(k + 1, blocks - 1)
        a = band[part, k]
        b = band[part, k2]
        return jnp.where(row_id >= (y & 255), a.astype(F32), b.astype(F32)).astype(BF)

    loads[6].wait()
    loads[0].wait()
    for part in range(2):
        w_left[part] = window(q_left, part)
    for part in range(2):
        w_right[part] = window(q_right, part)
    for part in range(2):
        w_part[part] = window(other, part)
    pl.semaphore_wait(barrier, 4)

    def remote(src, dst, ss, rs, dev):
        return pltpu.make_async_remote_copy(src_ref=src, dst_ref=dst, send_sem=ss, recv_sem=rs,
                                            device_id=dev, device_id_type=MESH)

    c_left = remote(w_left, farw.at[d], obj_send.at[0], obj_recv.at[d], (0, left))
    c_right = remote(w_right, farw.at[d], obj_send.at[1], obj_recv.at[d], (1, right))
    c_part = remote(w_part, near.at[d], near_send, near_recv, (1 - d, p))
    c_part.start()

    @pl.when(d == 0)
    def _():
        c_left.start()
        c_right.start()

    for part in range(2):
        near[d, part] = window(mine, part)

    loads[1].wait()
    c_meas = remote(meas.at[0], meas.at[1], m_send, m_recv, (1, right))
    meas[0] = mtmp[...].astype(BF)

    y = pos[0, mine] & 255
    c = pos[1, mine] & 255
    loads[2].wait()
    loads[3].wait()
    prep_tables(tb, tbt, tab, y, c)
    loads[4].wait()
    prep_probe(probe, pr, None, y, c)
    @pl.when(d == 1)
    def _():
        c_left.start()
        c_right.start()
        c_meas.start()

    loads[5].wait()
    prep_k(phase, kk)
    inten[...] = jnp.zeros_like(inten)
    g[...] = jnp.zeros_like(g)

    near_mask = (iota((N, N), 1) - c) * (1 - 2 * d) - d >= 0

    def merge(s):
        for part in range(2):
            ob[s, part] = jnp.where(near_mask, near[s, part].astype(F32),
                                    farw[s, part].astype(F32)).astype(BF)

    def loop(f):
        for m in range(MODES):
            f(m)

    c_part.wait_recv()
    remote(w_left, farw.at[0], obj_send.at[0], obj_recv.at[0], (0, left)).wait_recv()
    merge(0)
    loop(lambda m: phase_a(m, tab, pr, ob.at[0], kk, P, L, psi1))
    remote(w_left, farw.at[1], obj_send.at[0], obj_recv.at[1], (0, left)).wait_recv()
    merge(1)
    loop(lambda m: phase_b(m, tab, ob.at[1], P, L, psi1, far, inten))

    @pl.when(d == 1)
    def _():
        c_meas.wait()

    prep_meas(meas.at[d], mp)
    for cp in range(2):
        inten[cp] = (inten[cp] - mp[:, cp * 128:cp * 128 + 128]) * 0.125
    loop(lambda m: phase_c(m, tab, ob.at[1], P, L, psi1, far, inten, g, adj))

    gs[1] = g[...].astype(BF)
    far1 = remote(gs.at[1], out.at[2 + d], g_send.at[0], g_recv.at[2 + d], (1, nb))
    near1 = remote(gs.at[1], out.at[d], g_send.at[1], g_recv.at[d], (1, p))
    stay1 = pltpu.make_async_copy(gs.at[1], out.at[d], loc_sem)
    far1.start()

    @pl.when(d == 0)
    def _():
        near1.start()

    @pl.when(d == 1)
    def _():
        stay1.start()

    loop(lambda m: phase_d(m, tab, kk, P, L, L2, adj))

    def chunk(r, dev):
        rows = pl.ds(r * 64, 64)
        return remote(gs.at[0, :, rows, :], out.at[2 + d, :, rows, :], c_send.at[r], c_recv.at[d, r], dev)

    def incoming(slot, r):
        rows = pl.ds(r * 64, 64)
        return remote(gs.at[0, :, rows, :], out.at[2 + slot, :, rows, :], c_send.at[r], c_recv.at[slot, r],
                      (0, nb))

    for r in range(4):
        phase_e(r, tab, pr, L2, gs.at[0])
        chunk(r, (0, nb)).start()
    near0 = remote(gs.at[0], out.at[d], g_send.at[1], g_recv.at[d], (0, p))
    stay0 = pltpu.make_async_copy(gs.at[0], out.at[d], loc_sem)

    @pl.when(d == 1)
    def _():
        near0.start()
        stay1.wait()

    @pl.when(d == 0)
    def _():
        stay0.start()
        near1.wait_send()

    c_left.wait_send()
    c_right.wait_send()
    c_part.wait_send()
    far1.wait_send()
    for r in range(4):
        chunk(r, (0, nb)).wait_send()

    @pl.when(d == 1)
    def _():
        near0.wait_send()
        remote(gs.at[1], out.at[0], g_send.at[1], g_recv.at[0], (0, p)).wait_recv()
        for k in range(2):
            remote(gs.at[1], out.at[2 + k], g_send.at[0], g_recv.at[2 + k], (1, nb)).wait_recv()

    @pl.when(d == 0)
    def _():
        stay0.wait()
        remote(gs.at[0], out.at[1], g_send.at[1], g_recv.at[1], (0, p)).wait_recv()
        for k in range(2):
            for r in range(4):
                incoming(k, r).wait_recv()


def final_kernel(chips, blocks, pos_h, slots, out, pos, acc, ob, sem, pos_sem):
    load = pltpu.make_async_copy(pos_h, pos, pos_sem)
    load.start()
    p = lax.axis_index("pos")
    total = 2 * chips
    acc[...] = jnp.zeros_like(acc)
    load.wait()
    rows = iota((N, N), 0)
    cols = iota((N, N), 1)
    for slot, (off, ge) in enumerate(((0, True), (total - 1, False), (total - 2, False), (1, True))):
        q = lax.rem(2 * p + off, total)
        y = pos[0, q]
        k = y >> 8
        k2 = jnp.minimum(k + 1, blocks - 1)
        yy = y & 255
        c = pos[1, q] & 255
        cm = (cols >= c) if ge else (cols < c)
        for part in range(2):
            x = slots[slot, part].astype(F32)
            acc[part, k] += jnp.where(cm & (rows >= yy), x, 0.0)
            acc[part, k2] += jnp.where(cm & (rows < yy), x, 0.0)
    copies = []
    for i in range(blocks):
        ob[:, i] = acc[:, i].astype(BF)
        cp = pltpu.make_async_copy(ob.at[:, i], out.at[:, i], sem.at[i])
        cp.start()
        copies.append(cp)
    for cp in copies:
        cp.wait()


def local(object_field, probe, prop_phase, measured, positions):
    chips = lax.axis_size("pos")
    height = object_field.shape[2]
    blocks = height // N
    tb, tbt = tables()
    pos_t = positions.T
    any_ = pl.BlockSpec(memory_space=pl.ANY)
    V = pltpu.VMEM
    win = V((2, N, N), BF)
    dma = pltpu.SemaphoreType.DMA
    slots = pl.pallas_call(
        functools.partial(main_kernel, chips, height),
        out_shape=jax.ShapeDtypeStruct((4, 2, N, N), BF),
        in_specs=[pl.BlockSpec(memory_space=pltpu.HBM)] * 7,
        out_specs=any_,
        scratch_shapes=[
            pltpu.SMEM((2, 2 * chips), jnp.int32), V((2, blocks, N, N), BF), win, win, win, V((2, 2, N, N), BF), V((2, 2, N, N), BF),
            V((2, 2, N, N), BF), V((4, 2, N, N), BF), V((N, N), F32), V((2, N, N), BF), V((N, N), F32),
            V((512, N), BF), V((N, 512), BF), V((4, 2, N, N), BF), V((4, 2, N, N), BF),
            V((2, N, N), F32), V((N, N), F32), V((2, N, N), BF), V((2, N, N), BF),
            V((4, 2, N, N), F32), V((4, 2, N, N), F32), V((2, N, 128), F32), V((4, 2, N, N), BF),
            V((2, 4, 4, 64, N), BF), V((2, N, N), F32), V((2, 2, N, N), BF),
            dma((7,)), dma((2,)), dma((2,)), dma, dma, dma, dma, dma((2,)), dma((4,)), dma((4,)), dma((2, 4)), dma,
        ],
        compiler_params=pltpu.CompilerParams(
            collective_id=0, has_side_effects=True, vmem_limit_bytes=48 * 1024 * 1024),
        name="ptycho",
    )(*(pltpu.with_memory_space_constraint(a, pltpu.HBM) for a in (
        pos_t, object_field.reshape(2, blocks, N, N), probe, prop_phase, measured, tb, tbt)))
    band = pl.pallas_call(
        functools.partial(final_kernel, chips, blocks),
        out_shape=jax.ShapeDtypeStruct((2, blocks, N, N), BF),
        in_specs=[pl.BlockSpec(memory_space=pltpu.HBM), pl.BlockSpec(memory_space=pltpu.VMEM)],
        out_specs=pl.BlockSpec(memory_space=pltpu.HBM),
        scratch_shapes=[pltpu.SMEM((2, 2 * chips), jnp.int32), V((2, blocks, N, N), F32), V((2, blocks, N, N), BF),
                        dma((blocks,)), dma],
        compiler_params=pltpu.CompilerParams(vmem_limit_bytes=32 * 1024 * 1024),
        name="assemble",
    )(pltpu.with_memory_space_constraint(pos_t, pltpu.HBM), slots)
    return band.reshape(1, 2, height, N)


def solution(mesh):
    placed = (PS("depth", None, None, "pos"), PS(), PS(), PS("pos", None, None), PS())
    return jax.shard_map(
        local, mesh=mesh, in_specs=placed, out_specs=PS("depth", None, None, "pos"), check_vma=False
    )
```

```python
import functools
import math
import numpy as np
import jax, jax.numpy as jnp
from jax import lax
from jax.experimental import pallas as pl
from jax.experimental.pallas import tpu as pltpu
from jax.sharding import PartitionSpec as PS
BF=jnp.bfloat16; F32=jnp.float32
N=256; HF=128
MODES=4

def tables():
    k=np.arange(N); ph=(k[:,None]*k[None,:])%N
    ang=ph*(2*math.pi/N)
    fr=np.cos(ang)/16.0; fi=-np.sin(ang)/16.0
    tb=np.concatenate([fr[0::2],fi[0::2],fr[1::2],fi[1::2]],0)
    return jnp.asarray(tb,dtype=BF), jnp.asarray(tb.T,dtype=BF)

def dot(a,b): return jnp.dot(a,b,preferred_element_type=F32)
def iota(shape,d): return lax.broadcasted_iota(jnp.int32,shape,d)

def prep_tables(tb,tbt,tab,y,c):
    for r,f1,f2 in ((y,0,1),(c,3,2)):
        onehot=(iota((N,HF),0)==((iota((N,HF),1)-r)&255)).astype(F32).astype(BF)
        m1=dot(tb[...],onehot).astype(BF)
        onet=(iota((HF,N),1)==((iota((HF,N),0)-r)&255)).astype(F32).astype(BF)
        m2=dot(onet,tbt[...]).astype(BF)
        for par in range(2):
            a=m1[par*256:par*256+128]; b=m1[par*256+128:par*256+256]
            tab[f1,par,0:128,0:128]=a; tab[f1,par,0:128,128:256]=-b
            tab[f1,par,128:256,0:128]=b; tab[f1,par,128:256,128:256]=a
            a=m2[:,par*256:par*256+128]; b=m2[:,par*256+128:par*256+256]
            tab[f2,par,0:128,0:128]=a; tab[f2,par,0:128,128:256]=b
            tab[f2,par,128:256,0:128]=-b; tab[f2,par,128:256,128:256]=a

def prep_probe(probe,pr,tmp,y,c):
    ryt=(iota((N,N),1)==((iota((N,N),0)-y)&255)).astype(F32).astype(BF)
    rc=(iota((N,N),0)==((iota((N,N),1)-c)&255)).astype(F32).astype(BF)
    for m in range(4):
        for q in range(2):
            t=dot(ryt,probe[m,q]).astype(BF)
            pr[m,q]=dot(t,rc).astype(BF)

def perms():
    i0=iota((N,N),0); i1=iota((N,N),1)
    pt=(i1==(2*(i0&127)+(i0>>7))).astype(F32).astype(BF)
    p=(i0==(2*(i1&127)+(i1>>7))).astype(F32).astype(BF)
    return pt,p

def prep_k(phase,kk):
    pt,p=perms()
    x=phase[...]
    acc=None
    for _ in range(3):
        h=x.astype(BF)
        x=x-h.astype(F32)
        t=dot(dot(pt,h).astype(BF),p)
        acc=t if acc is None else acc+t
    kk[0]=jnp.cos(acc); kk[1]=jnp.sin(acc)

def prep_meas(meas,mp):
    pt,p=perms()
    mp[...]=dot(dot(pt,meas[...]).astype(BF),p)

def s1f(tab,P,L):
    for par in range(2):
        V=dot(tab[0,par],P[par])
        for q in range(2):
            lo=V[q*128:q*128+128,:128]; hi=V[q*128:q*128+128,128:]
            L[0,par*128:par*128+128,q*128:q*128+128]=(lo+hi).astype(BF)
            L[1,par*128:par*128+128,q*128:q*128+128]=(lo-hi).astype(BF)

def s1i(tab,P,L):
    E0=dot(tab[1,0],P[0]); E1=dot(tab[1,1],P[1])
    for q in range(2):
        for cp in range(2):
            a=E0[q*128:q*128+128,cp*128:cp*128+128]; b=E1[q*128:q*128+128,cp*128:cp*128+128]
            L[cp,0:128,q*128:q*128+128]=(a+b).astype(BF)
            L[cp,128:256,q*128:q*128+128]=(a-b).astype(BF)

def s2f(tab,L,cp): return dot(L[cp],tab[2,cp])
def s2i(tab,L):
    D0=dot(L[0],tab[3,0]); D1=dot(L[1],tab[3,1])
    return [[D0[:,q*128:q*128+128]+D1[:,q*128:q*128+128], D0[:,q*128:q*128+128]-D1[:,q*128:q*128+128]] for q in range(2)]

def put_rows(P,q,uc,x):
    a=x[:128]; b=x[128:]
    P[0,q*128:q*128+128,uc*128:uc*128+128]=(a+b).astype(BF)
    P[1,q*128:q*128+128,uc*128:uc*128+128]=(a-b).astype(BF)

def put_freq(P,q,cp,x):
    P[0,q*128:q*128+128,cp*128:cp*128+128]=x[:128].astype(BF)
    P[1,q*128:q*128+128,cp*128:cp*128+128]=x[128:].astype(BF)

def phase_a(m,tab,pr,o0,kk,P,L,psi1):
    for uc in range(2):
        sl=slice(uc*128,uc*128+128)
        a=pr[m,0,:,sl].astype(F32); b=pr[m,1,:,sl].astype(F32)
        c=o0[0,:,sl].astype(F32); d=o0[1,:,sl].astype(F32)
        put_rows(P,0,uc,a*c-b*d); put_rows(P,1,uc,a*d+b*c)
    s1f(tab,P,L)
    for cp in range(2):
        S=s2f(tab,L,cp)
        sl=slice(cp*128,cp*128+128)
        kr=kk[0,:,sl]; ki=kk[1,:,sl]
        put_freq(P,0,cp,S[:,:128]*kr-S[:,128:]*ki)
        put_freq(P,1,cp,S[:,:128]*ki+S[:,128:]*kr)
    s1i(tab,P,L)
    D=s2i(tab,L)
    for uc in range(2):
        sl=slice(uc*128,uc*128+128)
        for q in range(2): psi1[m,q,:,sl]=D[q][uc]

def phase_b(m,tab,o1,P,L,psi1,far,inten):
    for uc in range(2):
        sl=slice(uc*128,uc*128+128)
        a=psi1[m,0,:,sl]; b=psi1[m,1,:,sl]
        c=o1[0,:,sl].astype(F32); d=o1[1,:,sl].astype(F32)
        put_rows(P,0,uc,a*c-b*d); put_rows(P,1,uc,a*d+b*c)
    s1f(tab,P,L)
    for cp in range(2):
        S=s2f(tab,L,cp)
        far[m,cp]=S
        inten[cp]+=S[:,:128]*S[:,:128]+S[:,128:]*S[:,128:]

def phase_c(m,tab,o1,P,L,psi1,far,inten,g1,adj):
    for cp in range(2):
        w=inten[cp]
        put_freq(P,0,cp,w*far[m,cp,:,:128]); put_freq(P,1,cp,w*far[m,cp,:,128:])
    s1i(tab,P,L)
    D=s2i(tab,L)
    for uc in range(2):
        sl=slice(uc*128,uc*128+128)
        br=D[0][uc]; bi=D[1][uc]
        a=psi1[m,0,:,sl]; b=psi1[m,1,:,sl]
        g1[0,:,sl]+=a*br+b*bi; g1[1,:,sl]+=a*bi-b*br
        c=o1[0,:,sl].astype(F32); d=o1[1,:,sl].astype(F32)
        put_rows(adj.at[m],0,uc,c*br+d*bi); put_rows(adj.at[m],1,uc,c*bi-d*br)

def phase_d(m,tab,kk,P,L,L2,adj):
    s1f(tab,adj.at[m],L)
    for cp in range(2):
        S=s2f(tab,L,cp).astype(BF).astype(F32)
        sl=slice(cp*128,cp*128+128)
        kr=kk[0,:,sl]; ki=kk[1,:,sl]
        put_freq(P,0,cp,kr*S[:,:128]+ki*S[:,128:])
        put_freq(P,1,cp,kr*S[:,128:]-ki*S[:,:128])
    E0=dot(tab[1,0],P[0]); E1=dot(tab[1,1],P[1])
    for q in range(2):
        for cp in range(2):
            for h in range(2):
                r=slice(q*128+h*64,q*128+h*64+64); sl=slice(cp*128,cp*128+128); to=slice(q*128,q*128+128)
                L2[cp,h,m,:,to]=(E0[r,sl]+E1[r,sl]).astype(BF)
                L2[cp,2+h,m,:,to]=(E0[r,sl]-E1[r,sl]).astype(BF)

def phase_e(r,tab,pr,L2,gs):
    D0=dot(L2[0,r].reshape(256,256),tab[3,0]); D1=dot(L2[1,r].reshape(256,256),tab[3,1])
    rows=slice(r*64,r*64+64)
    for uc in range(2):
        sl=slice(uc*128,uc*128+128)
        W=[D0[:,q*128:q*128+128]+D1[:,q*128:q*128+128] if uc==0 else D0[:,q*128:q*128+128]-D1[:,q*128:q*128+128] for q in range(2)]
        gr=None
        for m in range(4):
            wr=W[0][m*64:m*64+64]; wi=W[1][m*64:m*64+64]
            a=pr[m,0,rows,sl].astype(F32); b=pr[m,1,rows,sl].astype(F32)
            tr=a*wr+b*wi; ti=a*wi-b*wr
            gr,gi=(tr,ti) if gr is None else (gr+tr,gi+ti)
        gs[0,rows,sl]=gr.astype(BF); gs[1,rows,sl]=gi.astype(BF)


MESH = pl.DeviceIdType.MESH


def main_kernel(chips, height, pos_h, obj, probe_h, phase_h, meas_h, tb_h, tbt_h, out,
                pos, band, w_left, w_right, w_part, near, farw, ob, probe, phase, meas, mtmp,
                tb, tbt, tab, pr, kk, mp, P, L, psi1, far, inten, adj, L2, g, gs,
                in_sem, obj_send, obj_recv, near_send, near_recv, m_send, m_recv,
                g_send, g_recv, c_send, c_recv, loc_sem, turn):
    d = lax.axis_index("depth")
    p = lax.axis_index("pos")
    left = lax.rem(p + chips - 1, chips)
    right = lax.rem(p + 1, chips)
    nb = lax.rem(p + 1 - 2 * d + chips, chips)
    total = 2 * chips
    mine = lax.rem(2 * p - d + total, total)
    other = lax.rem(2 * p + d - 1 + total, total)
    q_left = lax.rem(2 * p - 2 + total, total)
    q_right = 2 * p + 1

    loads = [
        pltpu.make_async_copy(obj, band, in_sem.at[0]),
        pltpu.make_async_copy(meas_h.at[d], mtmp, in_sem.at[1]),
        pltpu.make_async_copy(tb_h, tb, in_sem.at[2]),
        pltpu.make_async_copy(tbt_h, tbt, in_sem.at[3]),
        pltpu.make_async_copy(probe_h, probe, in_sem.at[4]),
        pltpu.make_async_copy(phase_h, phase, in_sem.at[5]),
        pltpu.make_async_copy(pos_h, pos, in_sem.at[6]),
    ]
    for cp in loads:
        cp.start()
    barrier = pltpu.get_barrier_semaphore()
    peers = ((1 - d, p), (0, left), (1, right), (d, nb))
    for peer in peers:
        pl.semaphore_signal(barrier, inc=1, device_id=peer, device_id_type=MESH)

    blocks = height // N
    row_id = iota((N, N), 0)

    def window(q, part):
        y = pos[0, q]
        k = y >> 8
        k2 = jnp.minimum(k + 1, blocks - 1)
        a = band[part, k]
        b = band[part, k2]
        return jnp.where(row_id >= (y & 255), a.astype(F32), b.astype(F32)).astype(BF)

    loads[6].wait()
    loads[0].wait()
    for part in range(2):
        w_left[part] = window(q_left, part)
    for part in range(2):
        w_right[part] = window(q_right, part)
    for part in range(2):
        w_part[part] = window(other, part)
    for part in range(2):
        near[d, part] = window(mine, part)
    y = pos[0, mine] & 255
    c = pos[1, mine] & 255
    loads[2].wait()
    loads[3].wait()
    prep_tables(tb, tbt, tab, y, c)
    loads[4].wait()
    prep_probe(probe, pr, None, y, c)
    pl.semaphore_wait(barrier, 4)

    def remote(src, dst, ss, rs, dev):
        return pltpu.make_async_remote_copy(src_ref=src, dst_ref=dst, send_sem=ss, recv_sem=rs,
                                            device_id=dev, device_id_type=MESH)

    c_left = remote(w_left, farw.at[d], obj_send.at[0], obj_recv.at[d], (0, left))
    c_right = remote(w_right, farw.at[d], obj_send.at[1], obj_recv.at[d], (1, right))
    c_part = remote(w_part, near.at[d], near_send, near_recv, (1 - d, p))
    go_left = p > 0
    wrap_a = jnp.logical_and(d == 0, p == chips - 1)

    def send_object():
        @pl.when(go_left)
        def _():
            c_left.start()

        c_right.start()

    def sent_object():
        @pl.when(go_left)
        def _():
            c_left.wait_send()

        c_right.wait_send()

    @pl.when(d == 0)
    def _():
        send_object()

    c_part.start()
    loads[1].wait()
    c_meas = remote(meas.at[0], meas.at[1], m_send, m_recv, (1, right))
    meas[0] = mtmp[...].astype(BF)
    loads[5].wait()
    prep_k(phase, kk)

    @pl.when(d == 0)
    def _():
        sent_object()
        pl.semaphore_signal(turn, inc=1, device_id=(1, p), device_id_type=MESH)

    @pl.when(d == 1)
    def _():
        pl.semaphore_wait(turn, 1)
        send_object()
        c_meas.start()

    inten[...] = jnp.zeros_like(inten)
    g[...] = jnp.zeros_like(g)

    near_mask = (iota((N, N), 1) - c) * (1 - 2 * d) - d >= 0

    def merge(s):
        for part in range(2):
            ob[s, part] = jnp.where(near_mask, near[s, part].astype(F32),
                                    farw[s, part].astype(F32)).astype(BF)

    def loop(f):
        for m in range(MODES):
            f(m)

    c_part.wait_recv()

    def got_far(k):
        @pl.when(jnp.logical_not(wrap_a))
        def _():
            remote(w_left, farw.at[k], obj_send.at[0], obj_recv.at[k], (0, left)).wait_recv()

    got_far(0)
    merge(0)
    loop(lambda m: phase_a(m, tab, pr, ob.at[0], kk, P, L, psi1))
    got_far(1)
    merge(1)
    loop(lambda m: phase_b(m, tab, ob.at[1], P, L, psi1, far, inten))

    @pl.when(d == 1)
    def _():
        c_meas.wait()

    prep_meas(meas.at[d], mp)
    for cp in range(2):
        inten[cp] = (inten[cp] - mp[:, cp * 128:cp * 128 + 128]) * 0.125
    loop(lambda m: phase_c(m, tab, ob.at[1], P, L, psi1, far, inten, g, adj))

    gs[1] = g[...].astype(BF)
    far1 = remote(gs.at[1], out.at[2 + d], g_send.at[0], g_recv.at[2 + d], (1, nb))
    near1 = remote(gs.at[1], out.at[d], g_send.at[1], g_recv.at[d], (1, p))
    stay1 = pltpu.make_async_copy(gs.at[1], out.at[d], loc_sem)

    @pl.when(jnp.logical_not(wrap_a))
    def _():
        far1.start()

    @pl.when(d == 0)
    def _():
        near1.start()

    @pl.when(d == 1)
    def _():
        stay1.start()

    loop(lambda m: phase_d(m, tab, kk, P, L, L2, adj))

    def chunk(r, dev):
        rows = pl.ds(r * 64, 64)
        return remote(gs.at[0, :, rows, :], out.at[2 + d, :, rows, :], c_send.at[r], c_recv.at[d, r], dev)

    def incoming(slot, r):
        rows = pl.ds(r * 64, 64)
        return remote(gs.at[0, :, rows, :], out.at[2 + slot, :, rows, :], c_send.at[r], c_recv.at[slot, r],
                      (0, nb))

    for r in range(4):
        phase_e(r, tab, pr, L2, gs.at[0])

        @pl.when(jnp.logical_not(wrap_a))
        def _():
            chunk(r, (0, nb)).start()

    near0 = remote(gs.at[0], out.at[d], g_send.at[1], g_recv.at[d], (0, p))
    stay0 = pltpu.make_async_copy(gs.at[0], out.at[d], loc_sem)

    @pl.when(d == 1)
    def _():
        near0.start()
        stay1.wait()

    @pl.when(d == 0)
    def _():
        stay0.start()
        near1.wait_send()

    @pl.when(d == 1)
    def _():
        sent_object()

    c_part.wait_send()

    @pl.when(jnp.logical_not(wrap_a))
    def _():
        far1.wait_send()
        for r in range(4):
            chunk(r, (0, nb)).wait_send()

    @pl.when(d == 1)
    def _():
        near0.wait_send()
        remote(gs.at[1], out.at[0], g_send.at[1], g_recv.at[0], (0, p)).wait_recv()
        remote(gs.at[1], out.at[3], g_send.at[0], g_recv.at[3], (1, nb)).wait_recv()

        @pl.when(p > 0)
        def _():
            remote(gs.at[1], out.at[2], g_send.at[0], g_recv.at[2], (1, nb)).wait_recv()

    @pl.when(d == 0)
    def _():
        stay0.wait()
        remote(gs.at[0], out.at[1], g_send.at[1], g_recv.at[1], (0, p)).wait_recv()
        for r in range(4):
            incoming(1, r).wait_recv()

        @pl.when(p > 0)
        def _():
            for r in range(4):
                incoming(0, r).wait_recv()


def final_kernel(chips, blocks, pos_h, slots, out, pos, acc, ob, sem, pos_sem):
    load = pltpu.make_async_copy(pos_h, pos, pos_sem)
    load.start()
    p = lax.axis_index("pos")
    total = 2 * chips
    acc[...] = jnp.zeros_like(acc)
    load.wait()
    rows = iota((N, N), 0)
    cols = iota((N, N), 1)
    for slot, (off, ge) in enumerate(((0, True), (total - 1, False), (total - 2, False), (1, True))):
        q = lax.rem(2 * p + off, total)
        y = pos[0, q]
        k = y >> 8
        k2 = jnp.minimum(k + 1, blocks - 1)
        yy = y & 255
        c = pos[1, q] & 255
        cm = (cols >= c) if ge else (cols < c)
        for part in range(2):
            x = slots[slot, part].astype(F32)
            acc[part, k] += jnp.where(cm & (rows >= yy), x, 0.0)
            acc[part, k2] += jnp.where(cm & (rows < yy), x, 0.0)
    copies = []
    for i in range(blocks):
        ob[:, i] = acc[:, i].astype(BF)
        cp = pltpu.make_async_copy(ob.at[:, i], out.at[:, i], sem.at[i])
        cp.start()
        copies.append(cp)
    for cp in copies:
        cp.wait()


def local(object_field, probe, prop_phase, measured, positions):
    chips = lax.axis_size("pos")
    height = object_field.shape[2]
    blocks = height // N
    tb, tbt = tables()
    pos_t = positions.T
    any_ = pl.BlockSpec(memory_space=pl.ANY)
    V = pltpu.VMEM
    win = V((2, N, N), BF)
    dma = pltpu.SemaphoreType.DMA
    slots = pl.pallas_call(
        functools.partial(main_kernel, chips, height),
        out_shape=jax.ShapeDtypeStruct((4, 2, N, N), BF),
        in_specs=[pl.BlockSpec(memory_space=pltpu.HBM)] * 7,
        out_specs=any_,
        scratch_shapes=[
            pltpu.SMEM((2, 2 * chips), jnp.int32), V((2, blocks, N, N), BF), win, win, win, V((2, 2, N, N), BF), V((2, 2, N, N), BF),
            V((2, 2, N, N), BF), V((4, 2, N, N), BF), V((N, N), F32), V((2, N, N), BF), V((N, N), F32),
            V((512, N), BF), V((N, 512), BF), V((4, 2, N, N), BF), V((4, 2, N, N), BF),
            V((2, N, N), F32), V((N, N), F32), V((2, N, N), BF), V((2, N, N), BF),
            V((4, 2, N, N), F32), V((4, 2, N, N), F32), V((2, N, 128), F32), V((4, 2, N, N), BF),
            V((2, 4, 4, 64, N), BF), V((2, N, N), F32), V((2, 2, N, N), BF),
            dma((7,)), dma((2,)), dma((2,)), dma, dma, dma, dma, dma((2,)), dma((4,)), dma((4,)), dma((2, 4)), dma, pltpu.SemaphoreType.REGULAR,
        ],
        compiler_params=pltpu.CompilerParams(
            collective_id=0, has_side_effects=True, vmem_limit_bytes=48 * 1024 * 1024),
        name="ptycho",
    )(*(pltpu.with_memory_space_constraint(a, pltpu.HBM) for a in (
        pos_t, object_field.reshape(2, blocks, N, N), probe, prop_phase, measured, tb, tbt)))
    band = pl.pallas_call(
        functools.partial(final_kernel, chips, blocks),
        out_shape=jax.ShapeDtypeStruct((2, blocks, N, N), BF),
        in_specs=[pl.BlockSpec(memory_space=pltpu.HBM), pl.BlockSpec(memory_space=pltpu.VMEM)],
        out_specs=pl.BlockSpec(memory_space=pltpu.HBM),
        scratch_shapes=[pltpu.SMEM((2, 2 * chips), jnp.int32), V((2, blocks, N, N), F32), V((2, blocks, N, N), BF),
                        dma((blocks,)), dma],
        compiler_params=pltpu.CompilerParams(vmem_limit_bytes=32 * 1024 * 1024),
        name="assemble",
    )(pltpu.with_memory_space_constraint(pos_t, pltpu.HBM), slots)
    return band.reshape(1, 2, height, N)


def solution(mesh):
    placed = (PS("depth", None, None, "pos"), PS(), PS(), PS("pos", None, None), PS())
    return jax.shard_map(
        local, mesh=mesh, in_specs=placed, out_specs=PS("depth", None, None, "pos"), check_vma=False
    )
```

```python
import functools
import math
import numpy as np
import jax, jax.numpy as jnp
from jax import lax
from jax.experimental import pallas as pl
from jax.experimental.pallas import tpu as pltpu
from jax.sharding import PartitionSpec as PS
BF=jnp.bfloat16; F32=jnp.float32
N=256; HF=128
MODES=4
WIDTH=4

def tables():
    k=np.arange(N); ph=(k[:,None]*k[None,:])%N
    ang=ph*(2*math.pi/N)
    fr=np.cos(ang)/16.0; fi=-np.sin(ang)/16.0
    tb=np.concatenate([fr[0::2],fi[0::2],fr[1::2],fi[1::2]],0)
    return jnp.asarray(tb,dtype=BF), jnp.asarray(tb.T,dtype=BF)

def dot(a,b): return jnp.dot(a,b,preferred_element_type=F32)
def iota(shape,d): return lax.broadcasted_iota(jnp.int32,shape,d)

def prep_tables(tb,tbt,tab,y,c):
    for r,f1,f2 in ((y,0,1),(c,3,2)):
        onehot=(iota((N,HF),0)==((iota((N,HF),1)-r)&255)).astype(F32).astype(BF)
        m1=dot(tb[...],onehot).astype(BF)
        onet=(iota((HF,N),1)==((iota((HF,N),0)-r)&255)).astype(F32).astype(BF)
        m2=dot(onet,tbt[...]).astype(BF)
        for par in range(2):
            a=m1[par*256:par*256+128]; b=m1[par*256+128:par*256+256]
            tab[f1,par,0:128,0:128]=a; tab[f1,par,0:128,128:256]=-b
            tab[f1,par,128:256,0:128]=b; tab[f1,par,128:256,128:256]=a
            a=m2[:,par*256:par*256+128]; b=m2[:,par*256+128:par*256+256]
            tab[f2,par,0:128,0:128]=a; tab[f2,par,0:128,128:256]=b
            tab[f2,par,128:256,0:128]=-b; tab[f2,par,128:256,128:256]=a

def prep_probe(probe,pr,tmp,y,c):
    ryt=(iota((N,N),1)==((iota((N,N),0)-y)&255)).astype(F32).astype(BF)
    rc=(iota((N,N),0)==((iota((N,N),1)-c)&255)).astype(F32).astype(BF)
    for m in range(4):
        for q in range(2):
            t=dot(ryt,probe[m,q]).astype(BF)
            pr[m,q]=dot(t,rc)

def perms():
    i0=iota((N,N),0); i1=iota((N,N),1)
    pt=(i1==(2*(i0&127)+(i0>>7))).astype(F32).astype(BF)
    p=(i0==(2*(i1&127)+(i1>>7))).astype(F32).astype(BF)
    return pt,p

def prep_k(phase,kk):
    pt,p=perms()
    x=phase[...]
    acc=None
    for _ in range(3):
        h=x.astype(BF)
        x=x-h.astype(F32)
        t=dot(dot(pt,h).astype(BF),p)
        acc=t if acc is None else acc+t
    kk[0]=jnp.cos(acc); kk[1]=jnp.sin(acc)

def prep_meas(meas,mp):
    pt,p=perms()
    mp[...]=dot(dot(pt,meas[...]).astype(BF),p)

RC=32
def dots1f(tab,P): return [dot(tab[0,par],P[par]) for par in range(2)]
def post1f(VV,L):
    for q in range(2):
        for r in range(0,128,RC):
            for par in range(2):
                V=VV[par][q*128+r:q*128+r+RC]
                lo=V[:,:128]; hi=V[:,128:]
                L[0,par*128+r:par*128+r+RC,q*128:q*128+128]=(lo+hi).astype(BF)
                L[1,par*128+r:par*128+r+RC,q*128:q*128+128]=(lo-hi).astype(BF)

def dots2f(tab,L): return [dot(L[cp],tab[2,cp]) for cp in range(2)]
def dots1i(tab,P): return [dot(tab[1,par],P[par]) for par in range(2)]
def post1i(E,L):
    for q in range(2):
        for r in range(0,128,RC):
            for cp in range(2):
                rr=slice(q*128+r,q*128+r+RC)
                a=E[0][rr,cp*128:cp*128+128]; b=E[1][rr,cp*128:cp*128+128]
                L[cp,r:r+RC,q*128:q*128+128]=(a+b).astype(BF)
                L[cp,128+r:128+r+RC,q*128:q*128+128]=(a-b).astype(BF)

def dots2i(tab,L): return [dot(L[cp],tab[3,cp]) for cp in range(2)]

def space(D,r,n,q,uc):
    a=D[0][r:r+n,q*128:q*128+128]; b=D[1][r:r+n,q*128:q*128+128]
    return a+b if uc==0 else a-b

def put2(P,q,r,sl,x0,x1):
    P[0,q*128+r:q*128+r+RC,sl]=(x0+x1).astype(BF)
    P[1,q*128+r:q*128+r+RC,sl]=(x0-x1).astype(BF)

def putf(P,q,r,sl,x):
    P[r//128,q*128+r%128:q*128+r%128+RC,sl]=x.astype(BF)

def halves(r): return (slice(r,r+RC),slice(128+r,128+r+RC))
def lanes(k): return slice(k*128,k*128+128)

def phase_a(m,tab,pr,o0,kk,P,L,psi1):
    for r in range(0,128,RC):
        for uc in range(2):
            sl=lanes(uc); xr=[];xi=[]
            for h in halves(r):
                a=pr[m,0,h,sl].astype(F32); b=pr[m,1,h,sl].astype(F32)
                c=o0[0,h,sl].astype(F32); d=o0[1,h,sl].astype(F32)
                xr.append(a*c-b*d); xi.append(a*d+b*c)
            put2(P,0,r,sl,*xr); put2(P,1,r,sl,*xi)
    V=dots1f(tab,P); yield
    post1f(V,L); SS=dots2f(tab,L); yield
    for r in range(0,256,RC):
        for cp in range(2):
            S=SS[cp][r:r+RC]; sl=lanes(cp)
            kr=kk[0,r:r+RC,sl]; ki=kk[1,r:r+RC,sl]
            putf(P,0,r,sl,S[:,:128]*kr-S[:,128:]*ki)
            putf(P,1,r,sl,S[:,:128]*ki+S[:,128:]*kr)
    E=dots1i(tab,P); yield
    post1i(E,L); D=dots2i(tab,L); yield
    for r in range(0,256,RC):
        for uc in range(2):
            for q in range(2): psi1[m,q,r:r+RC,lanes(uc)]=space(D,r,RC,q,uc)

def phase_b(m,tab,o1,P,L,psi1,far,inten):
    for r in range(0,128,RC):
        for uc in range(2):
            sl=lanes(uc); xr=[];xi=[]
            for h in halves(r):
                a=psi1[m,0,h,sl]; b=psi1[m,1,h,sl]
                c=o1[0,h,sl].astype(F32); d=o1[1,h,sl].astype(F32)
                xr.append(a*c-b*d); xi.append(a*d+b*c)
            put2(P,0,r,sl,*xr); put2(P,1,r,sl,*xi)
    V=dots1f(tab,P); yield
    post1f(V,L); SS=dots2f(tab,L); yield
    for r in range(0,256,RC):
        for cp in range(2):
            S=SS[cp][r:r+RC]
            far[m,cp,r:r+RC]=S
            inten[cp,r:r+RC]+=S[:,:128]*S[:,:128]+S[:,128:]*S[:,128:]

def phase_c(m,tab,o1,P,L,psi1,far,inten,g1,adj):
    for r in range(0,256,RC):
        for cp in range(2):
            w=inten[cp,r:r+RC]
            putf(P,0,r,lanes(cp),w*far[m,cp,r:r+RC,:128]); putf(P,1,r,lanes(cp),w*far[m,cp,r:r+RC,128:])
    E=dots1i(tab,P); yield
    post1i(E,L); D=dots2i(tab,L); yield
    for r in range(0,128,RC):
        for uc in range(2):
            sl=lanes(uc); ar=[];ai=[]
            for h in halves(r):
                br=space(D,h.start,RC,0,uc); bi=space(D,h.start,RC,1,uc)
                a=psi1[m,0,h,sl]; b=psi1[m,1,h,sl]
                g1[0,h,sl]+=a*br+b*bi; g1[1,h,sl]+=a*bi-b*br
                c=o1[0,h,sl].astype(F32); d=o1[1,h,sl].astype(F32)
                ar.append(c*br+d*bi); ai.append(c*bi-d*br)
            put2(adj.at[m],0,r,sl,*ar); put2(adj.at[m],1,r,sl,*ai)

def phase_d(m,tab,kk,P,L,L2,adj):
    V=dots1f(tab,adj.at[m]); yield
    post1f(V,L); SS=dots2f(tab,L); yield
    for r in range(0,256,RC):
        for cp in range(2):
            S=SS[cp][r:r+RC].astype(BF).astype(F32); sl=lanes(cp)
            kr=kk[0,r:r+RC,sl]; ki=kk[1,r:r+RC,sl]
            putf(P,0,r,sl,kr*S[:,:128]+ki*S[:,128:])
            putf(P,1,r,sl,kr*S[:,128:]-ki*S[:,:128])
    E0,E1=dots1i(tab,P); yield
    for q in range(2):
        for r in range(0,128,RC):
            for cp in range(2):
                rr=slice(q*128+r,q*128+r+RC); sl=lanes(cp); to=lanes(q); h=r//64; k=r%64
                L2[cp,h,m,k:k+RC,to]=(E0[rr,sl]+E1[rr,sl]).astype(BF)
                L2[cp,2+h,m,k:k+RC,to]=(E0[rr,sl]-E1[rr,sl]).astype(BF)

def phase_e(r,tab,pr,L2,gs):
    D=(dot(L2[0,r].reshape(256,256),tab[3,0]), dot(L2[1,r].reshape(256,256),tab[3,1])); yield
    for k in range(0,64,RC):
        rows=slice(r*64+k,r*64+k+RC)
        for uc in range(2):
            sl=lanes(uc)
            gr=None
            for m in range(4):
                wr=space(D,m*64+k,RC,0,uc); wi=space(D,m*64+k,RC,1,uc)
                a=pr[m,0,rows,sl].astype(F32); b=pr[m,1,rows,sl].astype(F32)
                tr=a*wr+b*wi; ti=a*wi-b*wr
                gr,gi=(tr,ti) if gr is None else (gr+tr,gi+ti)
            gs[0,rows,sl]=gr.astype(BF); gs[1,rows,sl]=gi.astype(BF)


def weave(items,width=2):
    todo=list(items); live=[]
    while todo or live:
        if todo and len(live)<width:
            item=todo.pop(0)
            if item[0] is not None: item[0]()
        else:
            item=live.pop(0)
        try:
            next(item[1])
            live.append(item)
        except StopIteration:
            if item[2] is not None: item[2]()


MESH = pl.DeviceIdType.MESH


def main_kernel(chips, height, pos_h, obj, probe_h, phase_h, meas_h, tb_h, tbt_h, out,
                pos, band, w_left, w_right, w_part, near, farw, ob, probe, phase, meas, mtmp,
                tb, tbt, tab, pr, kk, mp, P, L, psi1, far, inten, adj, L2, g, gs,
                in_sem, obj_send, obj_recv, near_send, near_recv, m_send, m_recv,
                g_send, g_recv, c_send, c_recv, loc_sem, turn):
    d = lax.axis_index("depth")
    p = lax.axis_index("pos")
    left = lax.rem(p + chips - 1, chips)
    right = lax.rem(p + 1, chips)
    nb = lax.rem(p + 1 - 2 * d + chips, chips)
    total = 2 * chips
    mine = lax.rem(2 * p - d + total, total)
    other = lax.rem(2 * p + d - 1 + total, total)
    q_left = lax.rem(2 * p - 2 + total, total)
    q_right = 2 * p + 1

    loads = [
        pltpu.make_async_copy(obj, band, in_sem.at[0]),
        pltpu.make_async_copy(meas_h.at[d], mtmp, in_sem.at[1]),
        pltpu.make_async_copy(tb_h, tb, in_sem.at[2]),
        pltpu.make_async_copy(tbt_h, tbt, in_sem.at[3]),
        pltpu.make_async_copy(probe_h, probe, in_sem.at[4]),
        pltpu.make_async_copy(phase_h, phase, in_sem.at[5]),
        pltpu.make_async_copy(pos_h, pos, in_sem.at[6]),
    ]
    for cp in loads:
        cp.start()
    barrier = pltpu.get_barrier_semaphore()
    peers = ((1 - d, p), (0, left), (1, right), (d, nb))
    for peer in peers:
        pl.semaphore_signal(barrier, inc=1, device_id=peer, device_id_type=MESH)

    blocks = height // N
    row_id = iota((N, N), 0)

    def window(q, part):
        y = pos[0, q]
        k = y >> 8
        k2 = jnp.minimum(k + 1, blocks - 1)
        a = band[part, k]
        b = band[part, k2]
        return jnp.where(row_id >= (y & 255), a.astype(F32), b.astype(F32)).astype(BF)

    loads[6].wait()
    loads[0].wait()
    for part in range(2):
        w_left[part] = window(q_left, part)
    for part in range(2):
        w_right[part] = window(q_right, part)
    for part in range(2):
        w_part[part] = window(other, part)
    for part in range(2):
        near[d, part] = window(mine, part)
    y = pos[0, mine] & 255
    c = pos[1, mine] & 255
    loads[2].wait()
    loads[3].wait()
    prep_tables(tb, tbt, tab, y, c)
    loads[4].wait()
    prep_probe(probe, pr, None, y, c)
    pl.semaphore_wait(barrier, 4)

    def remote(src, dst, ss, rs, dev):
        return pltpu.make_async_remote_copy(src_ref=src, dst_ref=dst, send_sem=ss, recv_sem=rs,
                                            device_id=dev, device_id_type=MESH)

    c_left = remote(w_left, farw.at[d], obj_send.at[0], obj_recv.at[d], (0, left))
    c_right = remote(w_right, farw.at[d], obj_send.at[1], obj_recv.at[d], (1, right))
    c_part = remote(w_part, near.at[d], near_send, near_recv, (1 - d, p))
    go_left = p > 0
    wrap_a = jnp.logical_and(d == 0, p == chips - 1)

    def send_object():
        @pl.when(go_left)
        def _():
            c_left.start()

        c_right.start()

    def sent_object():
        @pl.when(go_left)
        def _():
            c_left.wait_send()

        c_right.wait_send()

    @pl.when(d == 0)
    def _():
        send_object()

    c_part.start()
    loads[1].wait()
    c_meas = remote(meas.at[0], meas.at[1], m_send, m_recv, (1, right))
    meas[0] = mtmp[...].astype(BF)
    loads[5].wait()
    prep_k(phase, kk)

    @pl.when(d == 0)
    def _():
        sent_object()
        pl.semaphore_signal(turn, inc=1, device_id=(1, p), device_id_type=MESH)

    @pl.when(d == 1)
    def _():
        pl.semaphore_wait(turn, 1)
        send_object()
        c_meas.start()

    inten[...] = jnp.zeros_like(inten)
    g[...] = jnp.zeros_like(g)

    near_mask = (iota((N, N), 1) - c) * (1 - 2 * d) - d >= 0

    def merge(s):
        for part in range(2):
            ob[s, part] = jnp.where(near_mask, near[s, part].astype(F32),
                                    farw[s, part].astype(F32))

    def bufs(m):
        return P.at[m % WIDTH], L.at[m % WIDTH]

    def run(gens):
        weave([(None, x, None) for x in gens], WIDTH)

    c_part.wait_recv()

    def got_far(k):
        @pl.when(jnp.logical_not(wrap_a))
        def _():
            remote(w_left, farw.at[k], obj_send.at[0], obj_recv.at[k], (0, left)).wait_recv()

    got_far(0)
    merge(0)
    run([phase_a(m, tab, pr, ob.at[0], kk, *bufs(m), psi1) for m in range(MODES)])
    got_far(1)
    merge(1)
    run([phase_b(m, tab, ob.at[1], *bufs(m), psi1, far, inten) for m in range(MODES)])

    @pl.when(d == 1)
    def _():
        c_meas.wait()

    prep_meas(meas.at[d], mp)
    for cp in range(2):
        inten[cp] = (inten[cp] - mp[:, cp * 128:cp * 128 + 128]) * 0.125
    run([phase_c(m, tab, ob.at[1], *bufs(m), psi1, far, inten, g, adj) for m in range(MODES)])

    gs[1] = g[...].astype(BF)
    far1 = remote(gs.at[1], out.at[2 + d], g_send.at[0], g_recv.at[2 + d], (1, nb))
    near1 = remote(gs.at[1], out.at[d], g_send.at[1], g_recv.at[d], (1, p))
    stay1 = pltpu.make_async_copy(gs.at[1], out.at[d], loc_sem)

    @pl.when(jnp.logical_not(wrap_a))
    def _():
        far1.start()

    @pl.when(d == 0)
    def _():
        near1.start()

    @pl.when(d == 1)
    def _():
        stay1.start()

    run([phase_d(m, tab, kk, *bufs(m), L2, adj) for m in range(MODES)])

    def chunk(r, dev):
        rows = pl.ds(r * 64, 64)
        return remote(gs.at[0, :, rows, :], out.at[2 + d, :, rows, :], c_send.at[r], c_recv.at[d, r], dev)

    def incoming(slot, r):
        rows = pl.ds(r * 64, 64)
        return remote(gs.at[0, :, rows, :], out.at[2 + slot, :, rows, :], c_send.at[r], c_recv.at[slot, r],
                      (0, nb))

    def ship(r):
        @pl.when(jnp.logical_not(wrap_a))
        def _():
            chunk(r, (0, nb)).start()

    weave([(None, phase_e(r, tab, pr, L2, gs.at[0]), functools.partial(ship, r)) for r in range(4)], 2)
    near0 = remote(gs.at[0], out.at[d], g_send.at[1], g_recv.at[d], (0, p))
    stay0 = pltpu.make_async_copy(gs.at[0], out.at[d], loc_sem)

    @pl.when(d == 1)
    def _():
        near0.start()
        stay1.wait()

    @pl.when(d == 0)
    def _():
        stay0.start()
        near1.wait_send()

    @pl.when(d == 1)
    def _():
        sent_object()

    c_part.wait_send()

    @pl.when(jnp.logical_not(wrap_a))
    def _():
        far1.wait_send()
        for r in range(4):
            chunk(r, (0, nb)).wait_send()

    @pl.when(d == 1)
    def _():
        near0.wait_send()
        remote(gs.at[1], out.at[0], g_send.at[1], g_recv.at[0], (0, p)).wait_recv()
        remote(gs.at[1], out.at[3], g_send.at[0], g_recv.at[3], (1, nb)).wait_recv()

        @pl.when(p > 0)
        def _():
            remote(gs.at[1], out.at[2], g_send.at[0], g_recv.at[2], (1, nb)).wait_recv()

    @pl.when(d == 0)
    def _():
        stay0.wait()
        remote(gs.at[0], out.at[1], g_send.at[1], g_recv.at[1], (0, p)).wait_recv()
        for r in range(4):
            incoming(1, r).wait_recv()

        @pl.when(p > 0)
        def _():
            for r in range(4):
                incoming(0, r).wait_recv()


def final_kernel(chips, blocks, pos_h, slots, out, pos, acc, ob, sem, pos_sem):
    load = pltpu.make_async_copy(pos_h, pos, pos_sem)
    load.start()
    p = lax.axis_index("pos")
    total = 2 * chips
    acc[...] = jnp.zeros_like(acc)
    load.wait()
    rows = iota((N, N), 0)
    cols = iota((N, N), 1)
    for slot, (off, ge) in enumerate(((0, True), (total - 1, False), (total - 2, False), (1, True))):
        q = lax.rem(2 * p + off, total)
        y = pos[0, q]
        k = y >> 8
        k2 = jnp.minimum(k + 1, blocks - 1)
        yy = y & 255
        c = pos[1, q] & 255
        cm = (cols >= c) if ge else (cols < c)
        for part in range(2):
            x = slots[slot, part].astype(F32)
            acc[part, k] += jnp.where(cm & (rows >= yy), x, 0.0)
            acc[part, k2] += jnp.where(cm & (rows < yy), x, 0.0)
    copies = []
    for i in range(blocks):
        ob[:, i] = acc[:, i].astype(BF)
        cp = pltpu.make_async_copy(ob.at[:, i], out.at[:, i], sem.at[i])
        cp.start()
        copies.append(cp)
    for cp in copies:
        cp.wait()


def local(object_field, probe, prop_phase, measured, positions):
    chips = lax.axis_size("pos")
    height = object_field.shape[2]
    blocks = height // N
    tb, tbt = tables()
    pos_t = positions.T
    any_ = pl.BlockSpec(memory_space=pl.ANY)
    V = pltpu.VMEM
    win = V((2, N, N), BF)
    dma = pltpu.SemaphoreType.DMA
    slots = pl.pallas_call(
        functools.partial(main_kernel, chips, height),
        out_shape=jax.ShapeDtypeStruct((4, 2, N, N), BF),
        in_specs=[pl.BlockSpec(memory_space=pltpu.HBM)] * 7,
        out_specs=any_,
        scratch_shapes=[
            pltpu.SMEM((2, 2 * chips), jnp.int32), V((2, blocks, N, N), BF), win, win, win, V((2, 2, N, N), BF), V((2, 2, N, N), BF),
            V((2, 2, N, N), F32), V((4, 2, N, N), BF), V((N, N), F32), V((2, N, N), BF), V((N, N), F32),
            V((512, N), BF), V((N, 512), BF), V((4, 2, N, N), BF), V((4, 2, N, N), F32),
            V((2, N, N), F32), V((N, N), F32), V((WIDTH, 2, N, N), BF), V((WIDTH, 2, N, N), BF),
            V((4, 2, N, N), F32), V((4, 2, N, N), F32), V((2, N, 128), F32), V((4, 2, N, N), BF),
            V((2, 4, 4, 64, N), BF), V((2, N, N), F32), V((2, 2, N, N), BF),
            dma((7,)), dma((2,)), dma((2,)), dma, dma, dma, dma, dma((2,)), dma((4,)), dma((4,)), dma((2, 4)), dma, pltpu.SemaphoreType.REGULAR,
        ],
        compiler_params=pltpu.CompilerParams(
            collective_id=0, has_side_effects=True, vmem_limit_bytes=48 * 1024 * 1024),
        name="ptycho",
    )(*(pltpu.with_memory_space_constraint(a, pltpu.HBM) for a in (
        pos_t, object_field.reshape(2, blocks, N, N), probe, prop_phase, measured, tb, tbt)))
    band = pl.pallas_call(
        functools.partial(final_kernel, chips, blocks),
        out_shape=jax.ShapeDtypeStruct((2, blocks, N, N), BF),
        in_specs=[pl.BlockSpec(memory_space=pltpu.HBM), pl.BlockSpec(memory_space=pltpu.VMEM)],
        out_specs=pl.BlockSpec(memory_space=pltpu.HBM),
        scratch_shapes=[pltpu.SMEM((2, 2 * chips), jnp.int32), V((2, blocks, N, N), F32), V((2, blocks, N, N), BF),
                        dma((blocks,)), dma],
        compiler_params=pltpu.CompilerParams(vmem_limit_bytes=32 * 1024 * 1024),
        name="assemble",
    )(pltpu.with_memory_space_constraint(pos_t, pltpu.HBM), slots)
    return band.reshape(1, 2, height, N)


def solution(mesh):
    placed = (PS("depth", None, None, "pos"), PS(), PS(), PS("pos", None, None), PS())
    return jax.shard_map(
        local, mesh=mesh, in_specs=placed, out_specs=PS("depth", None, None, "pos"), check_vma=False
    )
```

```python
import functools
import math
import numpy as np
import jax, jax.numpy as jnp
from jax import lax
from jax.experimental import pallas as pl
from jax.experimental.pallas import tpu as pltpu
from jax.sharding import PartitionSpec as PS
BF=jnp.bfloat16; F32=jnp.float32
N=256; HF=128
MODES=4
WIDTH=4

def tables():
    k=np.arange(N); ph=(k[:,None]*k[None,:])%N
    ang=ph*(2*math.pi/N)
    fr=np.cos(ang)/16.0; fi=-np.sin(ang)/16.0
    tb=np.concatenate([fr[0::2],fi[0::2],fr[1::2],fi[1::2]],0)
    return jnp.asarray(tb,dtype=BF), jnp.asarray(tb.T,dtype=BF)

def dot(a,b): return jnp.dot(a,b,preferred_element_type=F32)
def iota(shape,d): return lax.broadcasted_iota(jnp.int32,shape,d)

def prep_tables(tb,tbt,tab,y,c):
    for r,f1,f2 in ((y,0,1),(c,3,2)):
        onehot=(iota((N,HF),0)==((iota((N,HF),1)-r)&255)).astype(F32).astype(BF)
        m1=dot(tb[...],onehot).astype(BF)
        onet=(iota((HF,N),1)==((iota((HF,N),0)-r)&255)).astype(F32).astype(BF)
        m2=dot(onet,tbt[...]).astype(BF)
        for par in range(2):
            a=m1[par*256:par*256+128]; b=m1[par*256+128:par*256+256]
            tab[f1,par,0:128,0:128]=a; tab[f1,par,0:128,128:256]=-b
            tab[f1,par,128:256,0:128]=b; tab[f1,par,128:256,128:256]=a
            a=m2[:,par*256:par*256+128]; b=m2[:,par*256+128:par*256+256]
            tab[f2,par,0:128,0:128]=a; tab[f2,par,0:128,128:256]=b
            tab[f2,par,128:256,0:128]=-b; tab[f2,par,128:256,128:256]=a

def prep_probe(probe,pr,tmp,y,c):
    ryt=(iota((N,N),1)==((iota((N,N),0)-y)&255)).astype(F32).astype(BF)
    rc=(iota((N,N),0)==((iota((N,N),1)-c)&255)).astype(F32).astype(BF)
    for m in range(4):
        for q in range(2):
            t=dot(ryt,probe[m,q]).astype(BF)
            pr[m,q]=dot(t,rc)

def perms():
    i0=iota((N,N),0); i1=iota((N,N),1)
    pt=(i1==(2*(i0&127)+(i0>>7))).astype(F32).astype(BF)
    p=(i0==(2*(i1&127)+(i1>>7))).astype(F32).astype(BF)
    return pt,p

def prep_k(phase,kk):
    pt,p=perms()
    x=phase[...]
    acc=None
    for _ in range(3):
        h=x.astype(BF)
        x=x-h.astype(F32)
        t=dot(dot(pt,h).astype(BF),p)
        acc=t if acc is None else acc+t
    kk[0]=jnp.cos(acc); kk[1]=jnp.sin(acc)

def prep_meas(meas,mp):
    pt,p=perms()
    mp[...]=dot(dot(pt,meas[...]).astype(BF),p)

RC=32
def dots1f(tab,P): return [dot(tab[0,par],P[par]) for par in range(2)]
def post1f(VV,L):
    for q in range(2):
        for r in range(0,128,RC):
            for par in range(2):
                V=VV[par][q*128+r:q*128+r+RC]
                lo=V[:,:128]; hi=V[:,128:]
                L[0,par*128+r:par*128+r+RC,q*128:q*128+128]=(lo+hi).astype(BF)
                L[1,par*128+r:par*128+r+RC,q*128:q*128+128]=(lo-hi).astype(BF)

def dots2f(tab,L): return [dot(L[cp],tab[2,cp]) for cp in range(2)]
def dots1i(tab,P): return [dot(tab[1,par],P[par]) for par in range(2)]
def post1i(E,L):
    for q in range(2):
        for r in range(0,128,RC):
            for cp in range(2):
                rr=slice(q*128+r,q*128+r+RC)
                a=E[0][rr,cp*128:cp*128+128]; b=E[1][rr,cp*128:cp*128+128]
                L[cp,r:r+RC,q*128:q*128+128]=(a+b).astype(BF)
                L[cp,128+r:128+r+RC,q*128:q*128+128]=(a-b).astype(BF)

def dots2i(tab,L): return [dot(L[cp],tab[3,cp]) for cp in range(2)]

def space(D,r,n,q,uc):
    a=D[0][r:r+n,q*128:q*128+128]; b=D[1][r:r+n,q*128:q*128+128]
    return a+b if uc==0 else a-b

def put2(P,q,r,sl,x0,x1):
    P[0,q*128+r:q*128+r+RC,sl]=(x0+x1).astype(BF)
    P[1,q*128+r:q*128+r+RC,sl]=(x0-x1).astype(BF)

def putf(P,q,r,sl,x):
    P[r//128,q*128+r%128:q*128+r%128+RC,sl]=x.astype(BF)

def halves(r): return (slice(r,r+RC),slice(128+r,128+r+RC))
def lanes(k): return slice(k*128,k*128+128)

def phase_a(m,tab,pr,o0,kk,P,L,psi1):
    for r in range(0,128,RC):
        for uc in range(2):
            sl=lanes(uc); xr=[];xi=[]
            for h in halves(r):
                a=pr[m,0,h,sl].astype(F32); b=pr[m,1,h,sl].astype(F32)
                c=o0[0,h,sl].astype(F32); d=o0[1,h,sl].astype(F32)
                xr.append(a*c-b*d); xi.append(a*d+b*c)
            put2(P,0,r,sl,*xr); put2(P,1,r,sl,*xi)
    V=dots1f(tab,P); yield
    post1f(V,L); SS=dots2f(tab,L); yield
    for r in range(0,256,RC):
        for cp in range(2):
            S=SS[cp][r:r+RC]; sl=lanes(cp)
            kr=kk[0,r:r+RC,sl]; ki=kk[1,r:r+RC,sl]
            putf(P,0,r,sl,S[:,:128]*kr-S[:,128:]*ki)
            putf(P,1,r,sl,S[:,:128]*ki+S[:,128:]*kr)
    E=dots1i(tab,P); yield
    post1i(E,L); D=dots2i(tab,L); yield
    for r in range(0,256,RC):
        for uc in range(2):
            for q in range(2): psi1[m,q,r:r+RC,lanes(uc)]=space(D,r,RC,q,uc)

def phase_b(m,tab,o1,P,L,psi1,far,inten):
    for r in range(0,128,RC):
        for uc in range(2):
            sl=lanes(uc); xr=[];xi=[]
            for h in halves(r):
                a=psi1[m,0,h,sl]; b=psi1[m,1,h,sl]
                c=o1[0,h,sl].astype(F32); d=o1[1,h,sl].astype(F32)
                xr.append(a*c-b*d); xi.append(a*d+b*c)
            put2(P,0,r,sl,*xr); put2(P,1,r,sl,*xi)
    V=dots1f(tab,P); yield
    post1f(V,L); SS=dots2f(tab,L); yield
    for r in range(0,256,RC):
        for cp in range(2):
            S=SS[cp][r:r+RC]
            far[m,cp,r:r+RC]=S
            inten[cp,r:r+RC]+=S[:,:128]*S[:,:128]+S[:,128:]*S[:,128:]

def phase_c(m,tab,o1,P,L,psi1,far,inten,g1,adj):
    for r in range(0,256,RC):
        for cp in range(2):
            w=inten[cp,r:r+RC]
            putf(P,0,r,lanes(cp),w*far[m,cp,r:r+RC,:128]); putf(P,1,r,lanes(cp),w*far[m,cp,r:r+RC,128:])
    E=dots1i(tab,P); yield
    post1i(E,L); D=dots2i(tab,L); yield
    for r in range(0,128,RC):
        for uc in range(2):
            sl=lanes(uc); ar=[];ai=[]
            for h in halves(r):
                br=space(D,h.start,RC,0,uc); bi=space(D,h.start,RC,1,uc)
                a=psi1[m,0,h,sl]; b=psi1[m,1,h,sl]
                g1[0,h,sl]+=a*br+b*bi; g1[1,h,sl]+=a*bi-b*br
                c=o1[0,h,sl].astype(F32); d=o1[1,h,sl].astype(F32)
                ar.append(c*br+d*bi); ai.append(c*bi-d*br)
            put2(adj.at[m],0,r,sl,*ar); put2(adj.at[m],1,r,sl,*ai)

def phase_d(m,tab,kk,P,L,L2,adj):
    V=dots1f(tab,adj.at[m]); yield
    post1f(V,L); SS=dots2f(tab,L); yield
    for r in range(0,256,RC):
        for cp in range(2):
            S=SS[cp][r:r+RC].astype(BF).astype(F32); sl=lanes(cp)
            kr=kk[0,r:r+RC,sl]; ki=kk[1,r:r+RC,sl]
            putf(P,0,r,sl,kr*S[:,:128]+ki*S[:,128:])
            putf(P,1,r,sl,kr*S[:,128:]-ki*S[:,:128])
    E0,E1=dots1i(tab,P); yield
    for q in range(2):
        for r in range(0,128,RC):
            for cp in range(2):
                rr=slice(q*128+r,q*128+r+RC); sl=lanes(cp); to=lanes(q); h=r//64; k=r%64
                L2[cp,h,m,k:k+RC,to]=(E0[rr,sl]+E1[rr,sl]).astype(BF)
                L2[cp,2+h,m,k:k+RC,to]=(E0[rr,sl]-E1[rr,sl]).astype(BF)

def phase_e(r,tab,pr,L2,gs):
    D=(dot(L2[0,r].reshape(256,256),tab[3,0]), dot(L2[1,r].reshape(256,256),tab[3,1])); yield
    for k in range(0,64,RC):
        rows=slice(r*64+k,r*64+k+RC)
        for uc in range(2):
            sl=lanes(uc)
            gr=None
            for m in range(4):
                wr=space(D,m*64+k,RC,0,uc); wi=space(D,m*64+k,RC,1,uc)
                a=pr[m,0,rows,sl].astype(F32); b=pr[m,1,rows,sl].astype(F32)
                tr=a*wr+b*wi; ti=a*wi-b*wr
                gr,gi=(tr,ti) if gr is None else (gr+tr,gi+ti)
            gs[0,rows,sl]=gr.astype(BF); gs[1,rows,sl]=gi.astype(BF)


def weave(items,width=2):
    todo=list(items); live=[]
    while todo or live:
        if todo and len(live)<width:
            item=todo.pop(0)
            if item[0] is not None: item[0]()
        else:
            item=live.pop(0)
        try:
            next(item[1])
            live.append(item)
        except StopIteration:
            if item[2] is not None: item[2]()


MESH = pl.DeviceIdType.MESH


def main_kernel(chips, height, pos_h, obj, probe_h, phase_h, meas_h, tb_h, tbt_h, out,
                pos, band, w_left, w_right, w_part, near, farw, ob, probe, phase, meas, mtmp,
                tb, tbt, tab, pr, kk, mp, P, L, psi1, far, inten, adj, L2, g, gs,
                in_sem, obj_send, obj_recv, near_send, near_recv, m_send, m_recv,
                g_send, g_recv, c_send, c_recv, loc_sem):
    d = lax.axis_index("depth")
    p = lax.axis_index("pos")
    left = lax.rem(p + chips - 1, chips)
    right = lax.rem(p + 1, chips)
    nb = lax.rem(p + 1 - 2 * d + chips, chips)
    total = 2 * chips
    mine = lax.rem(2 * p - d + total, total)
    other = lax.rem(2 * p + d - 1 + total, total)
    q_left = lax.rem(2 * p - 2 + total, total)
    q_right = 2 * p + 1

    loads = [
        pltpu.make_async_copy(obj, band, in_sem.at[0]),
        pltpu.make_async_copy(meas_h.at[d], mtmp, in_sem.at[1]),
        pltpu.make_async_copy(tb_h, tb, in_sem.at[2]),
        pltpu.make_async_copy(tbt_h, tbt, in_sem.at[3]),
        pltpu.make_async_copy(probe_h, probe, in_sem.at[4]),
        pltpu.make_async_copy(phase_h, phase, in_sem.at[5]),
        pltpu.make_async_copy(pos_h, pos, in_sem.at[6]),
    ]
    for cp in loads:
        cp.start()
    barrier = pltpu.get_barrier_semaphore()
    peers = ((1 - d, p), (0, left), (1, right), (d, nb))
    for peer in peers:
        pl.semaphore_signal(barrier, inc=1, device_id=peer, device_id_type=MESH)

    blocks = height // N
    row_id = iota((N, N), 0)

    def window(q, part):
        y = pos[0, q]
        k = y >> 8
        k2 = jnp.minimum(k + 1, blocks - 1)
        a = band[part, k]
        b = band[part, k2]
        return jnp.where(row_id >= (y & 255), a.astype(F32), b.astype(F32)).astype(BF)

    loads[6].wait()
    loads[0].wait()
    for part in range(2):
        w_left[part] = window(q_left, part)
    for part in range(2):
        w_right[part] = window(q_right, part)
    for part in range(2):
        w_part[part] = window(other, part)
    for part in range(2):
        near[d, part] = window(mine, part)
    y = pos[0, mine] & 255
    c = pos[1, mine] & 255
    pl.semaphore_wait(barrier, 4)

    def remote(src, dst, ss, rs, dev):
        return pltpu.make_async_remote_copy(src_ref=src, dst_ref=dst, send_sem=ss, recv_sem=rs,
                                            device_id=dev, device_id_type=MESH)

    c_left = remote(w_left, farw.at[d], obj_send.at[0], obj_recv.at[d], (0, left))
    c_right = remote(w_right, farw.at[d], obj_send.at[1], obj_recv.at[d], (1, right))
    c_part = remote(w_part, near.at[d], near_send, near_recv, (1 - d, p))
    go_left = p > 0
    wrap_a = jnp.logical_and(d == 0, p == chips - 1)

    def send_object():
        @pl.when(go_left)
        def _():
            c_left.start()

        c_right.start()

    def sent_object():
        @pl.when(go_left)
        def _():
            c_left.wait_send()

        c_right.wait_send()

    @pl.when(d == 0)
    def _():
        send_object()

    c_part.start()
    loads[1].wait()
    c_meas = remote(meas.at[0], meas.at[1], m_send, m_recv, (1, right))
    meas[0] = mtmp[...].astype(BF)
    loads[2].wait()
    loads[3].wait()
    prep_tables(tb, tbt, tab, y, c)
    loads[4].wait()
    prep_probe(probe, pr, None, y, c)
    loads[5].wait()
    prep_k(phase, kk)

    @pl.when(d == 1)
    def _():
        send_object()
        c_meas.start()

    inten[...] = jnp.zeros_like(inten)
    g[...] = jnp.zeros_like(g)

    near_mask = (iota((N, N), 1) - c) * (1 - 2 * d) - d >= 0

    def merge(s):
        for part in range(2):
            ob[s, part] = jnp.where(near_mask, near[s, part].astype(F32),
                                    farw[s, part].astype(F32))

    def bufs(m):
        return P.at[m % WIDTH], L.at[m % WIDTH]

    def run(gens):
        weave([(None, x, None) for x in gens], WIDTH)

    c_part.wait_recv()

    def got_far(k):
        @pl.when(jnp.logical_not(wrap_a))
        def _():
            remote(w_left, farw.at[k], obj_send.at[0], obj_recv.at[k], (0, left)).wait_recv()

    got_far(0)
    merge(0)
    run([phase_a(m, tab, pr, ob.at[0], kk, *bufs(m), psi1) for m in range(MODES)])
    got_far(1)
    merge(1)
    run([phase_b(m, tab, ob.at[1], *bufs(m), psi1, far, inten) for m in range(MODES)])

    @pl.when(d == 1)
    def _():
        c_meas.wait()

    prep_meas(meas.at[d], mp)
    for cp in range(2):
        inten[cp] = (inten[cp] - mp[:, cp * 128:cp * 128 + 128]) * 0.125
    run([phase_c(m, tab, ob.at[1], *bufs(m), psi1, far, inten, g, adj) for m in range(MODES)])

    gs[1] = g[...].astype(BF)
    far1 = remote(gs.at[1], out.at[2 + d], g_send.at[0], g_recv.at[2 + d], (1, nb))
    near1 = remote(gs.at[1], out.at[d], g_send.at[1], g_recv.at[d], (1, p))
    stay1 = pltpu.make_async_copy(gs.at[1], out.at[d], loc_sem)

    @pl.when(jnp.logical_not(wrap_a))
    def _():
        far1.start()

    @pl.when(d == 0)
    def _():
        near1.start()

    @pl.when(d == 1)
    def _():
        stay1.start()

    run([phase_d(m, tab, kk, *bufs(m), L2, adj) for m in range(MODES)])

    def chunk(r, dev):
        rows = pl.ds(r * 64, 64)
        return remote(gs.at[0, :, rows, :], out.at[2 + d, :, rows, :], c_send.at[r], c_recv.at[d, r], dev)

    def incoming(slot, r):
        rows = pl.ds(r * 64, 64)
        return remote(gs.at[0, :, rows, :], out.at[2 + slot, :, rows, :], c_send.at[r], c_recv.at[slot, r],
                      (0, nb))

    def ship(r):
        @pl.when(jnp.logical_not(wrap_a))
        def _():
            chunk(r, (0, nb)).start()

    weave([(None, phase_e(r, tab, pr, L2, gs.at[0]), functools.partial(ship, r)) for r in range(4)], 2)
    near0 = remote(gs.at[0], out.at[d], g_send.at[1], g_recv.at[d], (0, p))
    stay0 = pltpu.make_async_copy(gs.at[0], out.at[d], loc_sem)

    @pl.when(d == 1)
    def _():
        near0.start()
        stay1.wait()

    @pl.when(d == 0)
    def _():
        stay0.start()
        near1.wait_send()

    sent_object()
    c_part.wait_send()

    @pl.when(jnp.logical_not(wrap_a))
    def _():
        far1.wait_send()
        for r in range(4):
            chunk(r, (0, nb)).wait_send()

    @pl.when(d == 1)
    def _():
        near0.wait_send()
        remote(gs.at[1], out.at[0], g_send.at[1], g_recv.at[0], (0, p)).wait_recv()
        remote(gs.at[1], out.at[3], g_send.at[0], g_recv.at[3], (1, nb)).wait_recv()

        @pl.when(p > 0)
        def _():
            remote(gs.at[1], out.at[2], g_send.at[0], g_recv.at[2], (1, nb)).wait_recv()

    @pl.when(d == 0)
    def _():
        stay0.wait()
        remote(gs.at[0], out.at[1], g_send.at[1], g_recv.at[1], (0, p)).wait_recv()
        for r in range(4):
            incoming(1, r).wait_recv()

        @pl.when(p > 0)
        def _():
            for r in range(4):
                incoming(0, r).wait_recv()


def final_kernel(chips, blocks, pos_h, slots, out, pos, acc, sem, pos_sem):
    load = pltpu.make_async_copy(pos_h, pos, pos_sem)
    load.start()
    p = lax.axis_index("pos")
    total = 2 * chips
    acc[...] = jnp.zeros_like(acc)
    load.wait()
    rows = iota((16, N), 0)
    cols = iota((16, N), 1)
    for slot, (off, ge) in enumerate(((0, True), (total - 1, False), (total - 2, False), (1, True))):
        q = lax.rem(2 * p + off, total)
        y = pos[0, q]
        k = y >> 8
        k2 = jnp.minimum(k + 1, blocks - 1)
        yy = y & 255
        c = pos[1, q] & 255
        cm = (cols >= c) if ge else (cols < c)
        for r0 in range(0, N, 16):
            later = r0 + 15 < yy
            to = jnp.where(later, k2, k)
            keep = cm & (rows >= jnp.where(later, 0, yy - r0))
            for part in range(2):
                x = slots[slot, part, r0:r0 + 16]
                acc[part, to, r0:r0 + 16] += jnp.where(keep, x, jnp.zeros_like(x))
        rb = pl.multiple_of((yy >> 4) * 16, 16)
        keep = cm & (rows < yy - rb)
        for part in range(2):
            x = slots[slot, part, pl.ds(rb, 16)]
            acc[part, k2, pl.ds(rb, 16)] += jnp.where(keep, x, jnp.zeros_like(x))
    copies = []
    for i in range(blocks):
        cp = pltpu.make_async_copy(acc.at[:, i], out.at[:, i], sem.at[i])
        cp.start()
        copies.append(cp)
    for cp in copies:
        cp.wait()


def local(object_field, probe, prop_phase, measured, positions):
    chips = lax.axis_size("pos")
    height = object_field.shape[2]
    blocks = height // N
    tb, tbt = tables()
    pos_t = positions.T
    any_ = pl.BlockSpec(memory_space=pl.ANY)
    V = pltpu.VMEM
    win = V((2, N, N), BF)
    dma = pltpu.SemaphoreType.DMA
    slots = pl.pallas_call(
        functools.partial(main_kernel, chips, height),
        out_shape=jax.ShapeDtypeStruct((4, 2, N, N), BF),
        in_specs=[pl.BlockSpec(memory_space=pltpu.HBM)] * 7,
        out_specs=any_,
        scratch_shapes=[
            pltpu.SMEM((2, 2 * chips), jnp.int32), V((2, blocks, N, N), BF), win, win, win, V((2, 2, N, N), BF), V((2, 2, N, N), BF),
            V((2, 2, N, N), F32), V((4, 2, N, N), BF), V((N, N), F32), V((2, N, N), BF), V((N, N), F32),
            V((512, N), BF), V((N, 512), BF), V((4, 2, N, N), BF), V((4, 2, N, N), F32),
            V((2, N, N), F32), V((N, N), F32), V((WIDTH, 2, N, N), BF), V((WIDTH, 2, N, N), BF),
            V((4, 2, N, N), F32), V((4, 2, N, N), F32), V((2, N, 128), F32), V((4, 2, N, N), BF),
            V((2, 4, 4, 64, N), BF), V((2, N, N), F32), V((2, 2, N, N), BF),
            dma((7,)), dma((2,)), dma((2,)), dma, dma, dma, dma, dma((2,)), dma((4,)), dma((4,)), dma((2, 4)), dma,
        ],
        compiler_params=pltpu.CompilerParams(
            collective_id=0, has_side_effects=True, vmem_limit_bytes=48 * 1024 * 1024),
        name="ptycho",
    )(*(pltpu.with_memory_space_constraint(a, pltpu.HBM) for a in (
        pos_t, object_field.reshape(2, blocks, N, N), probe, prop_phase, measured, tb, tbt)))
    band = pl.pallas_call(
        functools.partial(final_kernel, chips, blocks),
        out_shape=jax.ShapeDtypeStruct((2, blocks, N, N), BF),
        in_specs=[pl.BlockSpec(memory_space=pltpu.HBM), pl.BlockSpec(memory_space=pltpu.VMEM)],
        out_specs=pl.BlockSpec(memory_space=pltpu.HBM),
        scratch_shapes=[pltpu.SMEM((2, 2 * chips), jnp.int32), V((2, blocks, N, N), BF), dma((blocks,)), dma],
        compiler_params=pltpu.CompilerParams(vmem_limit_bytes=32 * 1024 * 1024),
        name="assemble",
    )(pltpu.with_memory_space_constraint(pos_t, pltpu.HBM), slots)
    return band.reshape(1, 2, height, N)


def solution(mesh):
    placed = (PS("depth", None, None, "pos"), PS(), PS(), PS("pos", None, None), PS())
    return jax.shard_map(
        local, mesh=mesh, in_specs=placed, out_specs=PS("depth", None, None, "pos"), check_vma=False
    )
```

```python
import functools
import math
import numpy as np
import jax, jax.numpy as jnp
from jax import lax
from jax.experimental import pallas as pl
from jax.experimental.pallas import tpu as pltpu
from jax.sharding import PartitionSpec as PS
BF=jnp.bfloat16; F32=jnp.float32
N=256; HF=128
MODES=4
WIDTH=4

def tables():
    k=np.arange(N); ph=(k[:,None]*k[None,:])%N
    ang=ph*(2*math.pi/N)
    fr=np.cos(ang)/16.0; fi=-np.sin(ang)/16.0
    tb=np.concatenate([fr[0::2],fi[0::2],fr[1::2],fi[1::2]],0)
    return jnp.asarray(tb,dtype=BF), jnp.asarray(tb.T,dtype=BF)

def dot(a,b): return jnp.dot(a,b,preferred_element_type=F32)
def iota(shape,d): return lax.broadcasted_iota(jnp.int32,shape,d)

def prep_tables(tb,tbt,tab,y,c):
    for r,f1,f2 in ((y,0,1),(c,3,2)):
        onehot=(iota((N,HF),0)==((iota((N,HF),1)-r)&255)).astype(F32).astype(BF)
        m1=dot(tb[...],onehot).astype(BF)
        onet=(iota((HF,N),1)==((iota((HF,N),0)-r)&255)).astype(F32).astype(BF)
        m2=dot(onet,tbt[...]).astype(BF)
        for par in range(2):
            a=m1[par*256:par*256+128]; b=m1[par*256+128:par*256+256]
            tab[f1,par,0:128,0:128]=a; tab[f1,par,0:128,128:256]=-b
            tab[f1,par,128:256,0:128]=b; tab[f1,par,128:256,128:256]=a
            a=m2[:,par*256:par*256+128]; b=m2[:,par*256+128:par*256+256]
            tab[f2,par,0:128,0:128]=a; tab[f2,par,0:128,128:256]=b
            tab[f2,par,128:256,0:128]=-b; tab[f2,par,128:256,128:256]=a

def prep_probe(probe,pr,tmp,y,c):
    ryt=(iota((N,N),1)==((iota((N,N),0)-y)&255)).astype(F32).astype(BF)
    rc=(iota((N,N),0)==((iota((N,N),1)-c)&255)).astype(F32).astype(BF)
    for m in range(4):
        for q in range(2):
            t=dot(ryt,probe[m,q]).astype(BF)
            pr[m,q]=dot(t,rc)

def perms():
    i0=iota((N,N),0); i1=iota((N,N),1)
    pt=(i1==(2*(i0&127)+(i0>>7))).astype(F32).astype(BF)
    p=(i0==(2*(i1&127)+(i1>>7))).astype(F32).astype(BF)
    return pt,p

def prep_k(phase,kk):
    pt,p=perms()
    x=phase[...]
    acc=None
    for _ in range(3):
        h=x.astype(BF)
        x=x-h.astype(F32)
        t=dot(dot(pt,h).astype(BF),p)
        acc=t if acc is None else acc+t
    kk[0]=jnp.cos(acc); kk[1]=jnp.sin(acc)

def prep_meas(meas,mp):
    pt,p=perms()
    mp[...]=dot(dot(pt,meas[...]).astype(BF),p)

RC=32
def dots1f(tab,P): return [dot(tab[0,par],P[par]) for par in range(2)]
def post1f(VV,L):
    for q in range(2):
        for r in range(0,128,RC):
            for par in range(2):
                V=VV[par][q*128+r:q*128+r+RC]
                lo=V[:,:128]; hi=V[:,128:]
                L[0,par*128+r:par*128+r+RC,q*128:q*128+128]=(lo+hi).astype(BF)
                L[1,par*128+r:par*128+r+RC,q*128:q*128+128]=(lo-hi).astype(BF)

def dots2f(tab,L): return [dot(L[cp],tab[2,cp]) for cp in range(2)]
def dots1i(tab,P): return [dot(tab[1,par],P[par]) for par in range(2)]
def post1i(E,L):
    for q in range(2):
        for r in range(0,128,RC):
            for cp in range(2):
                rr=slice(q*128+r,q*128+r+RC)
                a=E[0][rr,cp*128:cp*128+128]; b=E[1][rr,cp*128:cp*128+128]
                L[cp,r:r+RC,q*128:q*128+128]=(a+b).astype(BF)
                L[cp,128+r:128+r+RC,q*128:q*128+128]=(a-b).astype(BF)

def dots2i(tab,L): return [dot(L[cp],tab[3,cp]) for cp in range(2)]

def space(D,r,n,q,uc):
    a=D[0][r:r+n,q*128:q*128+128]; b=D[1][r:r+n,q*128:q*128+128]
    return a+b if uc==0 else a-b

def put2(P,q,r,sl,x0,x1):
    P[0,q*128+r:q*128+r+RC,sl]=(x0+x1).astype(BF)
    P[1,q*128+r:q*128+r+RC,sl]=(x0-x1).astype(BF)

def putf(P,q,r,sl,x):
    P[r//128,q*128+r%128:q*128+r%128+RC,sl]=x.astype(BF)

def halves(r): return (slice(r,r+RC),slice(128+r,128+r+RC))
def lanes(k): return slice(k*128,k*128+128)

def phase_a(m,tab,pr,o0,kk,P,L,psi1):
    for r in range(0,128,RC):
        for uc in range(2):
            sl=lanes(uc); xr=[];xi=[]
            for h in halves(r):
                a=pr[m,0,h,sl].astype(F32); b=pr[m,1,h,sl].astype(F32)
                c=o0[0,h,sl].astype(F32); d=o0[1,h,sl].astype(F32)
                xr.append(a*c-b*d); xi.append(a*d+b*c)
            put2(P,0,r,sl,*xr); put2(P,1,r,sl,*xi)
    V=dots1f(tab,P); yield
    post1f(V,L); SS=dots2f(tab,L); yield
    for r in range(0,256,RC):
        for cp in range(2):
            S=SS[cp][r:r+RC]; sl=lanes(cp)
            kr=kk[0,r:r+RC,sl]; ki=kk[1,r:r+RC,sl]
            putf(P,0,r,sl,S[:,:128]*kr-S[:,128:]*ki)
            putf(P,1,r,sl,S[:,:128]*ki+S[:,128:]*kr)
    E=dots1i(tab,P); yield
    post1i(E,L); D=dots2i(tab,L); yield
    for r in range(0,256,RC):
        for uc in range(2):
            for q in range(2): psi1[m,q,r:r+RC,lanes(uc)]=space(D,r,RC,q,uc)

def phase_b(m,tab,o1,P,L,psi1,far,inten):
    for r in range(0,128,RC):
        for uc in range(2):
            sl=lanes(uc); xr=[];xi=[]
            for h in halves(r):
                a=psi1[m,0,h,sl]; b=psi1[m,1,h,sl]
                c=o1[0,h,sl].astype(F32); d=o1[1,h,sl].astype(F32)
                xr.append(a*c-b*d); xi.append(a*d+b*c)
            put2(P,0,r,sl,*xr); put2(P,1,r,sl,*xi)
    V=dots1f(tab,P); yield
    post1f(V,L); SS=dots2f(tab,L); yield
    for r in range(0,256,RC):
        for cp in range(2):
            S=SS[cp][r:r+RC]
            far[m,cp,r:r+RC]=S
            inten[cp,r:r+RC]+=S[:,:128]*S[:,:128]+S[:,128:]*S[:,128:]

def phase_c(m,tab,P,L3,far,inten):
    for r in range(0,256,RC):
        for cp in range(2):
            w=inten[cp,r:r+RC]
            putf(P,0,r,lanes(cp),w*far[m,cp,r:r+RC,:128]); putf(P,1,r,lanes(cp),w*far[m,cp,r:r+RC,128:])
    E0,E1=dots1i(tab,P); yield
    for q in range(2):
        for r in range(4):
            for cp in range(2):
                rr=slice(q*128+r*32,q*128+r*32+32); sl=lanes(cp); to=lanes(q)
                L3[cp,r,m,0:32,to]=(E0[rr,sl]+E1[rr,sl]).astype(BF)
                L3[cp,r,m,32:64,to]=(E0[rr,sl]-E1[rr,sl]).astype(BF)

def phase_c2(r,tab,o1,L3,psi1,gs,adj):
    D=[dot(L3[cp,r].reshape(256,256),tab[3,cp]) for cp in range(2)]; yield
    for uc in range(2):
        sl=lanes(uc); gr=[None,None]; gi=[None,None]
        hs=(slice(r*32,r*32+32),slice(128+r*32,160+r*32))
        for m in range(4):
            ar=[];ai=[]
            for k,h in enumerate(hs):
                br=space(D,m*64+32*k,32,0,uc); bi=space(D,m*64+32*k,32,1,uc)
                a=psi1[m,0,h,sl]; b=psi1[m,1,h,sl]
                tr=a*br+b*bi; ti=a*bi-b*br
                gr[k]=tr if m==0 else gr[k]+tr; gi[k]=ti if m==0 else gi[k]+ti
                c=o1[0,h,sl]; d=o1[1,h,sl]
                ar.append(c*br+d*bi); ai.append(c*bi-d*br)
            put2(adj.at[m],0,r*32,sl,*ar); put2(adj.at[m],1,r*32,sl,*ai)
        for k,h in enumerate(hs):
            gs[0,h,sl]=gr[k].astype(BF); gs[1,h,sl]=gi[k].astype(BF)

def phase_d(m,tab,kk,P,L,L2,adj):
    V=dots1f(tab,adj.at[m]); yield
    post1f(V,L); SS=dots2f(tab,L); yield
    for r in range(0,256,RC):
        for cp in range(2):
            S=SS[cp][r:r+RC].astype(BF).astype(F32); sl=lanes(cp)
            kr=kk[0,r:r+RC,sl]; ki=kk[1,r:r+RC,sl]
            putf(P,0,r,sl,kr*S[:,:128]+ki*S[:,128:])
            putf(P,1,r,sl,kr*S[:,128:]-ki*S[:,:128])
    E0,E1=dots1i(tab,P); yield
    for q in range(2):
        for r in range(0,128,RC):
            for cp in range(2):
                rr=slice(q*128+r,q*128+r+RC); sl=lanes(cp); to=lanes(q); h=r//64; k=r%64
                L2[cp,h,m,k:k+RC,to]=(E0[rr,sl]+E1[rr,sl]).astype(BF)
                L2[cp,2+h,m,k:k+RC,to]=(E0[rr,sl]-E1[rr,sl]).astype(BF)

def phase_e(r,tab,pr,L2,gs):
    D=(dot(L2[0,r].reshape(256,256),tab[3,0]), dot(L2[1,r].reshape(256,256),tab[3,1])); yield
    for k in range(0,64,RC):
        rows=slice(r*64+k,r*64+k+RC)
        for uc in range(2):
            sl=lanes(uc)
            gr=None
            for m in range(4):
                wr=space(D,m*64+k,RC,0,uc); wi=space(D,m*64+k,RC,1,uc)
                a=pr[m,0,rows,sl].astype(F32); b=pr[m,1,rows,sl].astype(F32)
                tr=a*wr+b*wi; ti=a*wi-b*wr
                gr,gi=(tr,ti) if gr is None else (gr+tr,gi+ti)
            gs[0,rows,sl]=gr.astype(BF); gs[1,rows,sl]=gi.astype(BF)


def weave(items,width=2):
    todo=list(items); live=[]
    while todo or live:
        if todo and len(live)<width:
            item=todo.pop(0)
            if item[0] is not None: item[0]()
        else:
            item=live.pop(0)
        try:
            next(item[1])
            live.append(item)
        except StopIteration:
            if item[2] is not None: item[2]()


MESH = pl.DeviceIdType.MESH


def main_kernel(chips, height, pos_h, obj, probe_h, phase_h, meas_h, tb_h, tbt_h, out,
                pos, band, w_left, w_right, w_part, near, farw, ob, probe, phase, meas, mtmp,
                tb, tbt, tab, pr, kk, mp, P, L, psi1, far, inten, adj, L2, L3, gs,
                in_sem, obj_send, obj_recv, near_send, near_recv, m_send, m_recv,
                g_send, g_recv, h_send, h_recv, c_send, c_recv, loc_sem):
    d = lax.axis_index("depth")
    p = lax.axis_index("pos")
    left = lax.rem(p + chips - 1, chips)
    right = lax.rem(p + 1, chips)
    nb = lax.rem(p + 1 - 2 * d + chips, chips)
    total = 2 * chips
    mine = lax.rem(2 * p - d + total, total)
    other = lax.rem(2 * p + d - 1 + total, total)
    q_left = lax.rem(2 * p - 2 + total, total)
    q_right = 2 * p + 1

    loads = [
        pltpu.make_async_copy(obj, band, in_sem.at[0]),
        pltpu.make_async_copy(meas_h.at[d], mtmp, in_sem.at[1]),
        pltpu.make_async_copy(tb_h, tb, in_sem.at[2]),
        pltpu.make_async_copy(tbt_h, tbt, in_sem.at[3]),
        pltpu.make_async_copy(probe_h, probe, in_sem.at[4]),
        pltpu.make_async_copy(phase_h, phase, in_sem.at[5]),
        pltpu.make_async_copy(pos_h, pos, in_sem.at[6]),
    ]
    for cp in loads:
        cp.start()
    barrier = pltpu.get_barrier_semaphore()
    peers = ((1 - d, p), (0, left), (1, right), (d, nb))
    for peer in peers:
        pl.semaphore_signal(barrier, inc=1, device_id=peer, device_id_type=MESH)

    blocks = height // N
    row_id = iota((N, N), 0)

    def window(q, part):
        y = pos[0, q]
        k = y >> 8
        k2 = jnp.minimum(k + 1, blocks - 1)
        a = band[part, k]
        b = band[part, k2]
        return jnp.where(row_id >= (y & 255), a.astype(F32), b.astype(F32)).astype(BF)

    loads[6].wait()
    loads[0].wait()
    for part in range(2):
        w_left[part] = window(q_left, part)
    for part in range(2):
        w_right[part] = window(q_right, part)
    for part in range(2):
        w_part[part] = window(other, part)
    for part in range(2):
        near[d, part] = window(mine, part)
    y = pos[0, mine] & 255
    c = pos[1, mine] & 255
    pl.semaphore_wait(barrier, 4)

    def remote(src, dst, ss, rs, dev):
        return pltpu.make_async_remote_copy(src_ref=src, dst_ref=dst, send_sem=ss, recv_sem=rs,
                                            device_id=dev, device_id_type=MESH)

    c_left = remote(w_left, farw.at[d], obj_send.at[0], obj_recv.at[d], (0, left))
    c_right = remote(w_right, farw.at[d], obj_send.at[1], obj_recv.at[d], (1, right))
    c_part = remote(w_part, near.at[d], near_send, near_recv, (1 - d, p))
    go_left = p > 0
    wrap_a = jnp.logical_and(d == 0, p == chips - 1)

    def send_object():
        @pl.when(go_left)
        def _():
            c_left.start()

        c_right.start()

    def sent_object():
        @pl.when(go_left)
        def _():
            c_left.wait_send()

        c_right.wait_send()

    @pl.when(d == 0)
    def _():
        send_object()

    c_part.start()
    loads[1].wait()
    c_meas = remote(meas.at[0], meas.at[1], m_send, m_recv, (1, right))
    meas[0] = mtmp[...].astype(BF)
    loads[2].wait()
    loads[3].wait()
    prep_tables(tb, tbt, tab, y, c)
    loads[4].wait()
    prep_probe(probe, pr, None, y, c)
    loads[5].wait()
    prep_k(phase, kk)

    @pl.when(d == 1)
    def _():
        send_object()
        c_meas.start()

    inten[...] = jnp.zeros_like(inten)

    near_mask = (iota((N, N), 1) - c) * (1 - 2 * d) - d >= 0

    def merge(s):
        for part in range(2):
            ob[s, part] = jnp.where(near_mask, near[s, part].astype(F32),
                                    farw[s, part].astype(F32))

    def bufs(m):
        return P.at[m % WIDTH], L.at[m % WIDTH]

    def run(gens):
        weave([(None, x, None) for x in gens], WIDTH)

    c_part.wait_recv()

    def got_far(k):
        @pl.when(jnp.logical_not(wrap_a))
        def _():
            remote(w_left, farw.at[k], obj_send.at[0], obj_recv.at[k], (0, left)).wait_recv()

    got_far(0)
    merge(0)
    run([phase_a(m, tab, pr, ob.at[0], kk, *bufs(m), psi1) for m in range(MODES)])
    got_far(1)
    merge(1)
    run([phase_b(m, tab, ob.at[1], *bufs(m), psi1, far, inten) for m in range(MODES)])

    @pl.when(d == 1)
    def _():
        c_meas.wait()

    prep_meas(meas.at[d], mp)
    for cp in range(2):
        inten[cp] = (inten[cp] - mp[:, cp * 128:cp * 128 + 128]) * 0.125
    run([phase_c(m, tab, P.at[m], L3, far, inten) for m in range(MODES)])

    def strip(slot, i, dev):
        rows = pl.ds(i * 32, 32)
        return remote(gs.at[1, :, rows, :], out.at[2 + slot, :, rows, :], h_send.at[i], h_recv.at[slot, i], dev)

    def ship1(r):
        @pl.when(jnp.logical_not(wrap_a))
        def _():
            strip(d, r, (1, nb)).start()
            strip(d, r + 4, (1, nb)).start()

    weave([(None, phase_c2(r, tab, ob.at[1], L3, psi1, gs.at[1], adj), functools.partial(ship1, r))
           for r in range(4)], 2)

    near1 = remote(gs.at[1], out.at[d], g_send.at[1], g_recv.at[d], (1, p))
    stay1 = pltpu.make_async_copy(gs.at[1], out.at[d], loc_sem)

    @pl.when(d == 0)
    def _():
        near1.start()

    @pl.when(d == 1)
    def _():
        stay1.start()

    run([phase_d(m, tab, kk, *bufs(m), L2, adj) for m in range(MODES)])

    def chunk(r, dev):
        rows = pl.ds(r * 64, 64)
        return remote(gs.at[0, :, rows, :], out.at[2 + d, :, rows, :], c_send.at[r], c_recv.at[d, r], dev)

    def incoming(slot, r):
        rows = pl.ds(r * 64, 64)
        return remote(gs.at[0, :, rows, :], out.at[2 + slot, :, rows, :], c_send.at[r], c_recv.at[slot, r],
                      (0, nb))

    def ship(r):
        @pl.when(jnp.logical_not(wrap_a))
        def _():
            chunk(r, (0, nb)).start()

    weave([(None, phase_e(r, tab, pr, L2, gs.at[0]), functools.partial(ship, r)) for r in range(4)], 2)
    near0 = remote(gs.at[0], out.at[d], g_send.at[1], g_recv.at[d], (0, p))
    stay0 = pltpu.make_async_copy(gs.at[0], out.at[d], loc_sem)

    @pl.when(d == 1)
    def _():
        near0.start()
        stay1.wait()

    @pl.when(d == 0)
    def _():
        stay0.start()
        near1.wait_send()

    sent_object()
    c_part.wait_send()

    @pl.when(jnp.logical_not(wrap_a))
    def _():
        for i in range(8):
            strip(d, i, (1, nb)).wait_send()
        for r in range(4):
            chunk(r, (0, nb)).wait_send()

    @pl.when(d == 1)
    def _():
        near0.wait_send()
        remote(gs.at[1], out.at[0], g_send.at[1], g_recv.at[0], (0, p)).wait_recv()
        for i in range(8):
            strip(1, i, (1, nb)).wait_recv()

        @pl.when(p > 0)
        def _():
            for i in range(8):
                strip(0, i, (1, nb)).wait_recv()

    @pl.when(d == 0)
    def _():
        stay0.wait()
        remote(gs.at[0], out.at[1], g_send.at[1], g_recv.at[1], (0, p)).wait_recv()
        for r in range(4):
            incoming(1, r).wait_recv()

        @pl.when(p > 0)
        def _():
            for r in range(4):
                incoming(0, r).wait_recv()


def final_kernel(chips, blocks, pos_h, slots, out, pos, acc, sem, pos_sem):
    load = pltpu.make_async_copy(pos_h, pos, pos_sem)
    load.start()
    p = lax.axis_index("pos")
    total = 2 * chips
    acc[...] = jnp.zeros_like(acc)
    load.wait()
    rows = iota((16, N), 0)
    cols = iota((16, N), 1)
    places = []
    for off, ge in ((0, True), (total - 1, False), (total - 2, False), (1, True)):
        q = lax.rem(2 * p + off, total)
        y = pos[0, q]
        c = pos[1, q] & 255
        k = y >> 8
        places.append((k, jnp.minimum(k + 1, blocks - 1), y & 255, (cols >= c) if ge else (cols < c)))
    copies = []
    for part in range(2):
        for slot, (k, k2, yy, cm) in enumerate(places):
            for r0 in range(0, N, 16):
                later = r0 + 15 < yy
                to = jnp.where(later, k2, k)
                keep = cm & (rows >= jnp.where(later, 0, yy - r0))
                x = slots[slot, part, r0:r0 + 16]
                acc[part, to, r0:r0 + 16] += jnp.where(keep, x, jnp.zeros_like(x))
            rb = pl.multiple_of((yy >> 4) * 16, 16)
            keep = cm & (rows < yy - rb)
            x = slots[slot, part, pl.ds(rb, 16)]
            acc[part, k2, pl.ds(rb, 16)] += jnp.where(keep, x, jnp.zeros_like(x))
        cp = pltpu.make_async_copy(acc.at[part], out.at[part], sem.at[part])
        cp.start()
        copies.append(cp)
    for cp in copies:
        cp.wait()


def local(object_field, probe, prop_phase, measured, positions):
    chips = lax.axis_size("pos")
    height = object_field.shape[2]
    blocks = height // N
    tb, tbt = tables()
    pos_t = positions.T
    any_ = pl.BlockSpec(memory_space=pl.ANY)
    V = pltpu.VMEM
    win = V((2, N, N), BF)
    dma = pltpu.SemaphoreType.DMA
    slots = pl.pallas_call(
        functools.partial(main_kernel, chips, height),
        out_shape=jax.ShapeDtypeStruct((4, 2, N, N), BF),
        in_specs=[pl.BlockSpec(memory_space=pltpu.HBM)] * 7,
        out_specs=any_,
        scratch_shapes=[
            pltpu.SMEM((2, 2 * chips), jnp.int32), V((2, blocks, N, N), BF), win, win, win, V((2, 2, N, N), BF), V((2, 2, N, N), BF),
            V((2, 2, N, N), F32), V((4, 2, N, N), BF), V((N, N), F32), V((2, N, N), BF), V((N, N), F32),
            V((512, N), BF), V((N, 512), BF), V((4, 2, N, N), BF), V((4, 2, N, N), F32),
            V((2, N, N), F32), V((N, N), F32), V((WIDTH, 2, N, N), BF), V((WIDTH, 2, N, N), BF),
            V((4, 2, N, N), F32), V((4, 2, N, N), F32), V((2, N, 128), F32), V((4, 2, N, N), BF),
            V((2, 4, 4, 64, N), BF), V((2, 4, 4, 64, N), BF), V((2, 2, N, N), BF),
            dma((7,)), dma((2,)), dma((2,)), dma, dma, dma, dma,
            dma((2,)), dma((4,)), dma((8,)), dma((2, 8)), dma((4,)), dma((2, 4)), dma,
        ],
        compiler_params=pltpu.CompilerParams(
            collective_id=0, has_side_effects=True, vmem_limit_bytes=48 * 1024 * 1024),
        name="ptycho",
    )(*(pltpu.with_memory_space_constraint(a, pltpu.HBM) for a in (
        pos_t, object_field.reshape(2, blocks, N, N), probe, prop_phase, measured, tb, tbt)))
    band = pl.pallas_call(
        functools.partial(final_kernel, chips, blocks),
        out_shape=jax.ShapeDtypeStruct((2, blocks, N, N), BF),
        in_specs=[any_, pl.BlockSpec(memory_space=pltpu.VMEM)],
        out_specs=pl.BlockSpec(memory_space=pltpu.HBM),
        scratch_shapes=[pltpu.SMEM((2, 2 * chips), jnp.int32), V((2, blocks, N, N), BF), dma((2,)), dma],
        compiler_params=pltpu.CompilerParams(vmem_limit_bytes=32 * 1024 * 1024),
        name="assemble",
    )(pos_t, slots)
    return band.reshape(1, 2, height, N)


def solution(mesh):
    placed = (PS("depth", None, None, "pos"), PS(), PS(), PS("pos", None, None), PS())
    return jax.shard_map(
        local, mesh=mesh, in_specs=placed, out_specs=PS("depth", None, None, "pos"), check_vma=False
    )
```

```python
import functools
import math
import numpy as np
import jax, jax.numpy as jnp
from jax import lax
from jax.experimental import pallas as pl
from jax.experimental.pallas import tpu as pltpu
from jax.sharding import PartitionSpec as PS
BF=jnp.bfloat16; F32=jnp.float32
N=256; HF=128
MODES=4
WIDTH=4

def tables():
    k=np.arange(N); ph=(k[:,None]*k[None,:])%N
    ang=ph*(2*math.pi/N)
    fr=np.cos(ang)/16.0; fi=-np.sin(ang)/16.0
    tb=np.concatenate([fr[0::2],fi[0::2],fr[1::2],fi[1::2]],0)
    return jnp.asarray(tb,dtype=BF), jnp.asarray(tb.T,dtype=BF)

def dot(a,b): return jnp.dot(a,b,preferred_element_type=F32)
def iota(shape,d): return lax.broadcasted_iota(jnp.int32,shape,d)

def prep_tables(tb,tbt,tab,y,c):
    for r,f1,f2 in ((y,0,1),(c,3,2)):
        onehot=(iota((N,HF),0)==((iota((N,HF),1)-r)&255)).astype(F32).astype(BF)
        m1=dot(tb[...],onehot).astype(BF)
        onet=(iota((HF,N),1)==((iota((HF,N),0)-r)&255)).astype(F32).astype(BF)
        m2=dot(onet,tbt[...]).astype(BF)
        for par in range(2):
            a=m1[par*256:par*256+128]; b=m1[par*256+128:par*256+256]
            tab[f1,par,0:128,0:128]=a; tab[f1,par,0:128,128:256]=-b
            tab[f1,par,128:256,0:128]=b; tab[f1,par,128:256,128:256]=a
            a=m2[:,par*256:par*256+128]; b=m2[:,par*256+128:par*256+256]
            tab[f2,par,0:128,0:128]=a; tab[f2,par,0:128,128:256]=b
            tab[f2,par,128:256,0:128]=-b; tab[f2,par,128:256,128:256]=a

def prep_probe(probe,pr,tmp,y,c):
    ryt=(iota((N,N),1)==((iota((N,N),0)-y)&255)).astype(F32).astype(BF)
    rc=(iota((N,N),0)==((iota((N,N),1)-c)&255)).astype(F32).astype(BF)
    for m in range(4):
        for q in range(2):
            t=dot(ryt,probe[m,q]).astype(BF)
            pr[m,q]=dot(t,rc)

def perms():
    i0=iota((N,N),0); i1=iota((N,N),1)
    pt=(i1==(2*(i0&127)+(i0>>7))).astype(F32).astype(BF)
    p=(i0==(2*(i1&127)+(i1>>7))).astype(F32).astype(BF)
    return pt,p

def prep_k(phase,kk):
    pt,p=perms()
    x=phase[...]
    acc=None
    for _ in range(3):
        h=x.astype(BF)
        x=x-h.astype(F32)
        t=dot(dot(pt,h).astype(BF),p)
        acc=t if acc is None else acc+t
    kk[0]=jnp.cos(acc); kk[1]=jnp.sin(acc)

def prep_meas(meas,mp):
    pt,p=perms()
    mp[...]=dot(dot(pt,meas[...]).astype(BF),p)

RC=32
def dots1f(tab,P): return [dot(tab[0,par],P[par]) for par in range(2)]
def post1f(VV,L):
    for q in range(2):
        for r in range(0,128,RC):
            for par in range(2):
                V=VV[par][q*128+r:q*128+r+RC]
                lo=V[:,:128]; hi=V[:,128:]
                L[0,par*128+r:par*128+r+RC,q*128:q*128+128]=(lo+hi).astype(BF)
                L[1,par*128+r:par*128+r+RC,q*128:q*128+128]=(lo-hi).astype(BF)

def dots2f(tab,L): return [dot(L[cp],tab[2,cp]) for cp in range(2)]
def dots1i(tab,P): return [dot(tab[1,par],P[par]) for par in range(2)]
def post1i(E,L):
    for q in range(2):
        for r in range(0,128,RC):
            for cp in range(2):
                rr=slice(q*128+r,q*128+r+RC)
                a=E[0][rr,cp*128:cp*128+128]; b=E[1][rr,cp*128:cp*128+128]
                L[cp,r:r+RC,q*128:q*128+128]=(a+b).astype(BF)
                L[cp,128+r:128+r+RC,q*128:q*128+128]=(a-b).astype(BF)

def dots2i(tab,L): return [dot(L[cp],tab[3,cp]) for cp in range(2)]

def space(D,r,n,q,uc):
    a=D[0][r:r+n,q*128:q*128+128]; b=D[1][r:r+n,q*128:q*128+128]
    return a+b if uc==0 else a-b

def put2(P,q,r,sl,x0,x1):
    P[0,q*128+r:q*128+r+RC,sl]=(x0+x1).astype(BF)
    P[1,q*128+r:q*128+r+RC,sl]=(x0-x1).astype(BF)

def putf(P,q,r,sl,x):
    P[r//128,q*128+r%128:q*128+r%128+RC,sl]=x.astype(BF)

def halves(r): return (slice(r,r+RC),slice(128+r,128+r+RC))
def lanes(k): return slice(k*128,k*128+128)

def phase_a(m,tab,pr,o0,kk,P,L,psi1):
    for r in range(0,128,RC):
        for uc in range(2):
            sl=lanes(uc); xr=[];xi=[]
            for h in halves(r):
                a=pr[m,0,h,sl].astype(F32); b=pr[m,1,h,sl].astype(F32)
                c=o0[0,h,sl].astype(F32); d=o0[1,h,sl].astype(F32)
                xr.append(a*c-b*d); xi.append(a*d+b*c)
            put2(P,0,r,sl,*xr); put2(P,1,r,sl,*xi)
    V=dots1f(tab,P); yield
    post1f(V,L); SS=dots2f(tab,L); yield
    for r in range(0,256,RC):
        for cp in range(2):
            S=SS[cp][r:r+RC]; sl=lanes(cp)
            kr=kk[0,r:r+RC,sl]; ki=kk[1,r:r+RC,sl]
            putf(P,0,r,sl,S[:,:128]*kr-S[:,128:]*ki)
            putf(P,1,r,sl,S[:,:128]*ki+S[:,128:]*kr)
    E=dots1i(tab,P); yield
    post1i(E,L); D=dots2i(tab,L); yield
    for r in range(0,256,RC):
        for uc in range(2):
            for q in range(2): psi1[m,q,r:r+RC,lanes(uc)]=space(D,r,RC,q,uc)

def phase_b(m,tab,o1,P,L,psi1,far,inten):
    for r in range(0,128,RC):
        for uc in range(2):
            sl=lanes(uc); xr=[];xi=[]
            for h in halves(r):
                a=psi1[m,0,h,sl]; b=psi1[m,1,h,sl]
                c=o1[0,h,sl].astype(F32); d=o1[1,h,sl].astype(F32)
                xr.append(a*c-b*d); xi.append(a*d+b*c)
            put2(P,0,r,sl,*xr); put2(P,1,r,sl,*xi)
    V=dots1f(tab,P); yield
    post1f(V,L); SS=dots2f(tab,L); yield
    for r in range(0,256,RC):
        for cp in range(2):
            S=SS[cp][r:r+RC]
            far[m,cp,r:r+RC]=S
            inten[cp,r:r+RC]+=S[:,:128]*S[:,:128]+S[:,128:]*S[:,128:]

def phase_c(m,tab,P,L3,far,inten):
    for r in range(0,256,RC):
        for cp in range(2):
            w=inten[cp,r:r+RC]
            putf(P,0,r,lanes(cp),w*far[m,cp,r:r+RC,:128]); putf(P,1,r,lanes(cp),w*far[m,cp,r:r+RC,128:])
    E0,E1=dots1i(tab,P); yield
    for q in range(2):
        for r in range(4):
            for cp in range(2):
                rr=slice(q*128+r*32,q*128+r*32+32); sl=lanes(cp); to=lanes(q)
                L3[cp,r,m,0:32,to]=(E0[rr,sl]+E1[rr,sl]).astype(BF)
                L3[cp,r,m,32:64,to]=(E0[rr,sl]-E1[rr,sl]).astype(BF)

def phase_c2(r,tab,o1,L3,psi1,gs,adj):
    D=[dot(L3[cp,r].reshape(256,256),tab[3,cp]) for cp in range(2)]; yield
    for uc in range(2):
        sl=lanes(uc); gr=[None,None]; gi=[None,None]
        hs=(slice(r*32,r*32+32),slice(128+r*32,160+r*32))
        for m in range(4):
            ar=[];ai=[]
            for k,h in enumerate(hs):
                br=space(D,m*64+32*k,32,0,uc); bi=space(D,m*64+32*k,32,1,uc)
                a=psi1[m,0,h,sl]; b=psi1[m,1,h,sl]
                tr=a*br+b*bi; ti=a*bi-b*br
                gr[k]=tr if m==0 else gr[k]+tr; gi[k]=ti if m==0 else gi[k]+ti
                c=o1[0,h,sl]; d=o1[1,h,sl]
                ar.append(c*br+d*bi); ai.append(c*bi-d*br)
            put2(adj.at[m],0,r*32,sl,*ar); put2(adj.at[m],1,r*32,sl,*ai)
        for k,h in enumerate(hs):
            gs[0,h,sl]=gr[k].astype(BF); gs[1,h,sl]=gi[k].astype(BF)

def phase_d(m,tab,kk,P,L,L2,adj):
    V=dots1f(tab,adj.at[m]); yield
    post1f(V,L); SS=dots2f(tab,L); yield
    for r in range(0,256,RC):
        for cp in range(2):
            S=SS[cp][r:r+RC].astype(BF).astype(F32); sl=lanes(cp)
            kr=kk[0,r:r+RC,sl]; ki=kk[1,r:r+RC,sl]
            putf(P,0,r,sl,kr*S[:,:128]+ki*S[:,128:])
            putf(P,1,r,sl,kr*S[:,128:]-ki*S[:,:128])
    E0,E1=dots1i(tab,P); yield
    for q in range(2):
        for r in range(0,128,RC):
            for cp in range(2):
                rr=slice(q*128+r,q*128+r+RC); sl=lanes(cp); to=lanes(q); h=r//64; k=r%64
                L2[cp,h,m,k:k+RC,to]=(E0[rr,sl]+E1[rr,sl]).astype(BF)
                L2[cp,2+h,m,k:k+RC,to]=(E0[rr,sl]-E1[rr,sl]).astype(BF)

def phase_e(r,tab,pr,L2,gs):
    D=(dot(L2[0,r].reshape(256,256),tab[3,0]), dot(L2[1,r].reshape(256,256),tab[3,1])); yield
    for k in range(0,64,RC):
        rows=slice(r*64+k,r*64+k+RC)
        for uc in range(2):
            sl=lanes(uc)
            gr=None
            for m in range(4):
                wr=space(D,m*64+k,RC,0,uc); wi=space(D,m*64+k,RC,1,uc)
                a=pr[m,0,rows,sl].astype(F32); b=pr[m,1,rows,sl].astype(F32)
                tr=a*wr+b*wi; ti=a*wi-b*wr
                gr,gi=(tr,ti) if gr is None else (gr+tr,gi+ti)
            gs[0,rows,sl]=gr.astype(BF); gs[1,rows,sl]=gi.astype(BF)


def weave(items,width=2):
    todo=list(items); live=[]
    while todo or live:
        if todo and len(live)<width:
            item=todo.pop(0)
            if item[0] is not None: item[0]()
        else:
            item=live.pop(0)
        try:
            next(item[1])
            live.append(item)
        except StopIteration:
            if item[2] is not None: item[2]()


MESH = pl.DeviceIdType.MESH


def main_kernel(chips, height, pos_h, obj, probe_h, phase_h, meas_h, tb_h, tbt_h, out,
                pos, band, w_left, w_right, w_part, near, farw, ob, probe, phase, meas, mtmp,
                tb, tbt, tab, pr, kk, mp, P, L, psi1, far, inten, adj, L2, L3, gs,
                in_sem, obj_send, obj_recv, near_send, near_recv, m_send, m_recv,
                g_send, g_recv, h_send, h_recv, c_send, c_recv, loc_sem):
    d = lax.axis_index("depth")
    p = lax.axis_index("pos")
    left = lax.rem(p + chips - 1, chips)
    right = lax.rem(p + 1, chips)
    nb = lax.rem(p + 1 - 2 * d + chips, chips)
    total = 2 * chips
    mine = lax.rem(2 * p - d + total, total)
    other = lax.rem(2 * p + d - 1 + total, total)
    q_left = lax.rem(2 * p - 2 + total, total)
    q_right = 2 * p + 1

    barrier = pltpu.get_barrier_semaphore()
    peers = ((1 - d, p), (0, left), (1, right), (d, nb))
    for peer in peers:
        pl.semaphore_signal(barrier, inc=1, device_id=peer, device_id_type=MESH)

    loads = [
        pltpu.make_async_copy(obj, band, in_sem.at[0]),
        pltpu.make_async_copy(meas_h.at[d], mtmp, in_sem.at[1]),
        pltpu.make_async_copy(tb_h, tb, in_sem.at[2]),
        pltpu.make_async_copy(tbt_h, tbt, in_sem.at[3]),
        pltpu.make_async_copy(probe_h, probe, in_sem.at[4]),
        pltpu.make_async_copy(phase_h, phase, in_sem.at[5]),
        pltpu.make_async_copy(pos_h, pos, in_sem.at[6]),
    ]
    for cp in loads:
        cp.start()

    blocks = height // N
    row_id = iota((N, N), 0)

    def window(q, part):
        y = pos[0, q]
        k = y >> 8
        k2 = jnp.minimum(k + 1, blocks - 1)
        a = band[part, k]
        b = band[part, k2]
        return jnp.where(row_id >= (y & 255), a.astype(F32), b.astype(F32)).astype(BF)

    loads[6].wait()
    loads[0].wait()
    for part in range(2):
        w_left[part] = window(q_left, part)
    for part in range(2):
        w_right[part] = window(q_right, part)
    for part in range(2):
        w_part[part] = window(other, part)
    y = pos[0, mine] & 255
    c = pos[1, mine] & 255
    pl.semaphore_wait(barrier, 4)

    def remote(src, dst, ss, rs, dev):
        return pltpu.make_async_remote_copy(src_ref=src, dst_ref=dst, send_sem=ss, recv_sem=rs,
                                            device_id=dev, device_id_type=MESH)

    c_left = remote(w_left, farw.at[d], obj_send.at[0], obj_recv.at[d], (0, left))
    c_right = remote(w_right, farw.at[d], obj_send.at[1], obj_recv.at[d], (1, right))
    c_part = remote(w_part, near.at[d], near_send, near_recv, (1 - d, p))
    go_left = p > 0
    wrap_a = jnp.logical_and(d == 0, p == chips - 1)

    def send_object():
        @pl.when(go_left)
        def _():
            c_left.start()

        c_right.start()

    def sent_object():
        @pl.when(go_left)
        def _():
            c_left.wait_send()

        c_right.wait_send()

    @pl.when(d == 0)
    def _():
        send_object()

    c_part.start()
    loads[1].wait()
    c_meas = remote(meas.at[0], meas.at[1], m_send, m_recv, (1, right))
    meas[0] = mtmp[...].astype(BF)
    loads[2].wait()
    loads[3].wait()
    prep_tables(tb, tbt, tab, y, c)
    loads[4].wait()
    prep_probe(probe, pr, None, y, c)
    loads[5].wait()
    prep_k(phase, kk)
    for part in range(2):
        near[d, part] = window(mine, part)
    inten[...] = jnp.zeros_like(inten)

    @pl.when(d == 1)
    def _():
        send_object()
        c_meas.start()


    near_mask = (iota((N, N), 1) - c) * (1 - 2 * d) - d >= 0

    def merge(s):
        for part in range(2):
            ob[s, part] = jnp.where(near_mask, near[s, part].astype(F32),
                                    farw[s, part].astype(F32))

    def bufs(m):
        return P.at[m % WIDTH], L.at[m % WIDTH]

    def run(gens):
        weave([(None, x, None) for x in gens], WIDTH)

    c_part.wait_recv()

    def got_far(k):
        @pl.when(jnp.logical_not(wrap_a))
        def _():
            remote(w_left, farw.at[k], obj_send.at[0], obj_recv.at[k], (0, left)).wait_recv()

    got_far(0)
    merge(0)
    run([phase_a(m, tab, pr, ob.at[0], kk, *bufs(m), psi1) for m in range(MODES)])
    got_far(1)
    merge(1)
    run([phase_b(m, tab, ob.at[1], *bufs(m), psi1, far, inten) for m in range(MODES)])

    @pl.when(d == 1)
    def _():
        c_meas.wait()

    prep_meas(meas.at[d], mp)
    for cp in range(2):
        inten[cp] = (inten[cp] - mp[:, cp * 128:cp * 128 + 128]) * 0.125
    run([phase_c(m, tab, P.at[m], L3, far, inten) for m in range(MODES)])

    def strip(slot, i, dev):
        rows = pl.ds(i * 32, 32)
        return remote(gs.at[1, :, rows, :], out.at[2 + slot, :, rows, :], h_send.at[i], h_recv.at[slot, i], dev)

    def ship1(r):
        @pl.when(jnp.logical_not(wrap_a))
        def _():
            strip(d, r, (1, nb)).start()
            strip(d, r + 4, (1, nb)).start()

    weave([(None, phase_c2(r, tab, ob.at[1], L3, psi1, gs.at[1], adj), functools.partial(ship1, r))
           for r in range(4)], 2)

    near1 = remote(gs.at[1], out.at[d], g_send.at[1], g_recv.at[d], (1, p))
    stay1 = pltpu.make_async_copy(gs.at[1], out.at[d], loc_sem)

    @pl.when(d == 0)
    def _():
        near1.start()

    @pl.when(d == 1)
    def _():
        stay1.start()

    run([phase_d(m, tab, kk, *bufs(m), L2, adj) for m in range(MODES)])

    def chunk(r, dev):
        rows = pl.ds(r * 64, 64)
        return remote(gs.at[0, :, rows, :], out.at[2 + d, :, rows, :], c_send.at[r], c_recv.at[d, r], dev)

    def incoming(slot, r):
        rows = pl.ds(r * 64, 64)
        return remote(gs.at[0, :, rows, :], out.at[2 + slot, :, rows, :], c_send.at[r], c_recv.at[slot, r],
                      (0, nb))

    def ship(r):
        @pl.when(jnp.logical_not(wrap_a))
        def _():
            chunk(r, (0, nb)).start()

    weave([(None, phase_e(r, tab, pr, L2, gs.at[0]), functools.partial(ship, r)) for r in range(4)], 2)
    near0 = remote(gs.at[0], out.at[d], g_send.at[1], g_recv.at[d], (0, p))
    stay0 = pltpu.make_async_copy(gs.at[0], out.at[d], loc_sem)

    @pl.when(d == 1)
    def _():
        near0.start()
        stay1.wait()

    @pl.when(d == 0)
    def _():
        stay0.start()
        near1.wait_send()

    sent_object()
    c_part.wait_send()

    @pl.when(jnp.logical_not(wrap_a))
    def _():
        for i in range(8):
            strip(d, i, (1, nb)).wait_send()
        for r in range(4):
            chunk(r, (0, nb)).wait_send()

    @pl.when(d == 1)
    def _():
        near0.wait_send()
        remote(gs.at[1], out.at[0], g_send.at[1], g_recv.at[0], (0, p)).wait_recv()
        for i in range(8):
            strip(1, i, (1, nb)).wait_recv()

        @pl.when(p > 0)
        def _():
            for i in range(8):
                strip(0, i, (1, nb)).wait_recv()

    @pl.when(d == 0)
    def _():
        stay0.wait()
        remote(gs.at[0], out.at[1], g_send.at[1], g_recv.at[1], (0, p)).wait_recv()
        for r in range(4):
            incoming(1, r).wait_recv()

        @pl.when(p > 0)
        def _():
            for r in range(4):
                incoming(0, r).wait_recv()


def final_kernel(chips, blocks, pos_h, slots, out, pos, acc, sem, pos_sem):
    load = pltpu.make_async_copy(pos_h, pos, pos_sem)
    load.start()
    p = lax.axis_index("pos")
    total = 2 * chips
    acc[...] = jnp.zeros_like(acc)
    load.wait()
    rows = iota((16, N), 0)
    cols = iota((16, N), 1)
    places = []
    for off, ge in ((0, True), (total - 1, False), (total - 2, False), (1, True)):
        q = lax.rem(2 * p + off, total)
        y = pos[0, q]
        c = pos[1, q] & 255
        k = y >> 8
        places.append((k, jnp.minimum(k + 1, blocks - 1), y & 255, (cols >= c) if ge else (cols < c)))
    copies = []
    for part in range(2):
        for slot, (k, k2, yy, cm) in enumerate(places):
            to = [jnp.where(r0 + 15 < yy, k2, jnp.where(r0 >= yy, k, blocks)) for r0 in range(0, N, 16)]
            old = [acc[part, to[i], 16 * i:16 * i + 16] for i in range(N // 16)]
            for i in range(N // 16):
                x = slots[slot, part, 16 * i:16 * i + 16]
                acc[part, to[i], 16 * i:16 * i + 16] = old[i] + jnp.where(cm, x, jnp.zeros_like(x))
            rb = pl.multiple_of((yy >> 4) * 16, 16)
            x = slots[slot, part, pl.ds(rb, 16)]
            here = rows >= jnp.where((yy & 15) != 0, yy - rb, N)
            acc[part, k, pl.ds(rb, 16)] += jnp.where(cm & here, x, jnp.zeros_like(x))
            acc[part, k2, pl.ds(rb, 16)] += jnp.where(cm & (rows < yy - rb), x, jnp.zeros_like(x))
        cp = pltpu.make_async_copy(acc.at[part, 0:blocks], out.at[part], sem.at[part])
        cp.start()
        copies.append(cp)
    for cp in copies:
        cp.wait()


def local(object_field, probe, prop_phase, measured, positions):
    chips = lax.axis_size("pos")
    height = object_field.shape[2]
    blocks = height // N
    tb, tbt = tables()
    pos_t = positions.T
    any_ = pl.BlockSpec(memory_space=pl.ANY)
    V = pltpu.VMEM
    win = V((2, N, N), BF)
    dma = pltpu.SemaphoreType.DMA
    slots = pl.pallas_call(
        functools.partial(main_kernel, chips, height),
        out_shape=jax.ShapeDtypeStruct((4, 2, N, N), BF),
        in_specs=[pl.BlockSpec(memory_space=pltpu.HBM)] * 7,
        out_specs=any_,
        scratch_shapes=[
            pltpu.SMEM((2, 2 * chips), jnp.int32), V((2, blocks, N, N), BF), win, win, win, V((2, 2, N, N), BF), V((2, 2, N, N), BF),
            V((2, 2, N, N), F32), V((4, 2, N, N), BF), V((N, N), F32), V((2, N, N), BF), V((N, N), F32),
            V((512, N), BF), V((N, 512), BF), V((4, 2, N, N), BF), V((4, 2, N, N), F32),
            V((2, N, N), F32), V((N, N), F32), V((WIDTH, 2, N, N), BF), V((WIDTH, 2, N, N), BF),
            V((4, 2, N, N), F32), V((4, 2, N, N), F32), V((2, N, 128), F32), V((4, 2, N, N), BF),
            V((2, 4, 4, 64, N), BF), V((2, 4, 4, 64, N), BF), V((2, 2, N, N), BF),
            dma((7,)), dma((2,)), dma((2,)), dma, dma, dma, dma,
            dma((2,)), dma((4,)), dma((8,)), dma((2, 8)), dma((4,)), dma((2, 4)), dma,
        ],
        compiler_params=pltpu.CompilerParams(
            collective_id=0, has_side_effects=True, vmem_limit_bytes=48 * 1024 * 1024),
        name="ptycho",
    )(*(pltpu.with_memory_space_constraint(a, pltpu.HBM) for a in (
        pos_t, object_field.reshape(2, blocks, N, N), probe, prop_phase, measured, tb, tbt)))
    band = pl.pallas_call(
        functools.partial(final_kernel, chips, blocks),
        out_shape=jax.ShapeDtypeStruct((2, blocks, N, N), BF),
        in_specs=[any_, pl.BlockSpec(memory_space=pltpu.VMEM)],
        out_specs=pl.BlockSpec(memory_space=pltpu.HBM),
        scratch_shapes=[pltpu.SMEM((2, 2 * chips), jnp.int32), V((2, blocks + 1, N, N), BF), dma((2,)), dma],
        compiler_params=pltpu.CompilerParams(vmem_limit_bytes=32 * 1024 * 1024),
        name="assemble",
    )(pos_t, slots)
    return band.reshape(1, 2, height, N)


def solution(mesh):
    placed = (PS("depth", None, None, "pos"), PS(), PS(), PS("pos", None, None), PS())
    return jax.shard_map(
        local, mesh=mesh, in_specs=placed, out_specs=PS("depth", None, None, "pos"), check_vma=False
    )
```

```python
import functools
import math
import numpy as np
import jax, jax.numpy as jnp
from jax import lax
from jax.experimental import pallas as pl
from jax.experimental.pallas import tpu as pltpu
from jax.sharding import PartitionSpec as PS
BF=jnp.bfloat16; F32=jnp.float32
N=256; HF=128
MODES=4
WIDTH=4

def tables():
    k=np.arange(N); ph=(k[:,None]*k[None,:])%N
    ang=ph*(2*math.pi/N)
    fr=np.cos(ang)/16.0; fi=-np.sin(ang)/16.0
    tb=np.concatenate([fr[0::2],fi[0::2],fr[1::2],fi[1::2]],0)
    return jnp.asarray(tb,dtype=BF), jnp.asarray(tb.T,dtype=BF)

def dot(a,b): return jnp.dot(a,b,preferred_element_type=F32)
def iota(shape,d): return lax.broadcasted_iota(jnp.int32,shape,d)

def prep_tables(tb,tbt,tab,y,c):
    for r,f1,f2 in ((y,0,1),(c,3,2)):
        onehot=(iota((N,HF),0)==((iota((N,HF),1)-r)&255)).astype(F32).astype(BF)
        m1=dot(tb[...],onehot).astype(BF)
        onet=(iota((HF,N),1)==((iota((HF,N),0)-r)&255)).astype(F32).astype(BF)
        m2=dot(onet,tbt[...]).astype(BF)
        for par in range(2):
            a=m1[par*256:par*256+128]; b=m1[par*256+128:par*256+256]
            tab[f1,par,0:128,0:128]=a; tab[f1,par,0:128,128:256]=-b
            tab[f1,par,128:256,0:128]=b; tab[f1,par,128:256,128:256]=a
            a=m2[:,par*256:par*256+128]; b=m2[:,par*256+128:par*256+256]
            tab[f2,par,0:128,0:128]=a; tab[f2,par,0:128,128:256]=b
            tab[f2,par,128:256,0:128]=-b; tab[f2,par,128:256,128:256]=a

def prep_probe(probe,pr,tmp,y,c):
    ryt=(iota((N,N),1)==((iota((N,N),0)-y)&255)).astype(F32).astype(BF)
    rc=(iota((N,N),0)==((iota((N,N),1)-c)&255)).astype(F32).astype(BF)
    for m in range(4):
        for q in range(2):
            t=dot(ryt,probe[m,q]).astype(BF)
            pr[m,q]=dot(t,rc)

def perms():
    i0=iota((N,N),0); i1=iota((N,N),1)
    pt=(i1==(2*(i0&127)+(i0>>7))).astype(F32).astype(BF)
    p=(i0==(2*(i1&127)+(i1>>7))).astype(F32).astype(BF)
    return pt,p

def prep_k(phase,kk):
    pt,p=perms()
    x=phase[...]
    acc=None
    for _ in range(3):
        h=x.astype(BF)
        x=x-h.astype(F32)
        t=dot(dot(pt,h).astype(BF),p)
        acc=t if acc is None else acc+t
    kk[0]=jnp.cos(acc); kk[1]=jnp.sin(acc)

def prep_meas(meas,mp):
    pt,p=perms()
    mp[...]=dot(dot(pt,meas[...]).astype(BF),p)

RC=32
def dots1f(tab,P): return [dot(tab[0,par],P[par]) for par in range(2)]
def post1f(VV,L):
    for q in range(2):
        for r in range(0,128,RC):
            for par in range(2):
                V=VV[par][q*128+r:q*128+r+RC]
                lo=V[:,:128]; hi=V[:,128:]
                L[0,par*128+r:par*128+r+RC,q*128:q*128+128]=(lo+hi).astype(BF)
                L[1,par*128+r:par*128+r+RC,q*128:q*128+128]=(lo-hi).astype(BF)

def dots2f(tab,L): return [dot(L[cp],tab[2,cp]) for cp in range(2)]
def dots1i(tab,P): return [dot(tab[1,par],P[par]) for par in range(2)]
def post1i(E,L):
    for q in range(2):
        for r in range(0,128,RC):
            for cp in range(2):
                rr=slice(q*128+r,q*128+r+RC)
                a=E[0][rr,cp*128:cp*128+128]; b=E[1][rr,cp*128:cp*128+128]
                L[cp,r:r+RC,q*128:q*128+128]=(a+b).astype(BF)
                L[cp,128+r:128+r+RC,q*128:q*128+128]=(a-b).astype(BF)

def dots2i(tab,L): return [dot(L[cp],tab[3,cp]) for cp in range(2)]

def space(D,r,n,q,uc):
    a=D[0][r:r+n,q*128:q*128+128]; b=D[1][r:r+n,q*128:q*128+128]
    return a+b if uc==0 else a-b

def put2(P,q,r,sl,x0,x1):
    P[0,q*128+r:q*128+r+RC,sl]=(x0+x1).astype(BF)
    P[1,q*128+r:q*128+r+RC,sl]=(x0-x1).astype(BF)

def putf(P,q,r,sl,x):
    P[r//128,q*128+r%128:q*128+r%128+RC,sl]=x.astype(BF)

def halves(r): return (slice(r,r+RC),slice(128+r,128+r+RC))
def lanes(k): return slice(k*128,k*128+128)

def phase_a(m,tab,pr,o0,kk,P,L,psi1):
    for r in range(0,128,RC):
        for uc in range(2):
            sl=lanes(uc); xr=[];xi=[]
            for h in halves(r):
                a=pr[m,0,h,sl].astype(F32); b=pr[m,1,h,sl].astype(F32)
                c=o0[0,h,sl].astype(F32); d=o0[1,h,sl].astype(F32)
                xr.append(a*c-b*d); xi.append(a*d+b*c)
            put2(P,0,r,sl,*xr); put2(P,1,r,sl,*xi)
    V=dots1f(tab,P); yield
    post1f(V,L); SS=dots2f(tab,L); yield
    for r in range(0,256,RC):
        for cp in range(2):
            S=SS[cp][r:r+RC]; sl=lanes(cp)
            kr=kk[0,r:r+RC,sl]; ki=kk[1,r:r+RC,sl]
            putf(P,0,r,sl,S[:,:128]*kr-S[:,128:]*ki)
            putf(P,1,r,sl,S[:,:128]*ki+S[:,128:]*kr)
    E=dots1i(tab,P); yield
    post1i(E,L); D=dots2i(tab,L); yield
    for r in range(0,256,RC):
        for uc in range(2):
            for q in range(2): psi1[m,q,r:r+RC,lanes(uc)]=space(D,r,RC,q,uc)

def phase_b(m,tab,o1,P,L,psi1,far,inten):
    for r in range(0,128,RC):
        for uc in range(2):
            sl=lanes(uc); xr=[];xi=[]
            for h in halves(r):
                a=psi1[m,0,h,sl]; b=psi1[m,1,h,sl]
                c=o1[0,h,sl].astype(F32); d=o1[1,h,sl].astype(F32)
                xr.append(a*c-b*d); xi.append(a*d+b*c)
            put2(P,0,r,sl,*xr); put2(P,1,r,sl,*xi)
    V=dots1f(tab,P); yield
    post1f(V,L); SS=dots2f(tab,L); yield
    for r in range(0,256,RC):
        for cp in range(2):
            S=SS[cp][r:r+RC]
            far[m,cp,r:r+RC]=S
            inten[cp,r:r+RC]+=S[:,:128]*S[:,:128]+S[:,128:]*S[:,128:]

def phase_c(m,tab,P,L3,far,inten):
    for r in range(0,256,RC):
        for cp in range(2):
            w=inten[cp,r:r+RC]
            putf(P,0,r,lanes(cp),w*far[m,cp,r:r+RC,:128]); putf(P,1,r,lanes(cp),w*far[m,cp,r:r+RC,128:])
    E0,E1=dots1i(tab,P); yield
    for q in range(2):
        for r in range(4):
            for cp in range(2):
                rr=slice(q*128+r*32,q*128+r*32+32); sl=lanes(cp); to=lanes(q)
                L3[cp,r,m,0:32,to]=(E0[rr,sl]+E1[rr,sl]).astype(BF)
                L3[cp,r,m,32:64,to]=(E0[rr,sl]-E1[rr,sl]).astype(BF)

def phase_c2(r,tab,o1,L3,psi1,gs,adj):
    D=[dot(L3[cp,r].reshape(256,256),tab[3,cp]) for cp in range(2)]; yield
    for uc in range(2):
        sl=lanes(uc); gr=[None,None]; gi=[None,None]
        hs=(slice(r*32,r*32+32),slice(128+r*32,160+r*32))
        for m in range(4):
            ar=[];ai=[]
            for k,h in enumerate(hs):
                br=space(D,m*64+32*k,32,0,uc); bi=space(D,m*64+32*k,32,1,uc)
                a=psi1[m,0,h,sl]; b=psi1[m,1,h,sl]
                tr=a*br+b*bi; ti=a*bi-b*br
                gr[k]=tr if m==0 else gr[k]+tr; gi[k]=ti if m==0 else gi[k]+ti
                c=o1[0,h,sl]; d=o1[1,h,sl]
                ar.append(c*br+d*bi); ai.append(c*bi-d*br)
            put2(adj.at[m],0,r*32,sl,*ar); put2(adj.at[m],1,r*32,sl,*ai)
        for k,h in enumerate(hs):
            gs[0,h,sl]=gr[k].astype(BF); gs[1,h,sl]=gi[k].astype(BF)

def phase_d(m,tab,kk,P,L,L2,adj):
    V=dots1f(tab,adj.at[m]); yield
    post1f(V,L); SS=dots2f(tab,L); yield
    for r in range(0,256,RC):
        for cp in range(2):
            S=SS[cp][r:r+RC].astype(BF).astype(F32); sl=lanes(cp)
            kr=kk[0,r:r+RC,sl]; ki=kk[1,r:r+RC,sl]
            putf(P,0,r,sl,kr*S[:,:128]+ki*S[:,128:])
            putf(P,1,r,sl,kr*S[:,128:]-ki*S[:,:128])
    E0,E1=dots1i(tab,P); yield
    for q in range(2):
        for r in range(0,128,RC):
            for cp in range(2):
                rr=slice(q*128+r,q*128+r+RC); sl=lanes(cp); to=lanes(q); h=r//64; k=r%64
                L2[cp,h,m,k:k+RC,to]=(E0[rr,sl]+E1[rr,sl]).astype(BF)
                L2[cp,2+h,m,k:k+RC,to]=(E0[rr,sl]-E1[rr,sl]).astype(BF)

def phase_e(r,tab,pr,L2,gs):
    D=(dot(L2[0,r].reshape(256,256),tab[3,0]), dot(L2[1,r].reshape(256,256),tab[3,1])); yield
    for k in range(0,64,RC):
        rows=slice(r*64+k,r*64+k+RC)
        for uc in range(2):
            sl=lanes(uc)
            gr=None
            for m in range(4):
                wr=space(D,m*64+k,RC,0,uc); wi=space(D,m*64+k,RC,1,uc)
                a=pr[m,0,rows,sl].astype(F32); b=pr[m,1,rows,sl].astype(F32)
                tr=a*wr+b*wi; ti=a*wi-b*wr
                gr,gi=(tr,ti) if gr is None else (gr+tr,gi+ti)
            gs[0,rows,sl]=gr.astype(BF); gs[1,rows,sl]=gi.astype(BF)


def weave(items,width=2):
    todo=list(items); live=[]
    while todo or live:
        if todo and len(live)<width:
            item=todo.pop(0)
            if item[0] is not None: item[0]()
        else:
            item=live.pop(0)
        try:
            next(item[1])
            live.append(item)
        except StopIteration:
            if item[2] is not None: item[2]()


MESH = pl.DeviceIdType.MESH


def main_kernel(chips, height, pos_h, obj, probe_h, phase_h, meas_h, tb_h, tbt_h, out,
                pos, band, w_left, w_right, w_part, near, farw, ob, probe, phase, meas, mtmp,
                tb, tbt, tab, pr, kk, mp, P, L, psi1, far, inten, adj, L2, L3, gs,
                in_sem, obj_send, obj_recv, near_send, near_recv, m_send, m_recv,
                g_send, g_recv, h_send, h_recv, c_send, c_recv, loc_sem):
    d = lax.axis_index("depth")
    p = lax.axis_index("pos")
    left = lax.rem(p + chips - 1, chips)
    right = lax.rem(p + 1, chips)
    nb = lax.rem(p + 1 - 2 * d + chips, chips)
    total = 2 * chips
    mine = lax.rem(2 * p - d + total, total)
    other = lax.rem(2 * p + d - 1 + total, total)
    q_left = lax.rem(2 * p - 2 + total, total)
    q_right = 2 * p + 1

    barrier = pltpu.get_barrier_semaphore()
    peers = ((1 - d, p), (0, left), (1, right), (d, nb))
    for peer in peers:
        pl.semaphore_signal(barrier, inc=1, device_id=peer, device_id_type=MESH)

    loads = [
        pltpu.make_async_copy(obj, band, in_sem.at[0]),
        pltpu.make_async_copy(meas_h.at[d], mtmp, in_sem.at[1]),
        pltpu.make_async_copy(tb_h, tb, in_sem.at[2]),
        pltpu.make_async_copy(tbt_h, tbt, in_sem.at[3]),
        pltpu.make_async_copy(probe_h, probe, in_sem.at[4]),
        pltpu.make_async_copy(phase_h, phase, in_sem.at[5]),
        pltpu.make_async_copy(pos_h, pos, in_sem.at[6]),
    ]
    for cp in loads:
        cp.start()

    blocks = height // N
    row_id = iota((N, N), 0)

    def window(q, part):
        y = pos[0, q]
        k = y >> 8
        k2 = jnp.minimum(k + 1, blocks - 1)
        a = band[part, k]
        b = band[part, k2]
        return jnp.where(row_id >= (y & 255), a.astype(F32), b.astype(F32)).astype(BF)

    loads[6].wait()
    loads[0].wait()
    for part in range(2):
        w_left[part] = window(q_left, part)
    for part in range(2):
        w_right[part] = window(q_right, part)
    for part in range(2):
        w_part[part] = window(other, part)
    y = pos[0, mine] & 255
    c = pos[1, mine] & 255
    pl.semaphore_wait(barrier, 4)

    def remote(src, dst, ss, rs, dev):
        return pltpu.make_async_remote_copy(src_ref=src, dst_ref=dst, send_sem=ss, recv_sem=rs,
                                            device_id=dev, device_id_type=MESH)

    c_left = remote(w_left, farw.at[d], obj_send.at[0], obj_recv.at[d], (0, left))
    c_right = remote(w_right, farw.at[d], obj_send.at[1], obj_recv.at[d], (1, right))
    c_part = remote(w_part, near.at[d], near_send, near_recv, (1 - d, p))
    go_left = p > 0
    wrap_a = jnp.logical_and(d == 0, p == chips - 1)

    def send_object():
        @pl.when(go_left)
        def _():
            c_left.start()

        c_right.start()

    def sent_object():
        @pl.when(go_left)
        def _():
            c_left.wait_send()

        c_right.wait_send()

    @pl.when(d == 0)
    def _():
        send_object()

    c_part.start()
    loads[1].wait()
    c_meas = remote(meas.at[0], meas.at[1], m_send, m_recv, (1, right))
    meas[0] = mtmp[...].astype(BF)
    loads[2].wait()
    loads[3].wait()
    prep_tables(tb, tbt, tab, y, c)
    loads[4].wait()
    prep_probe(probe, pr, None, y, c)
    loads[5].wait()
    prep_k(phase, kk)
    for part in range(2):
        near[d, part] = window(mine, part)
    inten[...] = jnp.zeros_like(inten)

    @pl.when(d == 1)
    def _():
        send_object()
        c_meas.start()


    near_mask = (iota((N, N), 1) - c) * (1 - 2 * d) - d >= 0

    def merge(s):
        for part in range(2):
            ob[s, part] = jnp.where(near_mask, near[s, part].astype(F32),
                                    farw[s, part].astype(F32))

    def bufs(m):
        return P.at[m % WIDTH], L.at[m % WIDTH]

    def run(gens):
        weave([(None, x, None) for x in gens], WIDTH)

    @pl.when(d == 0)
    def _():
        prep_meas(meas.at[0], mp)

    c_part.wait_recv()

    def got_far(k):
        @pl.when(jnp.logical_not(wrap_a))
        def _():
            remote(w_left, farw.at[k], obj_send.at[0], obj_recv.at[k], (0, left)).wait_recv()

    got_far(0)
    merge(0)
    run([phase_a(m, tab, pr, ob.at[0], kk, *bufs(m), psi1) for m in range(MODES)])
    got_far(1)
    merge(1)
    run([phase_b(m, tab, ob.at[1], *bufs(m), psi1, far, inten) for m in range(MODES)])

    @pl.when(d == 1)
    def _():
        c_meas.wait()
        prep_meas(meas.at[1], mp)

    for cp in range(2):
        inten[cp] = (inten[cp] - mp[:, cp * 128:cp * 128 + 128]) * 0.125
    run([phase_c(m, tab, P.at[m], L3, far, inten) for m in range(MODES)])

    def strip(slot, i, dev):
        rows = pl.ds(i * 32, 32)
        return remote(gs.at[1, :, rows, :], out.at[2 + slot, :, rows, :], h_send.at[i], h_recv.at[slot, i], dev)

    def ship1(r):
        @pl.when(jnp.logical_not(wrap_a))
        def _():
            strip(d, r, (1, nb)).start()
            strip(d, r + 4, (1, nb)).start()

    weave([(None, phase_c2(r, tab, ob.at[1], L3, psi1, gs.at[1], adj), functools.partial(ship1, r))
           for r in range(4)], 2)

    near1 = remote(gs.at[1], out.at[d], g_send.at[1], g_recv.at[d], (1, p))
    stay1 = pltpu.make_async_copy(gs.at[1], out.at[d], loc_sem)

    @pl.when(d == 0)
    def _():
        near1.start()

    @pl.when(d == 1)
    def _():
        stay1.start()

    run([phase_d(m, tab, kk, *bufs(m), L2, adj) for m in range(MODES)])

    def chunk(r, dev):
        rows = pl.ds(r * 64, 64)
        return remote(gs.at[0, :, rows, :], out.at[2 + d, :, rows, :], c_send.at[r], c_recv.at[d, r], dev)

    def incoming(slot, r):
        rows = pl.ds(r * 64, 64)
        return remote(gs.at[0, :, rows, :], out.at[2 + slot, :, rows, :], c_send.at[r], c_recv.at[slot, r],
                      (0, nb))

    def ship(r):
        @pl.when(jnp.logical_not(wrap_a))
        def _():
            chunk(r, (0, nb)).start()

    weave([(None, phase_e(r, tab, pr, L2, gs.at[0]), functools.partial(ship, r)) for r in range(4)], 2)
    near0 = remote(gs.at[0], out.at[d], g_send.at[1], g_recv.at[d], (0, p))
    stay0 = pltpu.make_async_copy(gs.at[0], out.at[d], loc_sem)

    @pl.when(d == 1)
    def _():
        near0.start()
        stay1.wait()

    @pl.when(d == 0)
    def _():
        stay0.start()
        near1.wait_send()

    sent_object()
    c_part.wait_send()

    @pl.when(jnp.logical_not(wrap_a))
    def _():
        for i in range(8):
            strip(d, i, (1, nb)).wait_send()
        for r in range(4):
            chunk(r, (0, nb)).wait_send()

    @pl.when(d == 1)
    def _():
        near0.wait_send()
        remote(gs.at[1], out.at[0], g_send.at[1], g_recv.at[0], (0, p)).wait_recv()
        for i in range(8):
            strip(1, i, (1, nb)).wait_recv()

        @pl.when(p > 0)
        def _():
            for i in range(8):
                strip(0, i, (1, nb)).wait_recv()

    @pl.when(d == 0)
    def _():
        stay0.wait()
        remote(gs.at[0], out.at[1], g_send.at[1], g_recv.at[1], (0, p)).wait_recv()
        for r in range(4):
            incoming(1, r).wait_recv()

        @pl.when(p > 0)
        def _():
            for r in range(4):
                incoming(0, r).wait_recv()


def final_kernel(chips, blocks, pos_h, slots, out, pos, acc, sem, pos_sem):
    load = pltpu.make_async_copy(pos_h, pos, pos_sem)
    load.start()
    p = lax.axis_index("pos")
    total = 2 * chips
    acc[...] = jnp.zeros_like(acc)
    load.wait()
    rows = iota((16, N), 0)
    cols = iota((16, N), 1)
    places = []
    for off, ge in ((0, True), (total - 1, False), (total - 2, False), (1, True)):
        q = lax.rem(2 * p + off, total)
        y = pos[0, q]
        c = pos[1, q] & 255
        k = y >> 8
        places.append((k, jnp.minimum(k + 1, blocks - 1), y & 255, (cols >= c) if ge else (cols < c)))
    copies = []
    for part in range(2):
        for slot, (k, k2, yy, cm) in enumerate(places):
            to = [jnp.where(r0 + 15 < yy, k2, jnp.where(r0 >= yy, k, blocks)) for r0 in range(0, N, 16)]
            old = [acc[part, to[i], 16 * i:16 * i + 16] for i in range(N // 16)]
            for i in range(N // 16):
                x = slots[slot, part, 16 * i:16 * i + 16]
                acc[part, to[i], 16 * i:16 * i + 16] = old[i] + jnp.where(cm, x, jnp.zeros_like(x))
            rb = pl.multiple_of((yy >> 4) * 16, 16)
            x = slots[slot, part, pl.ds(rb, 16)]
            here = rows >= jnp.where((yy & 15) != 0, yy - rb, N)
            acc[part, k, pl.ds(rb, 16)] += jnp.where(cm & here, x, jnp.zeros_like(x))
            acc[part, k2, pl.ds(rb, 16)] += jnp.where(cm & (rows < yy - rb), x, jnp.zeros_like(x))
        for i in range(0, blocks, 2):
            cp = pltpu.make_async_copy(acc.at[part, i:i + 2], out.at[part, i:i + 2], sem.at[part, i // 2])
            cp.start()
            copies.append(cp)
    for cp in copies:
        cp.wait()


def local(object_field, probe, prop_phase, measured, positions):
    chips = lax.axis_size("pos")
    height = object_field.shape[2]
    blocks = height // N
    tb, tbt = tables()
    pos_t = positions.T
    any_ = pl.BlockSpec(memory_space=pl.ANY)
    V = pltpu.VMEM
    win = V((2, N, N), BF)
    dma = pltpu.SemaphoreType.DMA
    slots = pl.pallas_call(
        functools.partial(main_kernel, chips, height),
        out_shape=jax.ShapeDtypeStruct((4, 2, N, N), BF),
        in_specs=[pl.BlockSpec(memory_space=pltpu.HBM)] * 7,
        out_specs=any_,
        scratch_shapes=[
            pltpu.SMEM((2, 2 * chips), jnp.int32), V((2, blocks, N, N), BF), win, win, win, V((2, 2, N, N), BF), V((2, 2, N, N), BF),
            V((2, 2, N, N), F32), V((4, 2, N, N), BF), V((N, N), F32), V((2, N, N), BF), V((N, N), F32),
            V((512, N), BF), V((N, 512), BF), V((4, 2, N, N), BF), V((4, 2, N, N), F32),
            V((2, N, N), F32), V((N, N), F32), V((WIDTH, 2, N, N), BF), V((WIDTH, 2, N, N), BF),
            V((4, 2, N, N), F32), V((4, 2, N, N), F32), V((2, N, 128), F32), V((4, 2, N, N), BF),
            V((2, 4, 4, 64, N), BF), V((2, 4, 4, 64, N), BF), V((2, 2, N, N), BF),
            dma((7,)), dma((2,)), dma((2,)), dma, dma, dma, dma,
            dma((2,)), dma((4,)), dma((8,)), dma((2, 8)), dma((4,)), dma((2, 4)), dma,
        ],
        compiler_params=pltpu.CompilerParams(
            collective_id=0, has_side_effects=True, vmem_limit_bytes=48 * 1024 * 1024),
        name="ptycho",
    )(*(pltpu.with_memory_space_constraint(a, pltpu.HBM) for a in (
        pos_t, object_field.reshape(2, blocks, N, N), probe, prop_phase, measured, tb, tbt)))
    band = pl.pallas_call(
        functools.partial(final_kernel, chips, blocks),
        out_shape=jax.ShapeDtypeStruct((2, blocks, N, N), BF),
        in_specs=[any_, pl.BlockSpec(memory_space=pltpu.VMEM)],
        out_specs=pl.BlockSpec(memory_space=pltpu.HBM),
        scratch_shapes=[pltpu.SMEM((2, 2 * chips), jnp.int32), V((2, blocks + 1, N, N), BF), dma((2, blocks // 2)), dma],
        compiler_params=pltpu.CompilerParams(vmem_limit_bytes=32 * 1024 * 1024),
        name="assemble",
    )(pos_t, slots)
    return band.reshape(1, 2, height, N)


def solution(mesh):
    placed = (PS("depth", None, None, "pos"), PS(), PS(), PS("pos", None, None), PS())
    return jax.shard_map(
        local, mesh=mesh, in_specs=placed, out_specs=PS("depth", None, None, "pos"), check_vma=False
    )
```

```python
import functools
import math
import numpy as np
import jax, jax.numpy as jnp
from jax import lax
from jax.experimental import pallas as pl
from jax.experimental.pallas import tpu as pltpu
from jax.sharding import PartitionSpec as PS
BF=jnp.bfloat16; F32=jnp.float32
N=256; HF=128
MODES=4
WIDTH=4

def tables():
    k=np.arange(N); ph=(k[:,None]*k[None,:])%N
    ang=ph*(2*math.pi/N)
    fr=np.cos(ang)/16.0; fi=-np.sin(ang)/16.0
    tb=np.concatenate([fr[0::2],fi[0::2],fr[1::2],fi[1::2]],0)
    return jnp.asarray(tb,dtype=BF), jnp.asarray(tb.T,dtype=BF)

def dot(a,b): return jnp.dot(a,b,preferred_element_type=F32)
def iota(shape,d): return lax.broadcasted_iota(jnp.int32,shape,d)

def prep_tables(tb,tbt,tab,y,c):
    for r,f1,f2 in ((y,0,1),(c,3,2)):
        onehot=(iota((N,HF),0)==((iota((N,HF),1)-r)&255)).astype(F32).astype(BF)
        m1=dot(tb[...],onehot).astype(BF)
        onet=(iota((HF,N),1)==((iota((HF,N),0)-r)&255)).astype(F32).astype(BF)
        m2=dot(onet,tbt[...]).astype(BF)
        for par in range(2):
            a=m1[par*256:par*256+128]; b=m1[par*256+128:par*256+256]
            tab[f1,par,0:128,0:128]=a; tab[f1,par,0:128,128:256]=-b
            tab[f1,par,128:256,0:128]=b; tab[f1,par,128:256,128:256]=a
            a=m2[:,par*256:par*256+128]; b=m2[:,par*256+128:par*256+256]
            tab[f2,par,0:128,0:128]=a; tab[f2,par,0:128,128:256]=b
            tab[f2,par,128:256,0:128]=-b; tab[f2,par,128:256,128:256]=a

def prep_probe(probe,pr,tmp,y,c):
    ryt=(iota((N,N),1)==((iota((N,N),0)-y)&255)).astype(F32).astype(BF)
    rc=(iota((N,N),0)==((iota((N,N),1)-c)&255)).astype(F32).astype(BF)
    for m in range(4):
        for q in range(2):
            t=dot(ryt,probe[m,q]).astype(BF)
            pr[m,q]=dot(t,rc)

def perms():
    i0=iota((N,N),0); i1=iota((N,N),1)
    pt=(i1==(2*(i0&127)+(i0>>7))).astype(F32).astype(BF)
    p=(i0==(2*(i1&127)+(i1>>7))).astype(F32).astype(BF)
    return pt,p

def prep_k(phase,kk):
    pt,p=perms()
    x=phase[...]
    acc=None
    for _ in range(3):
        h=x.astype(BF)
        x=x-h.astype(F32)
        t=dot(dot(pt,h).astype(BF),p)
        acc=t if acc is None else acc+t
    kk[0]=jnp.cos(acc); kk[1]=jnp.sin(acc)

def prep_meas(meas,mp):
    pt,p=perms()
    mp[...]=dot(dot(pt,meas[...]).astype(BF),p)

RC=32
def dots1f(tab,P): return [dot(tab[0,par],P[par]) for par in range(2)]
def post1f(VV,L):
    for q in range(2):
        for r in range(0,128,RC):
            for par in range(2):
                V=VV[par][q*128+r:q*128+r+RC]
                lo=V[:,:128]; hi=V[:,128:]
                L[0,par*128+r:par*128+r+RC,q*128:q*128+128]=(lo+hi).astype(BF)
                L[1,par*128+r:par*128+r+RC,q*128:q*128+128]=(lo-hi).astype(BF)

def dots2f(tab,L): return [dot(L[cp],tab[2,cp]) for cp in range(2)]
def dots1i(tab,P): return [dot(tab[1,par],P[par]) for par in range(2)]
def post1i(E,L):
    for q in range(2):
        for r in range(0,128,RC):
            for cp in range(2):
                rr=slice(q*128+r,q*128+r+RC)
                a=E[0][rr,cp*128:cp*128+128]; b=E[1][rr,cp*128:cp*128+128]
                L[cp,r:r+RC,q*128:q*128+128]=(a+b).astype(BF)
                L[cp,128+r:128+r+RC,q*128:q*128+128]=(a-b).astype(BF)

def dots2i(tab,L): return [dot(L[cp],tab[3,cp]) for cp in range(2)]

def space(D,r,n,q,uc):
    a=D[0][r:r+n,q*128:q*128+128]; b=D[1][r:r+n,q*128:q*128+128]
    return a+b if uc==0 else a-b

def put2(P,q,r,sl,x0,x1):
    P[0,q*128+r:q*128+r+RC,sl]=(x0+x1).astype(BF)
    P[1,q*128+r:q*128+r+RC,sl]=(x0-x1).astype(BF)

def putf(P,q,r,sl,x):
    P[r//128,q*128+r%128:q*128+r%128+RC,sl]=x.astype(BF)

def halves(r): return (slice(r,r+RC),slice(128+r,128+r+RC))
def lanes(k): return slice(k*128,k*128+128)

def phase_a(m,tab,pr,o0,kk,P,L,psi1):
    for r in range(0,128,RC):
        for uc in range(2):
            sl=lanes(uc); xr=[];xi=[]
            for h in halves(r):
                a=pr[m,0,h,sl].astype(F32); b=pr[m,1,h,sl].astype(F32)
                c=o0[0,h,sl].astype(F32); d=o0[1,h,sl].astype(F32)
                xr.append(a*c-b*d); xi.append(a*d+b*c)
            put2(P,0,r,sl,*xr); put2(P,1,r,sl,*xi)
    V=dots1f(tab,P); yield
    post1f(V,L); SS=dots2f(tab,L); yield
    for r in range(0,256,RC):
        for cp in range(2):
            S=SS[cp][r:r+RC]; sl=lanes(cp)
            kr=kk[0,r:r+RC,sl]; ki=kk[1,r:r+RC,sl]
            putf(P,0,r,sl,S[:,:128]*kr-S[:,128:]*ki)
            putf(P,1,r,sl,S[:,:128]*ki+S[:,128:]*kr)
    E=dots1i(tab,P); yield
    post1i(E,L); D=dots2i(tab,L); yield
    for r in range(0,256,RC):
        for uc in range(2):
            for q in range(2): psi1[m,q,r:r+RC,lanes(uc)]=space(D,r,RC,q,uc)

def phase_b(m,tab,o1,P,L,psi1,far,inten):
    for r in range(0,128,RC):
        for uc in range(2):
            sl=lanes(uc); xr=[];xi=[]
            for h in halves(r):
                a=psi1[m,0,h,sl]; b=psi1[m,1,h,sl]
                c=o1[0,h,sl].astype(F32); d=o1[1,h,sl].astype(F32)
                xr.append(a*c-b*d); xi.append(a*d+b*c)
            put2(P,0,r,sl,*xr); put2(P,1,r,sl,*xi)
    V=dots1f(tab,P); yield
    post1f(V,L); SS=dots2f(tab,L); yield
    for r in range(0,256,RC):
        for cp in range(2):
            S=SS[cp][r:r+RC]
            far[m,cp,r:r+RC]=S
            inten[cp,r:r+RC]+=S[:,:128]*S[:,:128]+S[:,128:]*S[:,128:]

def phase_c(m,tab,P,L3,far,inten):
    for r in range(0,256,RC):
        for cp in range(2):
            w=inten[cp,r:r+RC]
            putf(P,0,r,lanes(cp),w*far[m,cp,r:r+RC,:128]); putf(P,1,r,lanes(cp),w*far[m,cp,r:r+RC,128:])
    E0,E1=dots1i(tab,P); yield
    for q in range(2):
        for r in range(4):
            for cp in range(2):
                rr=slice(q*128+r*32,q*128+r*32+32); sl=lanes(cp); to=lanes(q)
                L3[cp,r,m,0:32,to]=(E0[rr,sl]+E1[rr,sl]).astype(BF)
                L3[cp,r,m,32:64,to]=(E0[rr,sl]-E1[rr,sl]).astype(BF)

def phase_c2(r,tab,o1,L3,psi1,gs,adj):
    D=[dot(L3[cp,r].reshape(256,256),tab[3,cp]) for cp in range(2)]; yield
    for uc in range(2):
        sl=lanes(uc); gr=[None,None]; gi=[None,None]
        hs=(slice(r*32,r*32+32),slice(128+r*32,160+r*32))
        for m in range(4):
            ar=[];ai=[]
            for k,h in enumerate(hs):
                br=space(D,m*64+32*k,32,0,uc); bi=space(D,m*64+32*k,32,1,uc)
                a=psi1[m,0,h,sl]; b=psi1[m,1,h,sl]
                tr=a*br+b*bi; ti=a*bi-b*br
                gr[k]=tr if m==0 else gr[k]+tr; gi[k]=ti if m==0 else gi[k]+ti
                c=o1[0,h,sl]; d=o1[1,h,sl]
                ar.append(c*br+d*bi); ai.append(c*bi-d*br)
            put2(adj.at[m],0,r*32,sl,*ar); put2(adj.at[m],1,r*32,sl,*ai)
        for k,h in enumerate(hs):
            gs[0,h,sl]=gr[k].astype(BF); gs[1,h,sl]=gi[k].astype(BF)

def phase_d(m,tab,kk,P,L,L2,adj):
    V=dots1f(tab,adj.at[m]); yield
    post1f(V,L); SS=dots2f(tab,L); yield
    for r in range(0,256,RC):
        for cp in range(2):
            S=SS[cp][r:r+RC].astype(BF).astype(F32); sl=lanes(cp)
            kr=kk[0,r:r+RC,sl]; ki=kk[1,r:r+RC,sl]
            putf(P,0,r,sl,kr*S[:,:128]+ki*S[:,128:])
            putf(P,1,r,sl,kr*S[:,128:]-ki*S[:,:128])
    E0,E1=dots1i(tab,P); yield
    for q in range(2):
        for r in range(0,128,RC):
            for cp in range(2):
                rr=slice(q*128+r,q*128+r+RC); sl=lanes(cp); to=lanes(q); h=r//64; k=r%64
                L2[cp,h,m,k:k+RC,to]=(E0[rr,sl]+E1[rr,sl]).astype(BF)
                L2[cp,2+h,m,k:k+RC,to]=(E0[rr,sl]-E1[rr,sl]).astype(BF)

def phase_e(r,tab,pr,L2,gs):
    D=(dot(L2[0,r].reshape(256,256),tab[3,0]), dot(L2[1,r].reshape(256,256),tab[3,1])); yield
    for k in range(0,64,RC):
        rows=slice(r*64+k,r*64+k+RC)
        for uc in range(2):
            sl=lanes(uc)
            gr=None
            for m in range(4):
                wr=space(D,m*64+k,RC,0,uc); wi=space(D,m*64+k,RC,1,uc)
                a=pr[m,0,rows,sl].astype(F32); b=pr[m,1,rows,sl].astype(F32)
                tr=a*wr+b*wi; ti=a*wi-b*wr
                gr,gi=(tr,ti) if gr is None else (gr+tr,gi+ti)
            gs[0,rows,sl]=gr.astype(BF); gs[1,rows,sl]=gi.astype(BF)


def weave(items,width=2):
    todo=list(items); live=[]
    while todo or live:
        if todo and len(live)<width:
            item=todo.pop(0)
            if item[0] is not None: item[0]()
        else:
            item=live.pop(0)
        try:
            next(item[1])
            live.append(item)
        except StopIteration:
            if item[2] is not None: item[2]()


MESH = pl.DeviceIdType.MESH


def main_kernel(chips, height, pos_h, obj, probe_h, phase_h, meas_h, tb_h, tbt_h, out,
                pos, band, w_left, w_right, w_part, near, farw, ob, probe, phase, meas, mtmp,
                tb, tbt, tab, pr, kk, mp, P, L, psi1, far, inten, adj, L2, L3, gs,
                in_sem, obj_send, obj_recv, near_send, near_recv, m_send, m_recv,
                g_send, g_recv, h_send, h_recv, c_send, c_recv, loc_sem):
    d = lax.axis_index("depth")
    p = lax.axis_index("pos")
    left = lax.rem(p + chips - 1, chips)
    right = lax.rem(p + 1, chips)
    nb = lax.rem(p + 1 - 2 * d + chips, chips)
    total = 2 * chips
    mine = lax.rem(2 * p - d + total, total)
    other = lax.rem(2 * p + d - 1 + total, total)
    q_left = lax.rem(2 * p - 2 + total, total)
    q_right = 2 * p + 1

    barrier = pltpu.get_barrier_semaphore()
    peers = ((1 - d, p), (0, left), (1, right), (d, nb))
    for peer in peers:
        pl.semaphore_signal(barrier, inc=1, device_id=peer, device_id_type=MESH)

    loads = [
        pltpu.make_async_copy(obj, band, in_sem.at[0]),
        pltpu.make_async_copy(meas_h.at[d], mtmp, in_sem.at[1]),
        pltpu.make_async_copy(tb_h, tb, in_sem.at[2]),
        pltpu.make_async_copy(tbt_h, tbt, in_sem.at[3]),
        pltpu.make_async_copy(probe_h, probe, in_sem.at[4]),
        pltpu.make_async_copy(phase_h, phase, in_sem.at[5]),
        pltpu.make_async_copy(pos_h, pos, in_sem.at[6]),
    ]
    for cp in loads:
        cp.start()

    blocks = height // N
    row_id = iota((N, N), 0)

    def window(q, part):
        y = pos[0, q]
        k = y >> 8
        k2 = jnp.minimum(k + 1, blocks - 1)
        a = band[part, k]
        b = band[part, k2]
        return jnp.where(row_id >= (y & 255), a, b)

    loads[6].wait()
    loads[0].wait()
    for part in range(2):
        w_left[part] = window(q_left, part)
    for part in range(2):
        w_right[part] = window(q_right, part)
    for part in range(2):
        w_part[part] = window(other, part)
    y = pos[0, mine] & 255
    c = pos[1, mine] & 255
    pl.semaphore_wait(barrier, 4)

    def remote(src, dst, ss, rs, dev):
        return pltpu.make_async_remote_copy(src_ref=src, dst_ref=dst, send_sem=ss, recv_sem=rs,
                                            device_id=dev, device_id_type=MESH)

    c_left = remote(w_left, farw.at[d], obj_send.at[0], obj_recv.at[d], (0, left))
    c_right = remote(w_right, farw.at[d], obj_send.at[1], obj_recv.at[d], (1, right))
    c_part = remote(w_part, near.at[d], near_send, near_recv, (1 - d, p))
    go_left = p > 0
    wrap_a = jnp.logical_and(d == 0, p == chips - 1)

    def send_object():
        @pl.when(go_left)
        def _():
            c_left.start()

        c_right.start()

    def sent_object():
        @pl.when(go_left)
        def _():
            c_left.wait_send()

        c_right.wait_send()

    @pl.when(d == 0)
    def _():
        send_object()

    c_part.start()
    loads[1].wait()
    c_meas = remote(meas.at[0], meas.at[1], m_send, m_recv, (1, right))
    meas[0] = mtmp[...].astype(BF)
    loads[2].wait()
    loads[3].wait()
    prep_tables(tb, tbt, tab, y, c)
    loads[4].wait()
    prep_probe(probe, pr, None, y, c)
    loads[5].wait()
    prep_k(phase, kk)
    for part in range(2):
        near[d, part] = window(mine, part)
    inten[...] = jnp.zeros_like(inten)

    @pl.when(d == 1)
    def _():
        send_object()
        c_meas.start()


    near_mask = (iota((N, N), 1) - c) * (1 - 2 * d) - d >= 0

    def merge(s):
        for part in range(2):
            ob[s, part] = jnp.where(near_mask, near[s, part], farw[s, part]).astype(F32)

    def bufs(m):
        return P.at[m % WIDTH], L.at[m % WIDTH]

    def run(gens):
        weave([(None, x, None) for x in gens], WIDTH)

    @pl.when(d == 0)
    def _():
        prep_meas(meas.at[0], mp)

    c_part.wait_recv()

    def got_far(k):
        @pl.when(jnp.logical_not(wrap_a))
        def _():
            remote(w_left, farw.at[k], obj_send.at[0], obj_recv.at[k], (0, left)).wait_recv()

    got_far(0)
    merge(0)
    run([phase_a(m, tab, pr, ob.at[0], kk, *bufs(m), psi1) for m in range(MODES)])
    got_far(1)
    merge(1)
    run([phase_b(m, tab, ob.at[1], *bufs(m), psi1, far, inten) for m in range(MODES)])

    @pl.when(d == 1)
    def _():
        c_meas.wait()
        prep_meas(meas.at[1], mp)

    for cp in range(2):
        inten[cp] = (inten[cp] - mp[:, cp * 128:cp * 128 + 128]) * 0.125
    run([phase_c(m, tab, P.at[m], L3, far, inten) for m in range(MODES)])

    def strip(slot, i, dev):
        rows = pl.ds(i * 32, 32)
        return remote(gs.at[1, :, rows, :], out.at[2 + slot, :, rows, :], h_send.at[i], h_recv.at[slot, i], dev)

    def ship1(r):
        @pl.when(jnp.logical_not(wrap_a))
        def _():
            strip(d, r, (1, nb)).start()
            strip(d, r + 4, (1, nb)).start()

    weave([(None, phase_c2(r, tab, ob.at[1], L3, psi1, gs.at[1], adj), functools.partial(ship1, r))
           for r in range(4)], 2)

    near1 = remote(gs.at[1], out.at[d], g_send.at[1], g_recv.at[d], (1, p))
    stay1 = pltpu.make_async_copy(gs.at[1], out.at[d], loc_sem)

    @pl.when(d == 0)
    def _():
        near1.start()

    @pl.when(d == 1)
    def _():
        stay1.start()

    run([phase_d(m, tab, kk, *bufs(m), L2, adj) for m in range(MODES)])

    def chunk(r, dev):
        rows = pl.ds(r * 64, 64)
        return remote(gs.at[0, :, rows, :], out.at[2 + d, :, rows, :], c_send.at[r], c_recv.at[d, r], dev)

    def incoming(slot, r):
        rows = pl.ds(r * 64, 64)
        return remote(gs.at[0, :, rows, :], out.at[2 + slot, :, rows, :], c_send.at[r], c_recv.at[slot, r],
                      (0, nb))

    def ship(r):
        @pl.when(jnp.logical_not(wrap_a))
        def _():
            chunk(r, (0, nb)).start()

    weave([(None, phase_e(r, tab, pr, L2, gs.at[0]), functools.partial(ship, r)) for r in range(4)], 2)
    near0 = remote(gs.at[0], out.at[d], g_send.at[1], g_recv.at[d], (0, p))
    stay0 = pltpu.make_async_copy(gs.at[0], out.at[d], loc_sem)

    @pl.when(d == 1)
    def _():
        near0.start()
        stay1.wait()

    @pl.when(d == 0)
    def _():
        stay0.start()
        near1.wait_send()

    sent_object()
    c_part.wait_send()

    @pl.when(jnp.logical_not(wrap_a))
    def _():
        for i in range(8):
            strip(d, i, (1, nb)).wait_send()
        for r in range(4):
            chunk(r, (0, nb)).wait_send()

    @pl.when(d == 1)
    def _():
        near0.wait_send()
        remote(gs.at[1], out.at[0], g_send.at[1], g_recv.at[0], (0, p)).wait_recv()
        for i in range(8):
            strip(1, i, (1, nb)).wait_recv()

        @pl.when(p > 0)
        def _():
            for i in range(8):
                strip(0, i, (1, nb)).wait_recv()

    @pl.when(d == 0)
    def _():
        stay0.wait()
        remote(gs.at[0], out.at[1], g_send.at[1], g_recv.at[1], (0, p)).wait_recv()
        for r in range(4):
            incoming(1, r).wait_recv()

        @pl.when(p > 0)
        def _():
            for r in range(4):
                incoming(0, r).wait_recv()


def final_kernel(chips, blocks, pos_h, slots, out, pos, acc, sem, pos_sem):
    load = pltpu.make_async_copy(pos_h, pos, pos_sem)
    load.start()
    p = lax.axis_index("pos")
    total = 2 * chips
    acc[...] = jnp.zeros_like(acc)
    load.wait()
    rows = iota((16, N), 0)
    cols = iota((16, N), 1)
    places = []
    for off, ge in ((0, True), (total - 1, False), (total - 2, False), (1, True)):
        q = lax.rem(2 * p + off, total)
        y = pos[0, q]
        c = pos[1, q] & 255
        k = y >> 8
        places.append((k, jnp.minimum(k + 1, blocks - 1), y & 255, (cols >= c) if ge else (cols < c)))
    copies = []
    for part in range(2):
        for slot, (k, k2, yy, cm) in enumerate(places):
            to = [jnp.where(r0 + 15 < yy, k2, jnp.where(r0 >= yy, k, blocks)) for r0 in range(0, N, 16)]
            old = [acc[part, to[i], 16 * i:16 * i + 16] for i in range(N // 16)]
            for i in range(N // 16):
                x = slots[slot, part, 16 * i:16 * i + 16]
                acc[part, to[i], 16 * i:16 * i + 16] = old[i] + jnp.where(cm, x, jnp.zeros_like(x))
            rb = pl.multiple_of((yy >> 4) * 16, 16)
            x = slots[slot, part, pl.ds(rb, 16)]
            here = rows >= jnp.where((yy & 15) != 0, yy - rb, N)
            acc[part, k, pl.ds(rb, 16)] += jnp.where(cm & here, x, jnp.zeros_like(x))
            acc[part, k2, pl.ds(rb, 16)] += jnp.where(cm & (rows < yy - rb), x, jnp.zeros_like(x))
        for i in range(0, blocks, 2):
            cp = pltpu.make_async_copy(acc.at[part, i:i + 2], out.at[part, i:i + 2], sem.at[part, i // 2])
            cp.start()
            copies.append(cp)
    for cp in copies:
        cp.wait()


def local(object_field, probe, prop_phase, measured, positions):
    chips = lax.axis_size("pos")
    height = object_field.shape[2]
    blocks = height // N
    tb, tbt = tables()
    pos_t = positions.T
    any_ = pl.BlockSpec(memory_space=pl.ANY)
    V = pltpu.VMEM
    win = V((2, N, N), BF)
    dma = pltpu.SemaphoreType.DMA
    slots = pl.pallas_call(
        functools.partial(main_kernel, chips, height),
        out_shape=jax.ShapeDtypeStruct((4, 2, N, N), BF),
        in_specs=[pl.BlockSpec(memory_space=pltpu.HBM)] * 7,
        out_specs=any_,
        scratch_shapes=[
            pltpu.SMEM((2, 2 * chips), jnp.int32), V((2, blocks, N, N), BF), win, win, win, V((2, 2, N, N), BF), V((2, 2, N, N), BF),
            V((2, 2, N, N), F32), V((4, 2, N, N), BF), V((N, N), F32), V((2, N, N), BF), V((N, N), F32),
            V((512, N), BF), V((N, 512), BF), V((4, 2, N, N), BF), V((4, 2, N, N), F32),
            V((2, N, N), F32), V((N, N), F32), V((WIDTH, 2, N, N), BF), V((WIDTH, 2, N, N), BF),
            V((4, 2, N, N), F32), V((4, 2, N, N), F32), V((2, N, 128), F32), V((4, 2, N, N), BF),
            V((2, 4, 4, 64, N), BF), V((2, 4, 4, 64, N), BF), V((2, 2, N, N), BF),
            dma((7,)), dma((2,)), dma((2,)), dma, dma, dma, dma,
            dma((2,)), dma((4,)), dma((8,)), dma((2, 8)), dma((4,)), dma((2, 4)), dma,
        ],
        compiler_params=pltpu.CompilerParams(
            collective_id=0, has_side_effects=True, vmem_limit_bytes=48 * 1024 * 1024),
        name="ptycho",
    )(*(pltpu.with_memory_space_constraint(a, pltpu.HBM) for a in (
        pos_t, object_field.reshape(2, blocks, N, N), probe, prop_phase, measured, tb, tbt)))
    band = pl.pallas_call(
        functools.partial(final_kernel, chips, blocks),
        out_shape=jax.ShapeDtypeStruct((2, blocks, N, N), BF),
        in_specs=[any_, pl.BlockSpec(memory_space=pltpu.VMEM)],
        out_specs=pl.BlockSpec(memory_space=pltpu.HBM),
        scratch_shapes=[pltpu.SMEM((2, 2 * chips), jnp.int32), V((2, blocks + 1, N, N), BF), dma((2, blocks // 2)), dma],
        compiler_params=pltpu.CompilerParams(vmem_limit_bytes=32 * 1024 * 1024),
        name="assemble",
    )(pos_t, slots)
    return band.reshape(1, 2, height, N)


def solution(mesh):
    placed = (PS("depth", None, None, "pos"), PS(), PS(), PS("pos", None, None), PS())
    return jax.shard_map(
        local, mesh=mesh, in_specs=placed, out_specs=PS("depth", None, None, "pos"), check_vma=False
    )
```
